32 devices in a mesh: groups: 2 (over y), qry: 4 (over x, core), ref: 4 (over z).
Axes of the slice: x: 2, y: 2, z: 4, core: 2. Of those that a mesh axis runs over, the one named last changes fastest.
Arguments:
- query_feats: bfloat16 [1024, 9, 3840], P(('groups', 'qry')), parts along dimension 0, may hold values from -6 to 6
- ref_feats: bfloat16 [256, 4, 9, 3840], P(('groups', 'ref'), 'qry'), parts along dimension 0, may hold values from -6 to 6
- pair_table: int32 [8, 4], P('groups'), parts along dimension 0, may hold values from 0 to 1, as said below
- lengths: int32 [4], P('groups'), parts along dimension 0, may hold values from 1 to 96, 128 in all
- query_len: int32 [2], P('groups'), parts along dimension 0, may hold values from 64 to 128
- conv1_weight: float32 [3, 3, 32], replicated, may hold values from -2 to 2
- conv1_bias: float32 [32], replicated, may hold values from -3 to 3
- conv2_weight: bfloat16 [3, 3, 64, 32], replicated, may hold values from -0.375 to 0.375
- conv2_bias: float32 [64], replicated, may hold values from -3 to 3
- conv3_weight: bfloat16 [3, 3, 128, 64], replicated, may hold values from -0.25 to 0.25
- conv3_bias: float32 [128], replicated, may hold values from -3 to 3
- conv4_weight: bfloat16 [128], replicated, may hold values from -0.5 to 0.5
- conv4_bias: float32 [1], replicated, may hold values from -3 to 3
Outputs:
- score_map: float32 [256, 128], P(('groups', 'qry'), 'ref'), parts along dimension 0
- video_scores: float32 [4], P('groups'), parts along dimension 0
The draws below stay inside these ranges and needn't reach their ends.
There are 2 independent parts, one for each index of `groups`. The reference program is written for one: setup_inputs(seed, part) draws one part's arguments, and reference() takes and returns one part's arrays. A program takes and returns all parts, laid end to end along the dimension named above; an argument that names none is the same for every part. Nothing has to cross between parts.
Inputs may be any that keep to these rules, and one draw needn't show every extreme that they name: `pair_table`: in each row, at most 1 of the 1 tiles in the block of one index of ref are 1, and some such block holds exactly 1 in every draw.
All inputs are finite; a program needn't handle non-finite values.
Results may differ from the reference program's by a relative error of at most 0.01.
Values may be sent and summed in bfloat16 or wider, within the bound.
A program may use at most 128 MiB of HBM per device.

```python
import math
import jax
import jax.numpy as jnp
import numpy as np
from jax import lax

D = 3840
REGIONS = 9
FT = 128
C1 = 32
C2 = 64
C3 = 128
MOST = 1
RTD = 1
QT = 4
RT = 4
NQ = 512
NR = 512
VIDEOS = 2
N_REF = 4


def draw_pair_table(key, part):
    subkeys = jax.random.split(jax.random.fold_in(key, 17), 4)
    counts = jax.random.randint(subkeys[0], (QT, N_REF), 0, MOST + 1)
    pick_row = jax.random.randint(subkeys[1], (), 0, QT)
    pick_col = jax.random.randint(subkeys[2], (), 0, N_REF)
    forced = (jnp.arange(QT)[:, None] == pick_row) & (jnp.arange(N_REF)[None, :] == pick_col)
    counts = jnp.where(forced, MOST, counts)
    scores = jax.random.randint(subkeys[3], (QT, N_REF, RTD), 0, 1 << 20) * RTD + jnp.arange(RTD)
    ordering = jnp.argsort(scores, axis=-1, stable=True)
    placing = jnp.argsort(ordering, axis=-1, stable=True)
    return (placing < counts[..., None]).astype(jnp.int32).reshape(QT, RT)


def block_levels(own_key, shape, cuts, least, high):
    def one(axis_at, shards_of):
        heights = jax.random.uniform(jax.random.fold_in(jax.random.fold_in(own_key, 6), axis_at), (shards_of,), jnp.float32, least / len(cuts), high / len(cuts))
        return jnp.repeat(jnp.exp(heights), shape[axis_at] // shards_of).reshape((-1,) + (1,) * (len(shape) - axis_at - 1))

    level = one(*cuts[0])
    for cut in cuts[1:]:
        level = level * one(*cut)
    return level


def split_up(number_of, total, bound, slope):
    loads = [(1 << 20) // math.isqrt(standing ** slope) + 1 for standing in range(2, number_of + 1)]
    spare, holding = total - bound - (number_of - 1), [1] * (number_of - 1)
    while spare > 0:
        movable = [i for i in range(number_of - 1) if holding[i] < bound]
        pool, left = sum([loads[i] for i in movable]), spare
        for i in movable:
            addition = min(bound - holding[i], max(1, left * loads[i] // pool), spare)
            holding[i] = holding[i] + addition
            spare = spare - addition
    return np.array([bound] + holding)


def uneven_parts(key, number_of, total, most, slope):
    if number_of == 2:
        one = jax.random.randint(key, (), max(1, total - most), min(most, total - 1) + 1)
        return jnp.stack([one, total - one])
    sizes = jnp.asarray(split_up(number_of, total, most, slope), jnp.int32)
    pairs = (number_of - 1) // 2
    giver, receiver = sizes[1:1 + 2 * pairs:2], sizes[2:2 + 2 * pairs:2]
    slack = jnp.minimum(giver - 1, most - receiver)
    moved = jax.random.randint(jax.random.fold_in(key, 1), (pairs,), 0, 1 << 20) % (slack + 1)
    sizes = sizes.at[1:1 + 2 * pairs:2].set(giver - moved).at[2:2 + 2 * pairs:2].set(receiver + moved)
    return sizes[jax.random.permutation(jax.random.fold_in(key, 2), number_of)]


def gaussian(own_key, shape, scale, most, shards=(), kind=jnp.bfloat16):
    entries = jax.random.normal(own_key, shape, jnp.float32) * scale
    if len(shards) > 0:
        entries = block_levels(own_key, shape, shards, -0.22, 0.18) * entries
    return jnp.clip(entries, min=-most, max=most).astype(kind)


def setup_inputs(seed: int = 0, part: int = 0) -> dict:
    streams_of = jax.random.split(jax.random.key(seed), 14)
    own_keys = jax.random.split(jax.random.fold_in(streams_of[13], part), 14)
    return {
        "query_feats": gaussian(own_keys[0], (NQ, REGIONS, D), 1.0, 6.0, ((0, 4),)),
        "ref_feats": gaussian(own_keys[1], (NR // QT, QT, REGIONS, D), 1.0, 6.0, ((0, 4), (1, 4))),
        "pair_table": draw_pair_table(jax.random.fold_in(jax.random.fold_in(streams_of[13], part), 71), part),
        "lengths": uneven_parts(own_keys[3], VIDEOS, NR // 4, 3 * FT // 4, 1).astype(jnp.int32),
        "query_len": jax.random.randint(own_keys[4], (1,), NQ // 8, NQ // 4 + 1).astype(jnp.int32),
        "conv1_weight": gaussian(streams_of[5], (3, 3, C1), 9 ** -0.5, 2.0, (), jnp.float32),
        "conv1_bias": gaussian(streams_of[6], (C1,), 0.5, 3.0, (), jnp.float32),
        "conv2_weight": gaussian(streams_of[7], (3, 3, C2, C1), (9 * C1) ** -0.5, 0.375),
        "conv2_bias": gaussian(streams_of[8], (C2,), 0.5, 3.0, (), jnp.float32),
        "conv3_weight": gaussian(streams_of[9], (3, 3, C3, C2), (9 * C2) ** -0.5, 0.25),
        "conv3_bias": gaussian(streams_of[10], (C3,), 0.5, 3.0, (), jnp.float32),
        "conv4_weight": gaussian(streams_of[11], (C3,), C3 ** -0.5, 0.5),
        "conv4_bias": gaussian(streams_of[12], (1,), 0.5, 3.0, (), jnp.float32),
    }


def slot_table(mask, most):
    width = mask.shape[-1]
    ranking = (jnp.cumsum(mask, axis=-1) - 1).astype(jnp.int32)
    slot_ids = jnp.arange(most, dtype=jnp.int32)
    chosen = (mask[..., None, :] == 1) & (ranking[..., None, :] == slot_ids[:, None])
    picked = lax.optimization_barrier(jnp.sum(jnp.where(chosen, jnp.arange(width, dtype=jnp.int32), 0), axis=-1)).astype(jnp.int32)
    return (chosen, picked)

def frame_sims(query_mat, ref_mat, regions):
    products = lax.dot_general(query_mat, ref_mat, (((1,), (1,)), ((), ())), preferred_element_type=jnp.float32, precision=lax.Precision.HIGHEST)
    frames = query_mat.shape[0] // regions
    others = ref_mat.shape[0] // regions
    best = lax.optimization_barrier(jnp.max(products.reshape(frames, regions, others, regions), axis=3))
    return lax.optimization_barrier(jnp.sum(best, axis=1)) * (1.0 / (regions * math.sqrt(query_mat.shape[1])))

def conv_layer(padded, weights, bias, block_rows, use_relu, use_pool):
    channels = padded.shape[0]
    height = padded.shape[1] - 2
    width = padded.shape[2] - 2
    block_rows = math.gcd(height, block_rows)
    outputs = weights.shape[0]

    def one_block(position):
        window = lax.dynamic_slice_in_dim(padded, position * block_rows, block_rows + 2, 1)
        stacked = jnp.concatenate([window[:, shift_row:shift_row + block_rows, shift_col:shift_col + width] for shift_row in range(3) for shift_col in range(3)], axis=0)
        result = jnp.dot(weights, stacked.reshape(9 * channels, block_rows * width), preferred_element_type=jnp.float32, precision=lax.Precision.HIGHEST)
        result = (result + bias[:, None]).reshape(outputs, block_rows, width)
        if use_relu:
            result = jnp.maximum(result, 0.0)
        if use_pool:
            result = lax.optimization_barrier(jnp.max(result.reshape(outputs, block_rows // 2, 2, width // 2, 2), axis=(2, 4)))
        return result
    blocks = lax.map(one_block, jnp.arange(height // block_rows, dtype=jnp.int32))
    return jnp.transpose(blocks, (1, 0, 2, 3)).reshape(outputs, -1, blocks.shape[-1])

def rounded(values):
    return lax.optimization_barrier(values.astype(jnp.bfloat16)).astype(jnp.float32)

def padded_map(values):
    return jnp.pad(values, ((0, 0), (1, 1), (1, 1)))

def weight_matrix(weight):
    return jnp.transpose(weight, (2, 0, 1, 3)).reshape(weight.shape[2], -1).astype(jnp.float32)

def reference(query_feats, ref_feats, pair_table, lengths, query_len, conv1_weight, conv1_bias, conv2_weight, conv2_bias, conv3_weight, conv3_bias, conv4_weight, conv4_bias):
    queries = query_feats.astype(jnp.float32).reshape(QT, FT * REGIONS, D)
    references = ref_feats.astype(jnp.float32).reshape(RT, FT * REGIONS, D)
    chosen, picked = slot_table(pair_table.reshape(QT, N_REF, RTD), MOST)

    def tile_block(position):
        qry_index = position // N_REF
        ref_index = position % N_REF
        query_mat = queries[qry_index]

        def one_slot(slot_id):
            return frame_sims(query_mat, references[ref_index * RTD + picked[qry_index, ref_index, slot_id]], REGIONS)
        sims = lax.map(one_slot, jnp.arange(MOST, dtype=jnp.int32))
        placed = jnp.einsum('st,sqf->qtf', chosen[qry_index, ref_index].astype(jnp.float32), sims, precision=lax.Precision.HIGHEST)
        return placed.reshape(FT, RTD * FT)
    blocks = lax.map(tile_block, jnp.arange(QT * N_REF, dtype=jnp.int32))
    sim_map = blocks.reshape(QT, N_REF, FT, RTD * FT).transpose(0, 2, 1, 3).reshape(1, NQ, NR)
    first_weights = conv1_weight.astype(jnp.float32).transpose(2, 0, 1).reshape(C1, 9)
    first = rounded(conv_layer(padded_map(sim_map), first_weights, conv1_bias, 32, True, True))
    second = rounded(conv_layer(padded_map(first), weight_matrix(conv2_weight), conv2_bias, 16, True, True))
    third = rounded(conv_layer(padded_map(second), weight_matrix(conv3_weight), conv3_bias, 16, True, False))
    last_weights = conv4_weight.astype(jnp.float32).reshape(1, C3)
    score_map = jnp.dot(last_weights, third.reshape(C3, -1), preferred_element_type=jnp.float32, precision=lax.Precision.HIGHEST).reshape(NQ // 4, NR // 4) + conv4_bias[0]
    ends = jnp.cumsum(lengths).astype(jnp.int32)
    starts = ends - lengths
    column = jnp.arange(NR // 4, dtype=jnp.int32)
    member = (column[:, None] >= starts[None, :]) & (column[:, None] < ends[None, :])
    peaks = lax.optimization_barrier(jnp.max(jnp.where(member[None], score_map[:, :, None], -jnp.inf), axis=1))
    row_ids = jnp.arange(NQ // 4, dtype=jnp.int32)
    totals = lax.optimization_barrier(jnp.sum(jnp.where((row_ids < query_len[0])[:, None], peaks, 0.0), axis=0))
    return (score_map, totals / query_len[0].astype(jnp.float32))
```

```python
import functools
import math

import jax
import jax.numpy as jnp
from jax import lax
from jax.experimental import pallas as pl
from jax.experimental.pallas import tpu as pltpu
from jax.sharding import PartitionSpec as P

MESH = pl.DeviceIdType.MESH
HALO = 8
PITCH = 40
LEAD = 48
GROUP = 8
NT = (((1,), (1,)), ((), ()))


def spans(flags):
    found = []
    for k, flag in enumerate(flags):
        if flag and (k == 0 or not flags[k - 1]):
            found.append([k, k + 1])
        elif flag:
            found[-1][1] = k + 1
    return [tuple(span) for span in found]


def plan(chunks, frames, tiles, last):
    side = tiles + 4
    width = frames // chunks

    def early(frame):
        chunk = chunks - 1 if frame < 0 else 0 if frame >= frames else frame // width
        return chunk != last

    ready = []
    for j in range(side):
        ready.append(all(early(4 * (j - 2) + k) for k in range(-1, 5)))
    passes = [[ready], [[not flag for flag in ready]]]
    for layer in (1, 2):
        wanted = [layer <= j < side - layer for j in range(side)]
        before = passes[0][-1]
        now = [wanted[j] and all(before[j + k] for k in (-1, 0, 1)) for j in range(1, side - 1)]
        now = [False] + now + [False]
        passes[0].append(now)
        passes[1].append([wanted[j] and not now[j] for j in range(side)])
    return [[spans(flags) for flags in one] for one in passes]


def chunk_order(chunks, k):
    return k // 2 + (k % 2) * (chunks - 1 - 2 * (k // 2))


def whole_kernel(
    chips, others, scale, cuts,
    pair_hbm, lengths_hbm, len_hbm, b4_hbm, w1_hbm, b1_hbm, w2_hbm, b2_hbm, w3_hbm, b3_hbm,
    w4_hbm, q_hbm, r_hbm,
    scores_ref, totals_ref,
    pair_ref, lengths_ref, len_ref, b4_ref, w1_ref, b1_ref, w2_ref, b2_ref, w3_ref, b3_ref, w4_ref,
    q_buf, r_own, r_far, acc, sims_buf, map_buf, z_buf, x_buf, first_buf, second_buf,
    w1_rep, w1_flat, w1_full, w2_full, w3_full, b1_full, b2_full, score_buf, peaks_buf,
    small_sem, q_sem, own_sem, send_o, recv_o, send_x, recv_x, send_s, recv_s, send_h, recv_h,
    send_p, recv_p,
):
    regions, shard, depth = r_hbm.shape
    frames = q_hbm.shape[0] // regions
    chunks = shard // GROUP
    width = GROUP * 2 * chips
    tiles = frames // 4
    last = chunk_order(chunks, chunks - 1)
    me = lax.axis_index("qry")
    chip = me // 2
    core = me % 2
    sibling = chip * 2 + (1 - core)
    right = ((chip + 1) % chips) * 2 + core
    senders = 2 * chips
    col = lax.axis_index("ref")
    peers = senders * others
    mine = me * others + col

    smalls = [
        pltpu.make_async_copy(source, target, small_sem.at[k])
        for k, (source, target) in enumerate(
            (
                (w1_hbm, w1_ref), (b1_hbm, b1_ref), (w2_hbm, w2_ref), (b2_hbm, b2_ref),
                (w3_hbm, w3_ref), (b3_hbm, b3_ref), (w4_hbm, w4_ref), (pair_hbm, pair_ref),
                (lengths_hbm, lengths_ref), (len_hbm, len_ref), (b4_hbm, b4_ref),
            )
        )
    ]

    def piece(p):
        return pl.ds(cuts[p], cuts[p + 1] - cuts[p])

    pieces = len(cuts) - 1

    def rows_of(g):
        return pl.ds(pl.multiple_of(g * GROUP, GROUP), GROUP)

    def own_copy(g):
        return pltpu.make_async_copy(r_hbm.at[:, rows_of(g)], r_own.at[0, g], own_sem.at[g])

    def own_to_sibling(g):
        return pltpu.make_async_remote_copy(
            src_ref=r_hbm.at[:, rows_of(g)],
            dst_ref=r_own.at[1, g],
            send_sem=send_o.at[g],
            recv_sem=recv_o.at[g],
            device_id={"qry": sibling},
            device_id_type=MESH,
        )

    def q_copy(k):
        rows = pl.ds(k * frames, frames)
        return pltpu.make_async_copy(q_hbm.at[rows], q_buf.at[rows], q_sem.at[k])

    def to_right(step, g, p):
        if step == 0:
            source = r_hbm.at[:, rows_of(g), piece(p)]
        else:
            source = r_far.at[step - 1, g, 0, :, :, piece(p)]
        return pltpu.make_async_remote_copy(
            src_ref=source,
            dst_ref=r_far.at[step, g, 0, :, :, piece(p)],
            send_sem=send_x.at[step, g, p],
            recv_sem=recv_x.at[step, g, p],
            device_id={"qry": right},
            device_id_type=MESH,
        )

    def to_sibling(step, g, p):
        return pltpu.make_async_remote_copy(
            src_ref=r_far.at[step, g, 0, :, :, piece(p)],
            dst_ref=r_far.at[step, g, 1, :, :, piece(p)],
            send_sem=send_s.at[step, g, p],
            recv_sem=recv_s.at[step, g, p],
            device_id={"qry": sibling},
            device_id_type=MESH,
        )

    for k in range(regions):
        q_copy(k).start()
    for g in range(chunks):
        own_copy(g).start()
    map_buf[...] = jnp.zeros_like(map_buf)
    barrier = pltpu.get_barrier_semaphore()

    def greet(k, carry):
        peer = (mine + k) % peers
        device = {"qry": peer // others, "ref": peer % others}
        pl.semaphore_signal(barrier, inc=1, device_id=device, device_id_type=MESH)
        return carry

    lax.fori_loop(1, peers, greet, 0)
    for copy in smalls:
        copy.start()
    pl.semaphore_wait(barrier, peers - 1)

    def start_sends(k, carry):
        g = chunk_order(chunks, k)
        for p in range(pieces):
            to_right(0, g, p).start()
        return carry

    lax.fori_loop(0, chunks, start_sends, 0)
    for g in range(chunks):
        own_to_sibling(g).start()

    z_buf[...] = jnp.zeros_like(z_buf)
    first_buf[...] = jnp.zeros_like(first_buf)
    second_buf[...] = jnp.zeros_like(second_buf)
    peaks_buf[mine] = jnp.zeros(peaks_buf.shape[1:], jnp.float32)
    for copy in smalls:
        copy.wait()
    build_weights(
        w1_ref, w2_ref, w3_ref, b1_ref, b2_ref, w1_rep, w1_flat, w1_full, w2_full, w3_full,
        b1_full, b2_full,
    )
    factor = pair_ref[me, col].astype(jnp.float32) * scale

    def similar(product, blocks):
        best = jnp.max(product.reshape(blocks, regions, GROUP, regions * frames), axis=1)
        total = best[:, :, :frames]
        for k in range(1, regions):
            total = total + best[:, :, k * frames : (k + 1) * frames]
        return total * factor

    def near(side):
        product = lax.dot_general(
            r_own[side].reshape(chunks * regions * GROUP, depth), q_buf[...], NT,
            preferred_element_type=jnp.float32,
        )
        return similar(product, chunks).reshape(shard, frames)

    for k in range(regions):
        q_copy(k).wait()
    for g in range(chunks):
        own_copy(g).wait()

    def near_side(side, carry):
        @pl.when(side == 1)
        def _():
            for g in range(chunks):
                own_to_sibling(g).wait_recv()

        sims_buf[chip * 2 + side * (1 - core) + (1 - side) * core] = near(side)
        return carry

    lax.fori_loop(0, 2, near_side, 0)

    def sources(step):
        origin = (chip + chips - 1 - step) % chips
        return origin * 2 + core, origin * 2 + (1 - core)

    def arrive(step, g, p):
        to_right(step, g, p).wait_recv()
        to_sibling(step, g, p).start()
        if step < chips - 2:
            to_right(step + 1, g, p).start()

    def part(step, g, first_piece, final_piece):
        columns = pl.ds(cuts[first_piece], cuts[final_piece] - cuts[first_piece])
        block = r_far[step, g, :, :, :, columns].reshape(2 * regions * GROUP, columns.size)
        return lax.dot_general(
            block, q_buf[:, columns], NT, preferred_element_type=jnp.float32
        )

    def keep(step, g, product):
        total = similar(product, 2)
        for k, source in enumerate(sources(step)):
            sims_buf[source, rows_of(g)] = total[k]

    def middle(k, carry):
        g = chunk_order(chunks, k)
        for step in range(chips - 1):
            for p in range(pieces):
                arrive(step, g, p)
            for p in range(pieces):
                to_sibling(step, g, p).wait_recv()
            keep(step, g, part(step, g, 0, pieces))
        return carry

    lax.fori_loop(0, chunks - 1, middle, 0)

    def reachable(move_q, move_r):
        fits = (me + move_q >= 0) & (me + move_q < senders)
        return fits & (col + move_r >= 0) & (col + move_r < others)

    def halo_copy(k, move_q, move_r, g):
        if move_r == 0:
            source = target = pl.ds(HALO + g * width, width)
        elif move_r == 1:
            source, target = pl.ds(frames, HALO), pl.ds(0, HALO)
        else:
            source, target = pl.ds(HALO, HALO), pl.ds(HALO + frames, HALO)
        return pltpu.make_async_remote_copy(
            src_ref=map_buf.at[1, source],
            dst_ref=map_buf.at[1 - move_q, target],
            send_sem=send_h.at[k],
            recv_sem=recv_h.at[k],
            device_id={"qry": me + move_q, "ref": col + move_r},
            device_id_type=MESH,
        )

    moves = [(q, 0, g) for g in range(chunks) for q in (-1, 1)]
    moves += [(q, r, 0 if r < 0 else chunks - 1) for r in (-1, 1) for q in (-1, 1, 0)]
    moves = list(enumerate(moves))

    def spread(done):
        for g in done:
            for b in range(senders):
                rows = pl.ds(HALO + g * width + b, GROUP, stride=senders)
                map_buf.at[1][rows, :] = sims_buf[b, g * GROUP : (g + 1) * GROUP]
        now = [(k, q, r, g) for k, (q, r, g) in moves if g in done]
        for k, q, r, g in now:

            @pl.when(reachable(q, r))
            def _():
                halo_copy(k, q, r, g).start()

        for k, q, r, g in now:

            @pl.when(reachable(-q, -r))
            def _():
                halo_copy(k, q, r, g).wait_recv()

    where = (me * tiles, col * tiles, senders * tiles, others * tiles)
    before, after = plan(chunks, frames, tiles, last)

    def network(layers):
        for lo, hi in layers[0]:
            conv1(lo, hi, where, map_buf, w1_full, b1_full, z_buf, x_buf, first_buf)
        for lo, hi in layers[1]:
            conv2(lo, hi, where, w2_full, b2_full, first_buf, second_buf)
        for lo, hi in layers[2]:
            score_buf[lo:hi, :PITCH] = conv3(lo, hi, w3_full, b3_ref, w4_ref, second_buf)

    if chunks > 1:
        spread([g for g in range(chunks) if g != last])
        network(before)

    for step in range(chips - 1):
        for p in range(pieces):
            arrive(step, last, p)
            to_sibling(step, last, p).wait_recv()
            if p == 0:
                acc[...] = part(step, last, p, p + 1)
            elif p < pieces - 1:
                acc[...] += part(step, last, p, p + 1)
            else:
                keep(step, last, acc[...] + part(step, last, p, p + 1))
    spread([last])
    network(after)

    scores = score_buf[...] + b4_ref[0]
    slot_f = lax.broadcasted_iota(jnp.int32, scores.shape, 0)
    column = slot_f + (col * tiles - 2)
    own = (slot_f >= 2) & (slot_f < 2 + tiles)
    begin = jnp.int32(0)
    for v in range(lengths_ref.shape[0]):
        end = begin + lengths_ref[v]
        member = own & (column >= begin) & (column < end)
        peaks_buf[mine, v : v + 1, :] = jnp.max(
            jnp.where(member, scores, -jnp.inf), axis=0, keepdims=True
        )
        begin = end

    def peak_copy(k):
        peer = (mine + k) % peers
        return pltpu.make_async_remote_copy(
            src_ref=peaks_buf.at[mine],
            dst_ref=peaks_buf.at[mine],
            send_sem=send_p.at[k],
            recv_sem=recv_p.at[mine],
            device_id={"qry": peer // others, "ref": peer % others},
            device_id_type=MESH,
        )

    def peak_wait(k, carry):
        peer = (mine + k) % peers
        pltpu.make_async_remote_copy(
            src_ref=peaks_buf.at[peer],
            dst_ref=peaks_buf.at[peer],
            send_sem=send_p.at[k],
            recv_sem=recv_p.at[peer],
            device_id={"qry": peer // others, "ref": peer % others},
            device_id_type=MESH,
        ).wait_recv()
        return carry

    def peak_start(k, carry):
        peak_copy(k).start()
        return carry

    lax.fori_loop(1, peers, peak_start, 0)
    scores_ref[...] = jnp.transpose(scores)[2 : 2 + tiles, 2 : 2 + tiles]

    def drain(g, carry):
        own_to_sibling(g).wait_send()
        for step in range(chips - 1):
            for p in range(pieces):
                to_right(step, g, p).wait_send()
                to_sibling(step, g, p).wait_send()
        return carry

    lax.fori_loop(0, chunks, drain, 0)
    for k, (q, r, g) in moves:

        @pl.when(reachable(q, r))
        def _():
            halo_copy(k, q, r, g).wait_send()

    lax.fori_loop(1, peers, peak_wait, 0)
    lane = lax.broadcasted_iota(jnp.int32, peaks_buf.shape[1:], 1)
    total = jnp.zeros(peaks_buf.shape[1:], jnp.float32)
    for s in range(senders):
        best = jnp.max(peaks_buf[s * others : (s + 1) * others], axis=0)
        counted = (lane >= 2) & (lane < 2 + tiles) & (lane + (s * tiles - 2) < len_ref[0])
        total = total + jnp.where(counted, best, 0.0)
    total = jnp.sum(total, axis=1, keepdims=True) / len_ref[0].astype(jnp.float32)
    for v in range(lengths_ref.shape[0]):
        totals_ref[v] = jnp.sum(total[v : v + 1])

    def peak_drain(k, carry):
        peak_copy(k).wait_send()
        return carry

    lax.fori_loop(1, peers, peak_drain, 0)


def build_weights(
    w1_ref, w2_ref, w3_ref, b1_ref, b2_ref, w1_rep, w1_flat, w1_full, w2_full, w3_full,
    b1_full, b2_full,
):
    for k in range(4):
        lanes = slice(k * 32, (k + 1) * 32)
        b1_full[:, lanes] = b1_ref[...]
        for di in range(3):
            w1_rep[3 * di : 3 * di + 3, lanes] = w1_ref[di]
    for k in range(2):
        b2_full[:, k * 64 : (k + 1) * 64] = b2_ref[...]
    w1_flat[...] = jnp.zeros_like(w1_flat)
    for u in range(2):
        for v in range(2):
            for a in range(2):
                for b in range(2):
                    at = (a * 2 + b) * 32
                    col = (u * 2 + v) * 128 + at
                    for k in range(9):
                        row = (2 * a + u + k // 3) * 8 + 2 * b + v + k % 3
                        w1_flat[row : row + 1, col : col + 32] = w1_rep[k : k + 1, at : at + 32]
    flat = w1_flat[...]
    high = flat.astype(jnp.bfloat16)
    w1_full[0:48] = high
    w1_full[48:96] = high
    w1_full[96:144] = (flat - high.astype(jnp.float32)).astype(jnp.bfloat16)

    w2_full[...] = jnp.zeros_like(w2_full)
    taps = {(0, 0): 0, (0, 1): 1, (1, 0): 2, (1, 1): -1}
    for g in range(2):
        for h in range(2):
            for a in range(2):
                for b in range(2):
                    row = ((g * 2 + h) * 4 + a * 2 + b) * 32
                    for u in range(2):
                        for v in range(2):
                            di = taps[g, a] - u + 1
                            dj = taps[h, b] - v + 1
                            if 0 <= di < 3 and 0 <= dj < 3:
                                col = u * 128 + v * 64
                                w2_full[row : row + 32, col : col + 64] = w2_ref[di * 3 + dj]
    for k in range(9):
        w3_full[k * 64 : (k + 1) * 64, :] = w3_ref[k]
    w3_full[576:640, :] = jnp.zeros((64, 128), jnp.bfloat16)


def inside_map(lo, hi, where):
    shape = (hi - lo, PITCH, 128)
    at_f = lax.broadcasted_iota(jnp.int32, shape, 0) + (where[1] - 2 + lo)
    at_p = lax.broadcasted_iota(jnp.int32, shape, 1) + (where[0] - 2)
    inside = (at_f >= 0) & (at_f < where[3]) & (at_p >= 0) & (at_p < where[2])
    return jnp.where(inside, 1.0, 0.0).reshape((hi - lo) * PITCH, 128)


def conv1(lo, hi, where, map_ref, w1_full, b1_full, z_buf, x_buf, first_buf):
    wide, frames = map_ref.shape[1:]
    top = max(0, (4 * lo - 1) // 8 * 8)
    end = min(wide, -(-(4 * hi + 3) // 8) * 8)
    source = lax.broadcasted_iota(jnp.int32, (3 * frames, 128), 0)
    target = lax.broadcasted_iota(jnp.int32, (3 * frames, 128), 1)
    whole = jnp.concatenate([map_ref[k, top:end] for k in range(3)], axis=1)
    high = whole.astype(jnp.bfloat16)
    lower = (whole - high.astype(jnp.float32)).astype(jnp.bfloat16)
    for rr in range(6):
        pick = jnp.where(source == 4 * target + (frames - 9) + rr, 1.0, 0.0).astype(jnp.bfloat16)
        for part, value in enumerate((high, lower)):
            z_buf[part, 8 + top : 8 + end, rr * 128 : (rr + 1) * 128] = jnp.dot(
                value, pick, preferred_element_type=jnp.float32
            )
    for block in range(lo, hi):
        pieces = []
        for part in (0, 1, 0):
            for rr in range(6):
                pieces.append(
                    z_buf[part, 4 * block + 7 : 4 * block + 15, rr * 128 : (rr + 1) * 128]
                )
        flat = jnp.concatenate(pieces, axis=0)
        x_buf[block * PITCH : (block + 1) * PITCH, :] = jnp.transpose(flat)[:PITCH]

    made = jnp.dot(
        x_buf[lo * PITCH : hi * PITCH].astype(jnp.bfloat16), w1_full[...],
        preferred_element_type=jnp.float32,
    )
    best = jnp.maximum(
        jnp.maximum(made[:, 0:128], made[:, 128:256]),
        jnp.maximum(made[:, 256:384], made[:, 384:512]),
    )
    first = jnp.maximum(best + b1_full[...], 0.0)
    first = jnp.where(inside_map(lo, hi, where) > 0.5, first, 0.0)
    first = first.astype(jnp.bfloat16).astype(jnp.float32)
    first_buf[LEAD + lo * PITCH : LEAD + hi * PITCH, :] = first


def conv2(lo, hi, where, w2_full, b2_full, first_buf, second_buf):
    lane = lax.broadcasted_iota(jnp.int32, (1, 128), 1)
    low_a = lane < 64
    low_b = (lane % 64) < 32
    rows = (hi - lo) * PITCH
    here = LEAD + lo * PITCH
    start = here - PITCH
    more = rows + 2 * PITCH
    first = first_buf[here : here + rows, :]
    shifted = jnp.where(
        low_a, first_buf[start + 1 : start + 1 + more, :], first_buf[start - 1 : start - 1 + more, :]
    )
    across = jnp.where(
        low_b, first_buf[here + PITCH : here + PITCH + rows, :], first_buf[start : start + rows, :]
    )
    both = jnp.where(low_b, shifted[2 * PITCH :], shifted[:rows])
    stacked = jnp.concatenate(
        [first, across, shifted[PITCH : PITCH + rows], both], axis=1
    ).astype(jnp.bfloat16)
    made = jnp.dot(stacked, w2_full[...], preferred_element_type=jnp.float32)
    best = jnp.maximum(made[:, 0:128], made[:, 128:256])
    best = jnp.maximum(best, pltpu.roll(best, 64, 1))
    second = jnp.maximum(best + b2_full[...], 0.0)
    second = jnp.where(inside_map(lo, hi, where) > 0.5, second, 0.0)
    second_buf[here : here + rows, :] = second.astype(jnp.bfloat16).astype(jnp.float32)


def conv3(lo, hi, w3_full, b3_ref, w4_ref, second_buf):
    lane = lax.broadcasted_iota(jnp.int32, (1, 128), 1)
    low_a = lane < 64
    rows = (hi - lo) * PITCH

    def moved(k):
        di, dj = k // 3, k % 3
        begin = LEAD + (lo + dj - 1) * PITCH + di - 1
        return second_buf[begin : begin + rows, :]

    groups = []
    for k in range(0, 9, 2):
        groups.append(jnp.where(low_a, moved(k), moved(k + 1)) if k < 8 else moved(k))
    stacked = jnp.concatenate(groups, axis=1).astype(jnp.bfloat16)
    made = jnp.dot(stacked, w3_full[...], preferred_element_type=jnp.float32)
    third = jnp.maximum(made + b3_ref[...], 0.0).astype(jnp.bfloat16).astype(jnp.float32)
    weighted = third * w4_ref[...].astype(jnp.float32)
    return jnp.sum(weighted.reshape(hi - lo, PITCH, 128), axis=2)


def body(
    query_feats, ref_feats, pair_table, lengths, query_len, conv1_weight, conv1_bias,
    conv2_weight, conv2_bias, conv3_weight, conv3_bias, conv4_weight, conv4_bias,
):
    senders = lax.axis_size("qry")
    others = lax.axis_size("ref")
    frames, regions, depth = query_feats.shape
    query_mat = jnp.transpose(query_feats, (1, 0, 2)).reshape(regions * frames, depth)
    ref_mat = jnp.transpose(ref_feats, (1, 2, 0, 3)).reshape(regions, -1, depth)
    videos = lengths.shape[0]
    video_rows = -(-videos // 8) * 8
    shard = ref_mat.shape[1]
    chunks = shard // GROUP
    chips = senders // 2
    steps = max(1, chips - 1)
    cuts = [0, depth * 9 // 15 // 128 * 128, depth * 13 // 15 // 128 * 128, depth]
    pieces = len(cuts) - 1
    tiles = frames // 4
    side = tiles + 4
    rows = side * PITCH
    scale = 1.0 / (regions * math.sqrt(depth))
    vmem = pl.BlockSpec(memory_space=pltpu.VMEM)
    smem = pl.BlockSpec(memory_space=pltpu.SMEM)
    hbm = pl.BlockSpec(memory_space=pl.ANY)
    dma = pltpu.SemaphoreType.DMA
    f32, bf16 = jnp.float32, jnp.bfloat16
    operands = (
        pair_table,
        lengths,
        query_len,
        conv4_bias,
        conv1_weight,
        conv1_bias[None],
        jnp.transpose(conv2_weight, (0, 1, 3, 2)).reshape(
            9, conv2_weight.shape[3], conv2_weight.shape[2]
        ),
        conv2_bias[None],
        jnp.transpose(conv3_weight, (0, 1, 3, 2)).reshape(
            9, conv3_weight.shape[3], conv3_weight.shape[2]
        ),
        conv3_bias[None],
        conv4_weight[None],
        query_mat,
        ref_mat,
    )
    kept = [
        (pltpu.SMEM if k < 4 else pltpu.VMEM)(operand.shape, operand.dtype)
        for k, operand in enumerate(operands[:11])
    ]
    scores, totals = pl.pallas_call(
        functools.partial(whole_kernel, chips, others, scale, cuts),
        out_shape=(
            jax.ShapeDtypeStruct((tiles, tiles), f32),
            jax.ShapeDtypeStruct((videos,), f32),
        ),
        in_specs=[hbm] * len(operands),
        out_specs=(vmem, smem),
        scratch_shapes=kept + [
            pltpu.VMEM(query_mat.shape, bf16),
            pltpu.VMEM((2, chunks, regions, GROUP, depth), bf16),
            pltpu.VMEM((steps, chunks, 2, regions, GROUP, depth), bf16),
            pltpu.VMEM((2 * regions * GROUP, regions * frames), f32),
            pltpu.VMEM((senders, shard, frames), f32),
            pltpu.VMEM((3, frames + 2 * HALO, frames), f32),
            pltpu.VMEM((2, frames + 4 * HALO, 768), f32),
            pltpu.VMEM((rows, 144), f32),
            pltpu.VMEM((rows + 2 * LEAD, 128), f32),
            pltpu.VMEM((rows + 2 * LEAD, 128), f32),
            pltpu.VMEM((16, 128), f32),
            pltpu.VMEM((48, 512), f32),
            pltpu.VMEM((144, 512), bf16),
            pltpu.VMEM((512, 256), bf16),
            pltpu.VMEM((640, 128), bf16),
            pltpu.VMEM((1, 128), f32),
            pltpu.VMEM((1, 128), f32),
            pltpu.VMEM((-(-side // 8) * 8, 128), f32),
            pltpu.VMEM((senders * others, video_rows, 128), f32),
            dma((11,)),
            dma((regions,)),
            dma((chunks,)),
            dma((chunks,)),
            dma((chunks,)),
            dma((steps, chunks, pieces)),
            dma((steps, chunks, pieces)),
            dma((steps, chunks, pieces)),
            dma((steps, chunks, pieces)),
            dma((2 * chunks + 6,)),
            dma((2 * chunks + 6,)),
            dma((senders * others,)),
            dma((senders * others,)),
        ],
        compiler_params=pltpu.CompilerParams(
            collective_id=0, has_side_effects=True, vmem_limit_bytes=56 << 20
        ),
        name="whole",
    )(*operands)
    return (scores, totals)


def solution(mesh):
    placed = (
        P(("groups", "qry"), None, None),
        P(("groups", "ref"), "qry", None, None),
        P("groups", None),
        P("groups"),
        P("groups"),
    ) + (P(),) * 8
    return jax.shard_map(
        body,
        mesh=mesh,
        in_specs=placed,
        out_specs=(P(("groups", "qry"), "ref"), P("groups")),
        check_vma=False,
    )
```

```python
import functools
import math

import jax
import jax.numpy as jnp
from jax import lax
from jax.experimental import pallas as pl
from jax.experimental.pallas import tpu as pltpu
from jax.sharding import PartitionSpec as P

MESH = pl.DeviceIdType.MESH
HALO = 8
PITCH = 40
LEAD = 48
GROUP = 8
NT = (((1,), (1,)), ((), ()))


def spans(flags):
    found = []
    for k, flag in enumerate(flags):
        if flag and (k == 0 or not flags[k - 1]):
            found.append([k, k + 1])
        elif flag:
            found[-1][1] = k + 1
    return [tuple(span) for span in found]


def plan(stages, chunks, frames, tiles):
    side = tiles + 4
    width = frames // chunks
    here, finished, work = set(), [[False] * side for _ in range(3)], []
    for stage in stages:
        here |= set(stage)
        ready = []
        for j in range(side):
            known = True
            for k in range(-1, 5):
                frame = 4 * (j - 2) + k
                outside = chunks - 1 if frame < 0 else 0
                known &= (frame // width if 0 <= frame < frames else outside) in here
            ready.append(known)
        layers = []
        for layer in range(3):
            if layer:
                edge = [False] * layer
                ready = [all(ready[j - 1 : j + 2]) for j in range(layer, side - layer)]
                ready = edge + ready + edge
            layers.append(spans([now and not was for now, was in zip(ready, finished[layer])]))
            finished[layer] = ready
        work.append(layers)
    return work


def chunk_order(chunks):
    return [k // 2 if k % 2 == 0 else chunks - 1 - k // 2 for k in range(chunks)]


def whole_kernel(
    chips, others, scale, cuts,
    pair_hbm, lengths_hbm, len_hbm, b4_hbm, w1_hbm, b1_hbm, w2_hbm, b2_hbm, w3_hbm, b3_hbm,
    w4_hbm, q_hbm, r_hbm,
    scores_ref, totals_ref,
    pair_ref, lengths_ref, len_ref, b4_ref, w1_ref, b1_ref, w2_ref, b2_ref, w3_ref, b3_ref, w4_ref,
    q_buf, r_own, r_far, acc, sims_buf, map_buf, z_buf, x_buf, first_buf, second_buf,
    w1_rep, w1_flat, w1_full, w2_full, w3_full, b1_full, b2_full, score_buf, peaks_buf,
    small_sem, q_sem, own_sem, send_o, recv_o, send_x, recv_x, send_s, recv_s, send_h, recv_h,
    send_p, recv_p, far_sem,
):
    regions, shard, depth = r_hbm.shape
    frames = q_hbm.shape[0] // regions
    chunks = shard // GROUP
    width = GROUP * 2 * chips
    tiles = frames // 4
    order = chunk_order(chunks)
    last = order[-1]
    me = lax.axis_index("qry")
    chip = me // 2
    core = me % 2
    sibling = chip * 2 + (1 - core)
    right = ((chip + 1) % chips) * 2 + core
    senders = 2 * chips
    col = lax.axis_index("ref")
    peers = senders * others
    mine = me * others + col

    smalls = [
        pltpu.make_async_copy(source, target, small_sem.at[k])
        for k, (source, target) in enumerate(
            (
                (w1_hbm, w1_ref), (b1_hbm, b1_ref), (w2_hbm, w2_ref), (b2_hbm, b2_ref),
                (w3_hbm, w3_ref), (b3_hbm, b3_ref), (w4_hbm, w4_ref), (pair_hbm, pair_ref),
                (lengths_hbm, lengths_ref), (len_hbm, len_ref), (b4_hbm, b4_ref),
            )
        )
    ]

    def piece(p):
        return pl.ds(cuts[p], cuts[p + 1] - cuts[p])

    pieces = len(cuts) - 1

    def rows_of(g):
        return pl.ds(pl.multiple_of(g * GROUP, GROUP), GROUP)

    def own_copy(g):
        return pltpu.make_async_copy(r_hbm.at[:, rows_of(g)], r_own.at[0, g], own_sem.at[g])

    def own_to_sibling(g):
        return pltpu.make_async_remote_copy(
            src_ref=r_hbm.at[:, rows_of(g)],
            dst_ref=r_own.at[1, g],
            send_sem=send_o.at[g],
            recv_sem=recv_o.at[g],
            device_id={"qry": sibling},
            device_id_type=MESH,
        )

    def q_copy(k):
        rows = pl.ds(k * frames, frames)
        return pltpu.make_async_copy(q_hbm.at[rows], q_buf.at[rows], q_sem.at[k])

    def to_right(step, g, p):
        if step == 0:
            source = r_hbm.at[:, rows_of(g), piece(p)]
        else:
            source = r_far.at[step - 1, g, 0, :, :, piece(p)]
        return pltpu.make_async_remote_copy(
            src_ref=source,
            dst_ref=r_far.at[step, g, 0, :, :, piece(p)],
            send_sem=send_x.at[step, g, p],
            recv_sem=recv_x.at[step, g, p],
            device_id={"qry": right},
            device_id_type=MESH,
        )

    def to_sibling(step, g, p):
        return pltpu.make_async_remote_copy(
            src_ref=r_far.at[step, g, 0, :, :, piece(p)],
            dst_ref=r_far.at[step, g, 1, :, :, piece(p)],
            send_sem=send_s.at[step, g, p],
            recv_sem=recv_s.at[step, g, p],
            device_id={"qry": sibling},
            device_id_type=MESH,
        )

    for k in range(regions):
        q_copy(k).start()
    for g in range(chunks):
        own_copy(g).start()
    map_buf[...] = jnp.zeros_like(map_buf)
    barrier = pltpu.get_barrier_semaphore()
    for k in range(1, senders):
        device = {"qry": (me + k) % senders}
        pl.semaphore_signal(barrier, inc=1, device_id=device, device_id_type=MESH)

    def tell_columns(semaphore):
        for move, there in ((-1, col > 0), (1, col < others - 1)):

            @pl.when(there)
            def _():
                pl.semaphore_signal(
                    semaphore, inc=1, device_id={"ref": col + move}, device_id_type=MESH
                )

    columns_near = jnp.where(col > 0, 1, 0) + jnp.where(col < others - 1, 1, 0)
    tell_columns(barrier)
    pl.semaphore_wait(barrier, senders - 1 + columns_near)

    def enqueue(lo, hi):
        for k in range(lo, min(hi, chunks * pieces)):
            to_right(0, order[k // pieces], k % pieces).start()

    enqueue(0, 3 * pieces // 2)
    for g in range(chunks):
        own_to_sibling(g).start()
    rounds = others - 1
    if rounds:
        tell_columns(far_sem.at[0])

    def next_round(k):
        if k < rounds:
            pl.semaphore_wait(far_sem.at[k], columns_near)
            if k + 1 < rounds:
                tell_columns(far_sem.at[k + 1])

    for copy in smalls:
        copy.start()
    z_buf[...] = jnp.zeros_like(z_buf)
    first_buf[...] = jnp.zeros_like(first_buf)
    second_buf[...] = jnp.zeros_like(second_buf)
    next_round(0)
    for copy in smalls:
        copy.wait()
    build_weights(
        w1_ref, w2_ref, w3_ref, b1_ref, b2_ref, w1_rep, w1_flat, w1_full, w2_full, w3_full,
        b1_full, b2_full,
    )
    next_round(1)
    factor = pair_ref[me, col].astype(jnp.float32) * scale

    def similar(product, blocks):
        best = jnp.max(product.reshape(blocks, regions, GROUP, regions * frames), axis=1)
        total = best[:, :, :frames]
        for k in range(1, regions):
            total = total + best[:, :, k * frames : (k + 1) * frames]
        return total * factor

    def near(side):
        product = lax.dot_general(
            r_own[side].reshape(chunks * regions * GROUP, depth), q_buf[...], NT,
            preferred_element_type=jnp.float32,
        )
        return similar(product, chunks).reshape(shard, frames)

    for k in range(regions):
        q_copy(k).wait()
    for g in range(chunks):
        own_copy(g).wait()

    def near_side(side, carry):
        @pl.when(side == 1)
        def _():
            for g in range(chunks):
                own_to_sibling(g).wait_recv()

        sims_buf[chip * 2 + side * (1 - core) + (1 - side) * core] = near(side)
        return carry

    lax.fori_loop(0, 2, near_side, 0)
    for k in range(2, rounds):
        next_round(k)

    def sources(step):
        origin = (chip + chips - 1 - step) % chips
        return origin * 2 + core, origin * 2 + (1 - core)

    def arrive(step, g, p):
        to_right(step, g, p).wait_recv()
        to_sibling(step, g, p).start()
        if step < chips - 2:
            to_right(step + 1, g, p).start()

    def part(step, g, first_piece, final_piece):
        columns = pl.ds(cuts[first_piece], cuts[final_piece] - cuts[first_piece])
        block = r_far[step, g, :, :, :, columns].reshape(2 * regions * GROUP, columns.size)
        return lax.dot_general(
            block, q_buf[:, columns], NT, preferred_element_type=jnp.float32
        )

    def keep(step, g, product):
        total = similar(product, 2)
        for k, source in enumerate(sources(step)):
            sims_buf[source, rows_of(g)] = total[k]

    def reachable(move_q, move_r):
        fits = (me + move_q >= 0) & (me + move_q < senders)
        return fits & (col + move_r >= 0) & (col + move_r < others)

    def halo_copy(k, move_q, move_r, g):
        if move_r == 0:
            source = target = pl.ds(HALO + g * width, width)
        elif move_r == 1:
            source, target = pl.ds(frames, HALO), pl.ds(0, HALO)
        else:
            source, target = pl.ds(HALO, HALO), pl.ds(HALO + frames, HALO)
        return pltpu.make_async_remote_copy(
            src_ref=map_buf.at[1, source],
            dst_ref=map_buf.at[1 - move_q, target],
            send_sem=send_h.at[k],
            recv_sem=recv_h.at[k],
            device_id={"qry": me + move_q, "ref": col + move_r},
            device_id_type=MESH,
        )

    moves = [(q, 0, g) for g in range(chunks) for q in (-1, 1)]
    moves += [(q, r, 0 if r < 0 else chunks - 1) for r in (-1, 1) for q in (-1, 1, 0)]
    moves = list(enumerate(moves))

    def spread(g):
        for b in range(senders):
            rows = pl.ds(HALO + g * width + b, GROUP, stride=senders)
            map_buf.at[1][rows, :] = sims_buf[b, g * GROUP : (g + 1) * GROUP]
        for k, (q, r, source) in moves:
            if source == g:

                @pl.when(reachable(q, r))
                def _():
                    halo_copy(k, q, r, g).start()

    def halos(stage):
        for k, (q, r, g) in moves:
            if g in stage:

                @pl.when(reachable(-q, -r))
                def _():
                    halo_copy(k, q, r, g).wait_recv()

    where = (me * tiles, col * tiles, senders * tiles, others * tiles)
    stages = (order[: max(chunks - 2, 0)], order[max(chunks - 2, 0) : chunks - 1], [last])
    work = plan(stages, chunks, frames, tiles)

    def network(k):
        halos(stages[k])
        for lo, hi in work[k][0]:
            conv1(lo, hi, where, map_buf, w1_full, b1_full, z_buf, x_buf, first_buf)
        for lo, hi in work[k][1]:
            conv2(lo, hi, where, w2_full, b2_full, first_buf, second_buf)
        for lo, hi in work[k][2]:
            score_buf[lo:hi, :PITCH] = conv3(lo, hi, w3_full, b3_ref, w4_ref, second_buf)

    for k, g in enumerate(order[:-1]):
        for step in range(chips - 1):
            for p in range(pieces):
                arrive(step, g, p)
            for p in range(pieces):
                to_sibling(step, g, p).wait_recv()
            keep(step, g, part(step, g, 0, pieces))
        spread(g)
        enqueue((2 * k + 3) * pieces // 2, (2 * k + 5) * pieces // 2)
    network(0)

    for step in range(chips - 1):
        for lo, hi in ((0, pieces - 3), (pieces - 3, pieces - 1), (pieces - 1, pieces)):
            for p in range(lo, hi):
                arrive(step, last, p)
            for p in range(lo, hi):
                to_sibling(step, last, p).wait_recv()
            if lo == 0:
                acc[...] = part(step, last, lo, hi)
                if step == 0:
                    network(1)
            elif hi < pieces:
                acc[...] += part(step, last, lo, hi)
            else:
                keep(step, last, acc[...] + part(step, last, lo, hi))
    spread(last)
    network(2)

    scores = score_buf[...] + b4_ref[0]
    slot_f = lax.broadcasted_iota(jnp.int32, scores.shape, 0)
    column = slot_f + (col * tiles - 2)
    own = (slot_f >= 2) & (slot_f < 2 + tiles)
    begin = jnp.int32(0)
    for v in range(lengths_ref.shape[0]):
        end = begin + lengths_ref[v]
        member = own & (column >= begin) & (column < end)
        peaks_buf[mine, v : v + 1, :] = jnp.max(
            jnp.where(member, scores, -jnp.inf), axis=0, keepdims=True
        )
        begin = end

    def peak_copy(k):
        peer = (mine + k) % peers
        return pltpu.make_async_remote_copy(
            src_ref=peaks_buf.at[mine],
            dst_ref=peaks_buf.at[mine],
            send_sem=send_p.at[k],
            recv_sem=recv_p.at[mine],
            device_id={"qry": peer // others, "ref": peer % others},
            device_id_type=MESH,
        )

    def peak_wait(k, carry):
        peer = (mine + k) % peers
        pltpu.make_async_remote_copy(
            src_ref=peaks_buf.at[peer],
            dst_ref=peaks_buf.at[peer],
            send_sem=send_p.at[k],
            recv_sem=recv_p.at[peer],
            device_id={"qry": peer // others, "ref": peer % others},
            device_id_type=MESH,
        ).wait_recv()
        return carry

    def peak_start(k, carry):
        peak_copy(k).start()
        return carry

    lax.fori_loop(1, peers, peak_start, 0)
    scores_ref[...] = jnp.transpose(scores)[2 : 2 + tiles, 2 : 2 + tiles]

    def drain(g, carry):
        own_to_sibling(g).wait_send()
        for step in range(chips - 1):
            for p in range(pieces):
                to_right(step, g, p).wait_send()
                to_sibling(step, g, p).wait_send()
        return carry

    lax.fori_loop(0, chunks, drain, 0)
    for k, (q, r, g) in moves:

        @pl.when(reachable(q, r))
        def _():
            halo_copy(k, q, r, g).wait_send()

    lax.fori_loop(1, peers, peak_wait, 0)
    lane = lax.broadcasted_iota(jnp.int32, peaks_buf.shape[1:], 1)
    total = jnp.zeros(peaks_buf.shape[1:], jnp.float32)
    for s in range(senders):
        best = jnp.max(peaks_buf[s * others : (s + 1) * others], axis=0)
        counted = (lane >= 2) & (lane < 2 + tiles) & (lane + (s * tiles - 2) < len_ref[0])
        total = total + jnp.where(counted, best, 0.0)
    total = jnp.sum(total, axis=1, keepdims=True) / len_ref[0].astype(jnp.float32)
    for v in range(lengths_ref.shape[0]):
        totals_ref[v] = jnp.sum(total[v : v + 1])

    def peak_drain(k, carry):
        peak_copy(k).wait_send()
        return carry

    lax.fori_loop(1, peers, peak_drain, 0)


def build_weights(
    w1_ref, w2_ref, w3_ref, b1_ref, b2_ref, w1_rep, w1_flat, w1_full, w2_full, w3_full,
    b1_full, b2_full,
):
    for k in range(4):
        lanes = slice(k * 32, (k + 1) * 32)
        b1_full[:, lanes] = b1_ref[...]
        for di in range(3):
            w1_rep[3 * di : 3 * di + 3, lanes] = w1_ref[di]
    for k in range(2):
        b2_full[:, k * 64 : (k + 1) * 64] = b2_ref[...]
    w1_flat[...] = jnp.zeros_like(w1_flat)
    for u in range(2):
        for v in range(2):
            for a in range(2):
                for b in range(2):
                    at = (a * 2 + b) * 32
                    col = (u * 2 + v) * 128 + at
                    for k in range(9):
                        row = (2 * a + u + k // 3) * 8 + 2 * b + v + k % 3
                        w1_flat[row : row + 1, col : col + 32] = w1_rep[k : k + 1, at : at + 32]
    flat = w1_flat[...]
    high = flat.astype(jnp.bfloat16)
    w1_full[0:48] = high
    w1_full[48:96] = high
    w1_full[96:144] = (flat - high.astype(jnp.float32)).astype(jnp.bfloat16)

    w2_full[...] = jnp.zeros_like(w2_full)
    taps = {(0, 0): 0, (0, 1): 1, (1, 0): 2, (1, 1): -1}
    for g in range(2):
        for h in range(2):
            for a in range(2):
                for b in range(2):
                    row = ((g * 2 + h) * 4 + a * 2 + b) * 32
                    for u in range(2):
                        for v in range(2):
                            di = taps[g, a] - u + 1
                            dj = taps[h, b] - v + 1
                            if 0 <= di < 3 and 0 <= dj < 3:
                                col = u * 128 + v * 64
                                w2_full[row : row + 32, col : col + 64] = w2_ref[di * 3 + dj]
    for k in range(9):
        w3_full[k * 64 : (k + 1) * 64, :] = w3_ref[k]
    w3_full[576:640, :] = jnp.zeros((64, 128), jnp.bfloat16)


def inside_map(lo, hi, where):
    shape = (hi - lo, PITCH, 128)
    at_f = lax.broadcasted_iota(jnp.int32, shape, 0) + (where[1] - 2 + lo)
    at_p = lax.broadcasted_iota(jnp.int32, shape, 1) + (where[0] - 2)
    inside = (at_f >= 0) & (at_f < where[3]) & (at_p >= 0) & (at_p < where[2])
    return jnp.where(inside, 1.0, 0.0).reshape((hi - lo) * PITCH, 128)


def conv1(lo, hi, where, map_ref, w1_full, b1_full, z_buf, x_buf, first_buf):
    wide, frames = map_ref.shape[1:]
    top = max(0, (4 * lo - 1) // 8 * 8)
    end = min(wide, -(-(4 * hi + 3) // 8) * 8)
    source = lax.broadcasted_iota(jnp.int32, (3 * frames, 128), 0)
    target = lax.broadcasted_iota(jnp.int32, (3 * frames, 128), 1)
    whole = jnp.concatenate([map_ref[k, top:end] for k in range(3)], axis=1)
    high = whole.astype(jnp.bfloat16)
    lower = (whole - high.astype(jnp.float32)).astype(jnp.bfloat16)
    for rr in range(6):
        pick = jnp.where(source == 4 * target + (frames - 9) + rr, 1.0, 0.0).astype(jnp.bfloat16)
        for part, value in enumerate((high, lower)):
            z_buf[part, 8 + top : 8 + end, rr * 128 : (rr + 1) * 128] = jnp.dot(
                value, pick, preferred_element_type=jnp.float32
            )
    for block in range(lo, hi):
        pieces = []
        for part in (0, 1, 0):
            for rr in range(6):
                pieces.append(
                    z_buf[part, 4 * block + 7 : 4 * block + 15, rr * 128 : (rr + 1) * 128]
                )
        flat = jnp.concatenate(pieces, axis=0)
        x_buf[block * PITCH : (block + 1) * PITCH, :] = jnp.transpose(flat)[:PITCH]

    made = jnp.dot(
        x_buf[lo * PITCH : hi * PITCH].astype(jnp.bfloat16), w1_full[...],
        preferred_element_type=jnp.float32,
    )
    best = jnp.maximum(
        jnp.maximum(made[:, 0:128], made[:, 128:256]),
        jnp.maximum(made[:, 256:384], made[:, 384:512]),
    )
    first = jnp.maximum(best + b1_full[...], 0.0)
    first = jnp.where(inside_map(lo, hi, where) > 0.5, first, 0.0)
    first = first.astype(jnp.bfloat16).astype(jnp.float32)
    first_buf[LEAD + lo * PITCH : LEAD + hi * PITCH, :] = first


def conv2(lo, hi, where, w2_full, b2_full, first_buf, second_buf):
    lane = lax.broadcasted_iota(jnp.int32, (1, 128), 1)
    low_a = lane < 64
    low_b = (lane % 64) < 32
    rows = (hi - lo) * PITCH
    here = LEAD + lo * PITCH
    start = here - PITCH
    more = rows + 2 * PITCH
    first = first_buf[here : here + rows, :]
    shifted = jnp.where(
        low_a, first_buf[start + 1 : start + 1 + more, :], first_buf[start - 1 : start - 1 + more, :]
    )
    across = jnp.where(
        low_b, first_buf[here + PITCH : here + PITCH + rows, :], first_buf[start : start + rows, :]
    )
    both = jnp.where(low_b, shifted[2 * PITCH :], shifted[:rows])
    stacked = jnp.concatenate(
        [first, across, shifted[PITCH : PITCH + rows], both], axis=1
    ).astype(jnp.bfloat16)
    made = jnp.dot(stacked, w2_full[...], preferred_element_type=jnp.float32)
    best = jnp.maximum(made[:, 0:128], made[:, 128:256])
    best = jnp.maximum(best, pltpu.roll(best, 64, 1))
    second = jnp.maximum(best + b2_full[...], 0.0)
    second = jnp.where(inside_map(lo, hi, where) > 0.5, second, 0.0)
    second_buf[here : here + rows, :] = second.astype(jnp.bfloat16).astype(jnp.float32)


def conv3(lo, hi, w3_full, b3_ref, w4_ref, second_buf):
    lane = lax.broadcasted_iota(jnp.int32, (1, 128), 1)
    low_a = lane < 64
    rows = (hi - lo) * PITCH

    def moved(k):
        di, dj = k // 3, k % 3
        begin = LEAD + (lo + dj - 1) * PITCH + di - 1
        return second_buf[begin : begin + rows, :]

    groups = []
    for k in range(0, 9, 2):
        groups.append(jnp.where(low_a, moved(k), moved(k + 1)) if k < 8 else moved(k))
    stacked = jnp.concatenate(groups, axis=1).astype(jnp.bfloat16)
    made = jnp.dot(stacked, w3_full[...], preferred_element_type=jnp.float32)
    third = jnp.maximum(made + b3_ref[...], 0.0).astype(jnp.bfloat16).astype(jnp.float32)
    weighted = third * w4_ref[...].astype(jnp.float32)
    return jnp.sum(weighted.reshape(hi - lo, PITCH, 128), axis=2)


def body(
    query_feats, ref_feats, pair_table, lengths, query_len, conv1_weight, conv1_bias,
    conv2_weight, conv2_bias, conv3_weight, conv3_bias, conv4_weight, conv4_bias,
):
    senders = lax.axis_size("qry")
    others = lax.axis_size("ref")
    frames, regions, depth = query_feats.shape
    query_mat = jnp.transpose(query_feats, (1, 0, 2)).reshape(regions * frames, depth)
    ref_mat = jnp.transpose(ref_feats, (1, 2, 0, 3)).reshape(regions, -1, depth)
    videos = lengths.shape[0]
    shard = ref_mat.shape[1]
    chunks = shard // GROUP
    chips = senders // 2
    steps = max(1, chips - 1)
    cuts = [depth * k // 6 // 128 * 128 for k in range(7)]
    pieces = len(cuts) - 1
    tiles = frames // 4
    side = tiles + 4
    rows = side * PITCH
    scale = 1.0 / (regions * math.sqrt(depth))
    vmem = pl.BlockSpec(memory_space=pltpu.VMEM)
    smem = pl.BlockSpec(memory_space=pltpu.SMEM)
    hbm = pl.BlockSpec(memory_space=pltpu.HBM)
    dma = pltpu.SemaphoreType.DMA
    f32, bf16 = jnp.float32, jnp.bfloat16
    operands = (
        pair_table,
        lengths,
        query_len,
        conv4_bias,
        conv1_weight,
        conv1_bias[None],
        jnp.transpose(conv2_weight, (0, 1, 3, 2)).reshape(
            9, conv2_weight.shape[3], conv2_weight.shape[2]
        ),
        conv2_bias[None],
        jnp.transpose(conv3_weight, (0, 1, 3, 2)).reshape(
            9, conv3_weight.shape[3], conv3_weight.shape[2]
        ),
        conv3_bias[None],
        conv4_weight[None],
        query_mat,
        ref_mat,
    )
    kept = [
        (pltpu.SMEM if k < 4 else pltpu.VMEM)(operand.shape, operand.dtype)
        for k, operand in enumerate(operands[:11])
    ]
    scores, totals = pl.pallas_call(
        functools.partial(whole_kernel, chips, others, scale, cuts),
        out_shape=(
            jax.ShapeDtypeStruct((tiles, tiles), f32),
            jax.ShapeDtypeStruct((videos,), f32),
        ),
        in_specs=[hbm] * len(operands),
        out_specs=(vmem, smem),
        scratch_shapes=kept + [
            pltpu.VMEM(query_mat.shape, bf16),
            pltpu.VMEM((2, chunks, regions, GROUP, depth), bf16),
            pltpu.VMEM((steps, chunks, 2, regions, GROUP, depth), bf16),
            pltpu.VMEM((2 * regions * GROUP, regions * frames), f32),
            pltpu.VMEM((senders, shard, frames), f32),
            pltpu.VMEM((3, frames + 2 * HALO, frames), f32),
            pltpu.VMEM((2, frames + 4 * HALO, 768), f32),
            pltpu.VMEM((rows, 144), f32),
            pltpu.VMEM((rows + 2 * LEAD, 128), f32),
            pltpu.VMEM((rows + 2 * LEAD, 128), f32),
            pltpu.VMEM((16, 128), f32),
            pltpu.VMEM((48, 512), f32),
            pltpu.VMEM((144, 512), bf16),
            pltpu.VMEM((512, 256), bf16),
            pltpu.VMEM((640, 128), bf16),
            pltpu.VMEM((1, 128), f32),
            pltpu.VMEM((1, 128), f32),
            pltpu.VMEM((-(-side // 8) * 8, 128), f32),
            pltpu.VMEM((senders * others, videos, 128), f32),
            dma((11,)),
            dma((regions,)),
            dma((chunks,)),
            dma((chunks,)),
            dma((chunks,)),
            dma((steps, chunks, pieces)),
            dma((steps, chunks, pieces)),
            dma((steps, chunks, pieces)),
            dma((steps, chunks, pieces)),
            dma((2 * chunks + 6,)),
            dma((2 * chunks + 6,)),
            dma((senders * others,)),
            dma((senders * others,)),
            pltpu.SemaphoreType.REGULAR((max(1, others - 1),)),
        ],
        compiler_params=pltpu.CompilerParams(
            collective_id=0, has_side_effects=True, vmem_limit_bytes=56 << 20
        ),
        name="whole",
    )(*operands)
    return (scores, totals)


def solution(mesh):
    placed = (
        P(("groups", "qry"), None, None),
        P(("groups", "ref"), "qry", None, None),
        P("groups", None),
        P("groups"),
        P("groups"),
    ) + (P(),) * 8
    return jax.shard_map(
        body,
        mesh=mesh,
        in_specs=placed,
        out_specs=(P(("groups", "qry"), "ref"), P("groups")),
        check_vma=False,
    )
```

```python
import functools
import math

import jax
import jax.numpy as jnp
from jax import lax
from jax.experimental import pallas as pl
from jax.experimental.pallas import tpu as pltpu
from jax.sharding import PartitionSpec as P

MESH = pl.DeviceIdType.MESH
HALO = 8
PITCH = 40
LEAD = 48
GROUP = 8
NT = (((1,), (1,)), ((), ()))


def spans(flags):
    found = []
    for k, flag in enumerate(flags):
        if flag and (k == 0 or not flags[k - 1]):
            found.append([k, k + 1])
        elif flag:
            found[-1][1] = k + 1
    return [tuple(span) for span in found]


def plan(stages, chunks, frames, tiles):
    side = tiles + 4
    width = frames // chunks
    here, finished, work = set(), [[False] * side for _ in range(3)], []
    for stage in stages:
        here |= set(stage)
        ready = []
        for j in range(side):
            known = True
            for k in range(-1, 5):
                frame = 4 * (j - 2) + k
                outside = chunks - 1 if frame < 0 else 0
                known &= (frame // width if 0 <= frame < frames else outside) in here
            ready.append(known)
        layers = []
        for layer in range(3):
            if layer:
                edge = [False] * layer
                ready = [all(ready[j - 1 : j + 2]) for j in range(layer, side - layer)]
                ready = edge + ready + edge
            layers.append(spans([now and not was for now, was in zip(ready, finished[layer])]))
            finished[layer] = ready
        work.append(layers)
    return work


def chunk_order(chunks):
    return [k // 2 if k % 2 == 0 else chunks - 1 - k // 2 for k in range(chunks)]


def whole_kernel(
    chips, others, scale, cuts,
    pair_hbm, lengths_hbm, len_hbm, b4_hbm, w1_hbm, b1_hbm, w2_hbm, b2_hbm, w3_hbm, b3_hbm,
    w4_hbm, q_hbm, r_hbm,
    scores_ref, totals_ref,
    pair_ref, lengths_ref, len_ref, b4_ref, w1_ref, b1_ref, w2_ref, b2_ref, w3_ref, b3_ref, w4_ref,
    q_buf, r_own, r_far, acc, sims_buf, map_buf, z_buf, x_buf, first_buf, second_buf,
    w1_rep, w1_flat, w1_full, w2_full, w3_full, b1_full, b2_full, score_buf, peaks_buf,
    small_sem, q_sem, own_sem, send_o, recv_o, send_x, recv_x, send_s, recv_s, send_h, recv_h,
    send_p, recv_p, far_sem,
):
    regions, shard, depth = r_hbm.shape
    frames = q_hbm.shape[0] // regions
    chunks = shard // GROUP
    width = GROUP * 2 * chips
    tiles = frames // 4
    order = chunk_order(chunks)
    last = order[-1]
    me = lax.axis_index("qry")
    chip = me // 2
    core = me % 2
    sibling = chip * 2 + (1 - core)
    right = ((chip + 1) % chips) * 2 + core
    senders = 2 * chips
    col = lax.axis_index("ref")
    peers = senders * others
    mine = me * others + col

    smalls = [
        pltpu.make_async_copy(source, target, small_sem.at[k])
        for k, (source, target) in enumerate(
            (
                (w1_hbm, w1_ref), (b1_hbm, b1_ref), (w2_hbm, w2_ref), (b2_hbm, b2_ref),
                (w3_hbm, w3_ref), (b3_hbm, b3_ref), (w4_hbm, w4_ref), (pair_hbm, pair_ref),
                (lengths_hbm, lengths_ref), (len_hbm, len_ref), (b4_hbm, b4_ref),
            )
        )
    ]

    def piece(p):
        return pl.ds(cuts[p], cuts[p + 1] - cuts[p])

    pieces = len(cuts) - 1

    def rows_of(g):
        return pl.ds(pl.multiple_of(g * GROUP, GROUP), GROUP)

    def own_copy(g):
        return pltpu.make_async_copy(r_hbm.at[:, rows_of(g)], r_own.at[0, g], own_sem.at[g])

    def own_to_sibling(g):
        return pltpu.make_async_remote_copy(
            src_ref=r_hbm.at[:, rows_of(g)],
            dst_ref=r_own.at[1, g],
            send_sem=send_o.at[g],
            recv_sem=recv_o.at[g],
            device_id={"qry": sibling},
            device_id_type=MESH,
        )

    def q_copy(k):
        rows = pl.ds(k * frames, frames)
        return pltpu.make_async_copy(q_hbm.at[rows], q_buf.at[rows], q_sem.at[k])

    def to_right(step, g, p):
        if step == 0:
            source = r_hbm.at[:, rows_of(g), piece(p)]
        else:
            source = r_far.at[step - 1, g, 0, :, :, piece(p)]
        return pltpu.make_async_remote_copy(
            src_ref=source,
            dst_ref=r_far.at[step, g, 0, :, :, piece(p)],
            send_sem=send_x.at[step, g, p],
            recv_sem=recv_x.at[step, g, p],
            device_id={"qry": right},
            device_id_type=MESH,
        )

    def to_sibling(step, g, p):
        return pltpu.make_async_remote_copy(
            src_ref=r_far.at[step, g, 0, :, :, piece(p)],
            dst_ref=r_far.at[step, g, 1, :, :, piece(p)],
            send_sem=send_s.at[step, g, p],
            recv_sem=recv_s.at[step, g, p],
            device_id={"qry": sibling},
            device_id_type=MESH,
        )

    for k in range(regions):
        q_copy(k).start()
    for g in range(chunks):
        own_copy(g).start()
    map_buf[...] = jnp.zeros_like(map_buf)
    barrier = pltpu.get_barrier_semaphore()
    for k in range(1, senders):
        device = {"qry": (me + k) % senders}
        pl.semaphore_signal(barrier, inc=1, device_id=device, device_id_type=MESH)

    def tell_columns(semaphore):
        for move, there in ((-1, col > 0), (1, col < others - 1)):

            @pl.when(there)
            def _():
                pl.semaphore_signal(
                    semaphore, inc=1, device_id={"ref": col + move}, device_id_type=MESH
                )

    columns_near = jnp.where(col > 0, 1, 0) + jnp.where(col < others - 1, 1, 0)
    tell_columns(barrier)
    pl.semaphore_wait(barrier, senders - 1 + columns_near)

    def enqueue(lo, hi):
        for k in range(lo, min(hi, chunks * pieces)):
            to_right(0, order[k // pieces], k % pieces).start()

    limits = [(chunks - 1) * pieces - 1] * chunks + [chunks * pieces - 2, chunks * pieces]
    limits = [max(limit, 0) for limit in limits[-chunks:]] if chunks > 1 else [pieces]
    enqueue(0, limits[0])
    for g in range(chunks):
        own_to_sibling(g).start()
    rounds = others - 1
    if rounds:
        tell_columns(far_sem.at[0])

    def next_round(k):
        if k < rounds:
            pl.semaphore_wait(far_sem.at[k], columns_near)
            if k + 1 < rounds:
                tell_columns(far_sem.at[k + 1])

    for copy in smalls:
        copy.start()
    z_buf[...] = jnp.zeros_like(z_buf)
    first_buf[...] = jnp.zeros_like(first_buf)
    second_buf[...] = jnp.zeros_like(second_buf)
    next_round(0)
    for copy in smalls:
        copy.wait()
    build_weights(
        w1_ref, w2_ref, w3_ref, b1_ref, b2_ref, w1_rep, w1_flat, w1_full, w2_full, w3_full,
        b1_full, b2_full,
    )
    next_round(1)
    factor = pair_ref[me, col].astype(jnp.float32) * scale

    def similar(product, blocks):
        best = jnp.max(product.reshape(blocks, regions, GROUP, regions * frames), axis=1)
        total = best[:, :, :frames]
        for k in range(1, regions):
            total = total + best[:, :, k * frames : (k + 1) * frames]
        return total * factor

    def near(side):
        product = lax.dot_general(
            r_own[side].reshape(chunks * regions * GROUP, depth), q_buf[...], NT,
            preferred_element_type=jnp.float32,
        )
        return similar(product, chunks).reshape(shard, frames)

    for k in range(regions):
        q_copy(k).wait()
    for g in range(chunks):
        own_copy(g).wait()

    def near_side(side, carry):
        @pl.when(side == 1)
        def _():
            for g in range(chunks):
                own_to_sibling(g).wait_recv()

        sims_buf[chip * 2 + side * (1 - core) + (1 - side) * core] = near(side)
        return carry

    lax.fori_loop(0, 2, near_side, 0)
    for k in range(2, rounds):
        next_round(k)

    def sources(step):
        origin = (chip + chips - 1 - step) % chips
        return origin * 2 + core, origin * 2 + (1 - core)

    def arrive(step, g, p):
        to_right(step, g, p).wait_recv()
        to_sibling(step, g, p).start()
        if step < chips - 2:
            to_right(step + 1, g, p).start()

    def part(step, g, first_piece, final_piece):
        columns = pl.ds(cuts[first_piece], cuts[final_piece] - cuts[first_piece])
        block = r_far[step, g, :, :, :, columns].reshape(2 * regions * GROUP, columns.size)
        return lax.dot_general(
            block, q_buf[:, columns], NT, preferred_element_type=jnp.float32
        )

    def keep(step, g, product):
        total = similar(product, 2)
        for k, source in enumerate(sources(step)):
            sims_buf[source, rows_of(g)] = total[k]

    def reachable(move_q, move_r):
        fits = (me + move_q >= 0) & (me + move_q < senders)
        return fits & (col + move_r >= 0) & (col + move_r < others)

    def halo_copy(k, move_q, move_r, g):
        if move_r == 0:
            source = target = pl.ds(HALO + g * width, width)
        elif move_r == 1:
            source, target = pl.ds(frames, HALO), pl.ds(0, HALO)
        else:
            source, target = pl.ds(HALO, HALO), pl.ds(HALO + frames, HALO)
        return pltpu.make_async_remote_copy(
            src_ref=map_buf.at[1, source],
            dst_ref=map_buf.at[1 - move_q, target],
            send_sem=send_h.at[k],
            recv_sem=recv_h.at[k],
            device_id={"qry": me + move_q, "ref": col + move_r},
            device_id_type=MESH,
        )

    moves = [(q, 0, g) for g in range(chunks) for q in (-1, 1)]
    moves += [(q, r, 0 if r < 0 else chunks - 1) for r in (-1, 1) for q in (-1, 1, 0)]
    moves = list(enumerate(moves))

    def spread(g):
        for b in range(senders):
            rows = pl.ds(HALO + g * width + b, GROUP, stride=senders)
            map_buf.at[1][rows, :] = sims_buf[b, g * GROUP : (g + 1) * GROUP]
        for k, (q, r, source) in moves:
            if source == g:

                @pl.when(reachable(q, r))
                def _():
                    halo_copy(k, q, r, g).start()

    def halos(stage):
        for k, (q, r, g) in moves:
            if g in stage:

                @pl.when(reachable(-q, -r))
                def _():
                    halo_copy(k, q, r, g).wait_recv()

    where = (me * tiles, col * tiles, senders * tiles, others * tiles)
    stages = (order[: max(chunks - 2, 0)], order[max(chunks - 2, 0) : chunks - 1], [last])
    work = plan(stages, chunks, frames, tiles)

    def network(k):
        halos(stages[k])
        for lo, hi in work[k][0]:
            conv1(lo, hi, where, map_buf, w1_full, b1_full, z_buf, x_buf, first_buf)
        for lo, hi in work[k][1]:
            conv2(lo, hi, where, w2_full, b2_full, first_buf, second_buf)
        for lo, hi in work[k][2]:
            score_buf[lo:hi, :PITCH] = conv3(lo, hi, w3_full, b3_ref, w4_ref, second_buf)

    for k, g in enumerate(order[:-1]):
        for step in range(chips - 1):
            for p in range(pieces):
                arrive(step, g, p)
            for p in range(pieces):
                to_sibling(step, g, p).wait_recv()
            keep(step, g, part(step, g, 0, pieces))
        spread(g)
        enqueue(limits[k], limits[k + 1])
    network(0)

    for step in range(chips - 1):
        for lo, hi in ((0, pieces - 3), (pieces - 3, pieces - 1), (pieces - 1, pieces)):
            for p in range(lo, hi):
                if lo == 0 or p > pieces - 3:
                    arrive(step, last, p)
            for p in range(lo, hi):
                to_sibling(step, last, p).wait_recv()
            if lo == 0:
                acc[...] = part(step, last, lo, hi)
                arrive(step, last, pieces - 3)
                if step == 0:
                    network(1)
            elif hi < pieces:
                acc[...] += part(step, last, lo, hi)
            else:
                keep(step, last, acc[...] + part(step, last, lo, hi))
    spread(last)
    network(2)

    scores = score_buf[...] + b4_ref[0]
    slot_f = lax.broadcasted_iota(jnp.int32, scores.shape, 0)
    column = slot_f + (col * tiles - 2)
    own = (slot_f >= 2) & (slot_f < 2 + tiles)
    begin = jnp.int32(0)
    for v in range(lengths_ref.shape[0]):
        end = begin + lengths_ref[v]
        member = own & (column >= begin) & (column < end)
        peaks_buf[mine, v : v + 1, :] = jnp.max(
            jnp.where(member, scores, -jnp.inf), axis=0, keepdims=True
        )
        begin = end

    def peak_copy(k):
        peer = (mine + k) % peers
        return pltpu.make_async_remote_copy(
            src_ref=peaks_buf.at[mine],
            dst_ref=peaks_buf.at[mine],
            send_sem=send_p.at[k],
            recv_sem=recv_p.at[mine],
            device_id={"qry": peer // others, "ref": peer % others},
            device_id_type=MESH,
        )

    def peak_wait(k, carry):
        peer = (mine + k) % peers
        pltpu.make_async_remote_copy(
            src_ref=peaks_buf.at[peer],
            dst_ref=peaks_buf.at[peer],
            send_sem=send_p.at[k],
            recv_sem=recv_p.at[peer],
            device_id={"qry": peer // others, "ref": peer % others},
            device_id_type=MESH,
        ).wait_recv()
        return carry

    def peak_start(k, carry):
        peak_copy(k).start()
        return carry

    lax.fori_loop(1, peers, peak_start, 0)
    scores_ref[...] = jnp.transpose(scores)[2 : 2 + tiles, 2 : 2 + tiles]

    def drain(g, carry):
        own_to_sibling(g).wait_send()
        for step in range(chips - 1):
            for p in range(pieces):
                to_right(step, g, p).wait_send()
                to_sibling(step, g, p).wait_send()
        return carry

    lax.fori_loop(0, chunks, drain, 0)
    for k, (q, r, g) in moves:

        @pl.when(reachable(q, r))
        def _():
            halo_copy(k, q, r, g).wait_send()

    lax.fori_loop(1, peers, peak_wait, 0)
    lane = lax.broadcasted_iota(jnp.int32, peaks_buf.shape[1:], 1)
    total = jnp.zeros(peaks_buf.shape[1:], jnp.float32)
    for s in range(senders):
        best = jnp.max(peaks_buf[s * others : (s + 1) * others], axis=0)
        counted = (lane >= 2) & (lane < 2 + tiles) & (lane + (s * tiles - 2) < len_ref[0])
        total = total + jnp.where(counted, best, 0.0)
    total = jnp.sum(total, axis=1, keepdims=True) / len_ref[0].astype(jnp.float32)
    for v in range(lengths_ref.shape[0]):
        totals_ref[v] = jnp.sum(total[v : v + 1])

    def peak_drain(k, carry):
        peak_copy(k).wait_send()
        return carry

    lax.fori_loop(1, peers, peak_drain, 0)


def build_weights(
    w1_ref, w2_ref, w3_ref, b1_ref, b2_ref, w1_rep, w1_flat, w1_full, w2_full, w3_full,
    b1_full, b2_full,
):
    for k in range(4):
        lanes = slice(k * 32, (k + 1) * 32)
        b1_full[:, lanes] = b1_ref[...]
        for di in range(3):
            w1_rep[3 * di : 3 * di + 3, lanes] = w1_ref[di]
    for k in range(2):
        b2_full[:, k * 64 : (k + 1) * 64] = b2_ref[...]
    w1_flat[...] = jnp.zeros_like(w1_flat)
    for u in range(2):
        for v in range(2):
            for a in range(2):
                for b in range(2):
                    at = (a * 2 + b) * 32
                    col = (u * 2 + v) * 128 + at
                    for k in range(9):
                        row = (2 * a + u + k // 3) * 8 + 2 * b + v + k % 3
                        w1_flat[row : row + 1, col : col + 32] = w1_rep[k : k + 1, at : at + 32]
    flat = w1_flat[...]
    high = flat.astype(jnp.bfloat16)
    w1_full[0:48] = high
    w1_full[48:96] = high
    w1_full[96:144] = (flat - high.astype(jnp.float32)).astype(jnp.bfloat16)

    w2_full[...] = jnp.zeros_like(w2_full)
    taps = {(0, 0): 0, (0, 1): 1, (1, 0): 2, (1, 1): -1}
    for g in range(2):
        for h in range(2):
            for a in range(2):
                for b in range(2):
                    row = ((g * 2 + h) * 4 + a * 2 + b) * 32
                    for u in range(2):
                        for v in range(2):
                            di = taps[g, a] - u + 1
                            dj = taps[h, b] - v + 1
                            if 0 <= di < 3 and 0 <= dj < 3:
                                col = u * 128 + v * 64
                                w2_full[row : row + 32, col : col + 64] = w2_ref[di * 3 + dj]
    for k in range(9):
        w3_full[k * 64 : (k + 1) * 64, :] = w3_ref[k]
    w3_full[576:640, :] = jnp.zeros((64, 128), jnp.bfloat16)


def inside_map(lo, hi, where):
    shape = (hi - lo, PITCH, 128)
    at_f = lax.broadcasted_iota(jnp.int32, shape, 0) + (where[1] - 2 + lo)
    at_p = lax.broadcasted_iota(jnp.int32, shape, 1) + (where[0] - 2)
    inside = (at_f >= 0) & (at_f < where[3]) & (at_p >= 0) & (at_p < where[2])
    return jnp.where(inside, 1.0, 0.0).reshape((hi - lo) * PITCH, 128)


def conv1(lo, hi, where, map_ref, w1_full, b1_full, z_buf, x_buf, first_buf):
    wide, frames = map_ref.shape[1:]
    top = max(0, (4 * lo - 1) // 8 * 8)
    end = min(wide, -(-(4 * hi + 3) // 8) * 8)
    source = lax.broadcasted_iota(jnp.int32, (3 * frames, 128), 0)
    target = lax.broadcasted_iota(jnp.int32, (3 * frames, 128), 1)
    whole = jnp.concatenate([map_ref[k, top:end] for k in range(3)], axis=1)
    high = whole.astype(jnp.bfloat16)
    lower = (whole - high.astype(jnp.float32)).astype(jnp.bfloat16)
    for rr in range(6):
        pick = jnp.where(source == 4 * target + (frames - 9) + rr, 1.0, 0.0).astype(jnp.bfloat16)
        for part, value in enumerate((high, lower)):
            z_buf[part, 8 + top : 8 + end, rr * 128 : (rr + 1) * 128] = jnp.dot(
                value, pick, preferred_element_type=jnp.float32
            )
    for block in range(lo, hi):
        pieces = []
        for part in (0, 1, 0):
            for rr in range(6):
                pieces.append(
                    z_buf[part, 4 * block + 7 : 4 * block + 15, rr * 128 : (rr + 1) * 128]
                )
        flat = jnp.concatenate(pieces, axis=0)
        x_buf[block * PITCH : (block + 1) * PITCH, :] = jnp.transpose(flat)[:PITCH]

    made = jnp.dot(
        x_buf[lo * PITCH : hi * PITCH].astype(jnp.bfloat16), w1_full[...],
        preferred_element_type=jnp.float32,
    )
    best = jnp.maximum(
        jnp.maximum(made[:, 0:128], made[:, 128:256]),
        jnp.maximum(made[:, 256:384], made[:, 384:512]),
    )
    first = jnp.maximum(best + b1_full[...], 0.0)
    first = jnp.where(inside_map(lo, hi, where) > 0.5, first, 0.0)
    first = first.astype(jnp.bfloat16).astype(jnp.float32)
    first_buf[LEAD + lo * PITCH : LEAD + hi * PITCH, :] = first


def conv2(lo, hi, where, w2_full, b2_full, first_buf, second_buf):
    lane = lax.broadcasted_iota(jnp.int32, (1, 128), 1)
    low_a = lane < 64
    low_b = (lane % 64) < 32
    rows = (hi - lo) * PITCH
    here = LEAD + lo * PITCH
    start = here - PITCH
    more = rows + 2 * PITCH
    first = first_buf[here : here + rows, :]
    shifted = jnp.where(
        low_a, first_buf[start + 1 : start + 1 + more, :], first_buf[start - 1 : start - 1 + more, :]
    )
    across = jnp.where(
        low_b, first_buf[here + PITCH : here + PITCH + rows, :], first_buf[start : start + rows, :]
    )
    both = jnp.where(low_b, shifted[2 * PITCH :], shifted[:rows])
    stacked = jnp.concatenate(
        [first, across, shifted[PITCH : PITCH + rows], both], axis=1
    ).astype(jnp.bfloat16)
    made = jnp.dot(stacked, w2_full[...], preferred_element_type=jnp.float32)
    best = jnp.maximum(made[:, 0:128], made[:, 128:256])
    best = jnp.maximum(best, pltpu.roll(best, 64, 1))
    second = jnp.maximum(best + b2_full[...], 0.0)
    second = jnp.where(inside_map(lo, hi, where) > 0.5, second, 0.0)
    second_buf[here : here + rows, :] = second.astype(jnp.bfloat16).astype(jnp.float32)


def conv3(lo, hi, w3_full, b3_ref, w4_ref, second_buf):
    lane = lax.broadcasted_iota(jnp.int32, (1, 128), 1)
    low_a = lane < 64
    rows = (hi - lo) * PITCH

    def moved(k):
        di, dj = k // 3, k % 3
        begin = LEAD + (lo + dj - 1) * PITCH + di - 1
        return second_buf[begin : begin + rows, :]

    groups = []
    for k in range(0, 9, 2):
        groups.append(jnp.where(low_a, moved(k), moved(k + 1)) if k < 8 else moved(k))
    stacked = jnp.concatenate(groups, axis=1).astype(jnp.bfloat16)
    made = jnp.dot(stacked, w3_full[...], preferred_element_type=jnp.float32)
    third = jnp.maximum(made + b3_ref[...], 0.0).astype(jnp.bfloat16).astype(jnp.float32)
    weighted = third * w4_ref[...].astype(jnp.float32)
    return jnp.sum(weighted.reshape(hi - lo, PITCH, 128), axis=2)


def body(
    query_feats, ref_feats, pair_table, lengths, query_len, conv1_weight, conv1_bias,
    conv2_weight, conv2_bias, conv3_weight, conv3_bias, conv4_weight, conv4_bias,
):
    senders = lax.axis_size("qry")
    others = lax.axis_size("ref")
    frames, regions, depth = query_feats.shape
    query_mat = jnp.transpose(query_feats, (1, 0, 2)).reshape(regions * frames, depth)
    ref_mat = jnp.transpose(ref_feats, (1, 2, 0, 3)).reshape(regions, -1, depth)
    videos = lengths.shape[0]
    shard = ref_mat.shape[1]
    chunks = shard // GROUP
    chips = senders // 2
    steps = max(1, chips - 1)
    cuts = [depth * k // 6 // 128 * 128 for k in range(7)]
    pieces = len(cuts) - 1
    tiles = frames // 4
    side = tiles + 4
    rows = side * PITCH
    scale = 1.0 / (regions * math.sqrt(depth))
    vmem = pl.BlockSpec(memory_space=pltpu.VMEM)
    smem = pl.BlockSpec(memory_space=pltpu.SMEM)
    hbm = pl.BlockSpec(memory_space=pltpu.HBM)
    dma = pltpu.SemaphoreType.DMA
    f32, bf16 = jnp.float32, jnp.bfloat16
    operands = (
        pair_table,
        lengths,
        query_len,
        conv4_bias,
        conv1_weight,
        conv1_bias[None],
        jnp.transpose(conv2_weight, (0, 1, 3, 2)).reshape(
            9, conv2_weight.shape[3], conv2_weight.shape[2]
        ),
        conv2_bias[None],
        jnp.transpose(conv3_weight, (0, 1, 3, 2)).reshape(
            9, conv3_weight.shape[3], conv3_weight.shape[2]
        ),
        conv3_bias[None],
        conv4_weight[None],
        query_mat,
        ref_mat,
    )
    kept = [
        (pltpu.SMEM if k < 4 else pltpu.VMEM)(operand.shape, operand.dtype)
        for k, operand in enumerate(operands[:11])
    ]
    scores, totals = pl.pallas_call(
        functools.partial(whole_kernel, chips, others, scale, cuts),
        out_shape=(
            pltpu.VMEM((tiles, tiles), f32),
            pltpu.SMEM((videos,), f32),
        ),
        in_specs=[hbm] * len(operands),
        out_specs=(vmem, smem),
        scratch_shapes=kept + [
            pltpu.VMEM(query_mat.shape, bf16),
            pltpu.VMEM((2, chunks, regions, GROUP, depth), bf16),
            pltpu.VMEM((steps, chunks, 2, regions, GROUP, depth), bf16),
            pltpu.VMEM((2 * regions * GROUP, regions * frames), f32),
            pltpu.VMEM((senders, shard, frames), f32),
            pltpu.VMEM((3, frames + 2 * HALO, frames), f32),
            pltpu.VMEM((2, frames + 4 * HALO, 768), f32),
            pltpu.VMEM((rows, 144), f32),
            pltpu.VMEM((rows + 2 * LEAD, 128), f32),
            pltpu.VMEM((rows + 2 * LEAD, 128), f32),
            pltpu.VMEM((16, 128), f32),
            pltpu.VMEM((48, 512), f32),
            pltpu.VMEM((144, 512), bf16),
            pltpu.VMEM((512, 256), bf16),
            pltpu.VMEM((640, 128), bf16),
            pltpu.VMEM((1, 128), f32),
            pltpu.VMEM((1, 128), f32),
            pltpu.VMEM((-(-side // 8) * 8, 128), f32),
            pltpu.VMEM((senders * others, videos, 128), f32),
            dma((11,)),
            dma((regions,)),
            dma((chunks,)),
            dma((chunks,)),
            dma((chunks,)),
            dma((steps, chunks, pieces)),
            dma((steps, chunks, pieces)),
            dma((steps, chunks, pieces)),
            dma((steps, chunks, pieces)),
            dma((2 * chunks + 6,)),
            dma((2 * chunks + 6,)),
            dma((senders * others,)),
            dma((senders * others,)),
            pltpu.SemaphoreType.REGULAR((max(1, others - 1),)),
        ],
        compiler_params=pltpu.CompilerParams(
            collective_id=0, has_side_effects=True, vmem_limit_bytes=56 << 20
        ),
        name="whole",
    )(*operands)
    return (scores, totals)


def solution(mesh):
    placed = (
        P(("groups", "qry"), None, None),
        P(("groups", "ref"), "qry", None, None),
        P("groups", None),
        P("groups"),
        P("groups"),
    ) + (P(),) * 8
    return jax.shard_map(
        body,
        mesh=mesh,
        in_specs=placed,
        out_specs=(P(("groups", "qry"), "ref"), P("groups")),
        check_vma=False,
    )
```

```python
import functools
import math

import jax
import jax.numpy as jnp
from jax import lax
from jax.experimental import pallas as pl
from jax.experimental.pallas import tpu as pltpu
from jax.sharding import PartitionSpec as P

MESH = pl.DeviceIdType.MESH
HALO = 8
PITCH = 40
LEAD = 48
GROUP = 8
NT = (((1,), (1,)), ((), ()))


def spans(flags):
    found = []
    for k, flag in enumerate(flags):
        if flag and (k == 0 or not flags[k - 1]):
            found.append([k, k + 1])
        elif flag:
            found[-1][1] = k + 1
    return [tuple(span) for span in found]


def plan(stages, chunks, frames, tiles):
    side = tiles + 4
    width = frames // chunks
    here, finished, work = set(), [[False] * side for _ in range(3)], []
    for stage in stages:
        here |= set(stage)
        ready = []
        for j in range(side):
            known = True
            for k in range(-1, 5):
                frame = 4 * (j - 2) + k
                outside = chunks - 1 if frame < 0 else 0
                known &= (frame // width if 0 <= frame < frames else outside) in here
            ready.append(known)
        layers = []
        for layer in range(3):
            if layer:
                edge = [False] * layer
                ready = [all(ready[j - 1 : j + 2]) for j in range(layer, side - layer)]
                ready = edge + ready + edge
            layers.append(spans([now and not was for now, was in zip(ready, finished[layer])]))
            finished[layer] = ready
        work.append(layers)
    return work


def chunk_order(chunks):
    return [k // 2 if k % 2 == 0 else chunks - 1 - k // 2 for k in range(chunks)]


def whole_kernel(
    chips, others, scale, cuts,
    pair_hbm, lengths_hbm, len_hbm, b4_hbm, w1_hbm, b1_hbm, w2_hbm, b2_hbm, w3_hbm, b3_hbm,
    w4_hbm, q_hbm, r_hbm,
    scores_ref, totals_ref,
    pair_ref, lengths_ref, len_ref, b4_ref, w1_ref, b1_ref, w2_ref, b2_ref, w3_ref, b3_ref, w4_ref,
    q_buf, r_own, r_far, acc, sims_buf, map_buf, z_buf, x_buf, first_buf, second_buf,
    w1_rep, w1_flat, w1_full, w2_full, w3_full, b1_full, b2_full, score_buf, peaks_buf,
    small_sem, q_sem, own_sem, send_o, recv_o, send_x, recv_x, send_s, recv_s, send_h, recv_h,
    send_p, recv_p, far_sem,
):
    regions, shard, depth = r_hbm.shape
    frames = q_hbm.shape[0] // regions
    chunks = shard // GROUP
    width = GROUP * 2 * chips
    tiles = frames // 4
    order = chunk_order(chunks)
    last = order[-1]
    me = lax.axis_index("qry")
    chip = me // 2
    core = me % 2
    sibling = chip * 2 + (1 - core)
    right = ((chip + 1) % chips) * 2 + core
    senders = 2 * chips
    col = lax.axis_index("ref")
    peers = senders * others
    mine = me * others + col

    smalls = [
        pltpu.make_async_copy(source, target, small_sem.at[k])
        for k, (source, target) in enumerate(
            (
                (w1_hbm, w1_ref), (b1_hbm, b1_ref), (w2_hbm, w2_ref), (b2_hbm, b2_ref),
                (w3_hbm, w3_ref), (b3_hbm, b3_ref), (w4_hbm, w4_ref), (pair_hbm, pair_ref),
                (lengths_hbm, lengths_ref), (len_hbm, len_ref), (b4_hbm, b4_ref),
            )
        )
    ]

    def piece(p):
        return pl.ds(cuts[p], cuts[p + 1] - cuts[p])

    pieces = len(cuts) - 1

    def rows_of(g):
        return pl.ds(pl.multiple_of(g * GROUP, GROUP), GROUP)

    def own_copy(g):
        return pltpu.make_async_copy(r_hbm.at[:, rows_of(g)], r_own.at[0, g], own_sem.at[g])

    def own_to_sibling(g):
        return pltpu.make_async_remote_copy(
            src_ref=r_hbm.at[:, rows_of(g)],
            dst_ref=r_own.at[1, g],
            send_sem=send_o.at[g],
            recv_sem=recv_o.at[g],
            device_id={"qry": sibling},
            device_id_type=MESH,
        )

    def q_copy(k):
        rows = pl.ds(k * frames, frames)
        return pltpu.make_async_copy(q_hbm.at[rows], q_buf.at[rows], q_sem.at[k])

    def to_right(step, g, p):
        if step == 0:
            source = r_hbm.at[:, rows_of(g), piece(p)]
        else:
            source = r_far.at[step - 1, g, 0, :, :, piece(p)]
        return pltpu.make_async_remote_copy(
            src_ref=source,
            dst_ref=r_far.at[step, g, 0, :, :, piece(p)],
            send_sem=send_x.at[step, g, p],
            recv_sem=recv_x.at[step, g, p],
            device_id={"qry": right},
            device_id_type=MESH,
        )

    def to_sibling(step, g, p):
        return pltpu.make_async_remote_copy(
            src_ref=r_far.at[step, g, 0, :, :, piece(p)],
            dst_ref=r_far.at[step, g, 1, :, :, piece(p)],
            send_sem=send_s.at[step, g, p],
            recv_sem=recv_s.at[step, g, p],
            device_id={"qry": sibling},
            device_id_type=MESH,
        )

    map_buf[...] = jnp.zeros_like(map_buf)
    barrier = pltpu.get_barrier_semaphore()
    for k in range(1, senders):
        device = {"qry": (me + k) % senders}
        pl.semaphore_signal(barrier, inc=1, device_id=device, device_id_type=MESH)

    def tell_columns(semaphore):
        for move, there in ((-1, col > 0), (1, col < others - 1)):

            @pl.when(there)
            def _():
                pl.semaphore_signal(
                    semaphore, inc=1, device_id={"ref": col + move}, device_id_type=MESH
                )

    columns_near = jnp.where(col > 0, 1, 0) + jnp.where(col < others - 1, 1, 0)
    tell_columns(barrier)
    pl.semaphore_wait(barrier, senders - 1 + columns_near)

    def enqueue(lo, hi):
        for k in range(lo, min(hi, chunks * pieces)):
            to_right(0, order[k // pieces], k % pieces).start()

    limits = [(chunks - 1) * pieces - 1] * chunks + [chunks * pieces - 2, chunks * pieces]
    limits = [max(limit, 0) for limit in limits[-chunks:]] if chunks > 1 else [pieces]
    enqueue(0, min(pieces, limits[0]))
    for k in range(regions):
        q_copy(k).start()
    for g in range(chunks):
        own_copy(g).start()
    for g in range(chunks):
        own_to_sibling(g).start()
    enqueue(min(pieces, limits[0]), limits[0])
    rounds = others - 1
    if rounds:
        tell_columns(far_sem.at[0])

    def next_round(k):
        if k < rounds:
            pl.semaphore_wait(far_sem.at[k], columns_near)
            if k + 1 < rounds:
                tell_columns(far_sem.at[k + 1])

    for copy in smalls:
        copy.start()
    z_buf[...] = jnp.zeros_like(z_buf)
    first_buf[...] = jnp.zeros_like(first_buf)
    second_buf[...] = jnp.zeros_like(second_buf)
    next_round(0)
    for copy in smalls:
        copy.wait()
    build_weights(
        w1_ref, w2_ref, w3_ref, b1_ref, b2_ref, w1_rep, w1_flat, w1_full, w2_full, w3_full,
        b1_full, b2_full,
    )
    next_round(1)
    factor = pair_ref[me, col].astype(jnp.float32) * scale

    def similar(product, blocks):
        best = jnp.max(product.reshape(blocks, regions, GROUP, regions * frames), axis=1)
        total = best[:, :, :frames]
        for k in range(1, regions):
            total = total + best[:, :, k * frames : (k + 1) * frames]
        return total * factor

    def near(side):
        product = lax.dot_general(
            r_own[side].reshape(chunks * regions * GROUP, depth), q_buf[...], NT,
            preferred_element_type=jnp.float32,
        )
        return similar(product, chunks).reshape(shard, frames)

    for k in range(regions):
        q_copy(k).wait()
    for g in range(chunks):
        own_copy(g).wait()

    def near_side(side, carry):
        @pl.when(side == 1)
        def _():
            for g in range(chunks):
                own_to_sibling(g).wait_recv()

        sims_buf[chip * 2 + side * (1 - core) + (1 - side) * core] = near(side)
        return carry

    lax.fori_loop(0, 2, near_side, 0)
    for k in range(2, rounds):
        next_round(k)

    def sources(step):
        origin = (chip + chips - 1 - step) % chips
        return origin * 2 + core, origin * 2 + (1 - core)

    def arrive(step, g, p):
        to_right(step, g, p).wait_recv()
        to_sibling(step, g, p).start()
        if step < chips - 2:
            to_right(step + 1, g, p).start()

    def part(step, g, first_piece, final_piece):
        columns = pl.ds(cuts[first_piece], cuts[final_piece] - cuts[first_piece])
        block = r_far[step, g, :, :, :, columns].reshape(2 * regions * GROUP, columns.size)
        return lax.dot_general(
            block, q_buf[:, columns], NT, preferred_element_type=jnp.float32
        )

    def keep(step, g, product):
        total = similar(product, 2)
        for k, source in enumerate(sources(step)):
            sims_buf[source, rows_of(g)] = total[k]

    def reachable(move_q, move_r):
        fits = (me + move_q >= 0) & (me + move_q < senders)
        return fits & (col + move_r >= 0) & (col + move_r < others)

    def halo_copy(k, move_q, move_r, g):
        if move_r == 0:
            source = target = pl.ds(HALO + g * width, width)
        elif move_r == 1:
            source, target = pl.ds(frames, HALO), pl.ds(0, HALO)
        else:
            source, target = pl.ds(HALO, HALO), pl.ds(HALO + frames, HALO)
        return pltpu.make_async_remote_copy(
            src_ref=map_buf.at[1, source],
            dst_ref=map_buf.at[1 - move_q, target],
            send_sem=send_h.at[k],
            recv_sem=recv_h.at[k],
            device_id={"qry": me + move_q, "ref": col + move_r},
            device_id_type=MESH,
        )

    moves = [(q, 0, g) for g in range(chunks) for q in (-1, 1)]
    moves += [(q, r, 0 if r < 0 else chunks - 1) for r in (-1, 1) for q in (-1, 1, 0)]
    moves = list(enumerate(moves))

    def spread(g):
        for b in range(senders):
            rows = pl.ds(HALO + g * width + b, GROUP, stride=senders)
            map_buf.at[1][rows, :] = sims_buf[b, g * GROUP : (g + 1) * GROUP]
        for k, (q, r, source) in moves:
            if source == g:

                @pl.when(reachable(q, r))
                def _():
                    halo_copy(k, q, r, g).start()

    def halos(stage):
        for k, (q, r, g) in moves:
            if g in stage:

                @pl.when(reachable(-q, -r))
                def _():
                    halo_copy(k, q, r, g).wait_recv()

    where = (me * tiles, col * tiles, senders * tiles, others * tiles)
    stages = (order[: max(chunks - 2, 0)], order[max(chunks - 2, 0) : chunks - 1], [last])
    work = plan(stages, chunks, frames, tiles)

    def network(k):
        halos(stages[k])
        for lo, hi in work[k][0]:
            conv1(lo, hi, where, map_buf, w1_full, b1_full, z_buf, x_buf, first_buf)
        for lo, hi in work[k][1]:
            conv2(lo, hi, where, w2_full, b2_full, first_buf, second_buf)
        for lo, hi in work[k][2]:
            score_buf[lo:hi, :PITCH] = conv3(lo, hi, w3_full, b3_ref, w4_ref, second_buf)

    for k, g in enumerate(order[:-1]):
        for step in range(chips - 1):
            for lo, hi in ((0, pieces - 2), (pieces - 2, pieces)):
                for p in range(lo, hi):
                    arrive(step, g, p)
                for p in range(lo, hi):
                    to_sibling(step, g, p).wait_recv()
                if lo == 0:
                    acc[...] = part(step, g, lo, hi)
                else:
                    keep(step, g, acc[...] + part(step, g, lo, hi))
        spread(g)
        enqueue(limits[k], limits[k + 1])
    network(0)

    def settle(step, lo, hi):
        for p in range(lo, hi):
            to_sibling(step, last, p).wait_recv()
        return part(step, last, lo, hi)

    for step in range(chips - 1):
        for p in range(pieces - 3):
            arrive(step, last, p)
        acc[...] = settle(step, 0, pieces - 3)
        arrive(step, last, pieces - 3)
        if step == 0:
            network(1)
        arrive(step, last, pieces - 2)
        arrive(step, last, pieces - 1)
        acc[...] += settle(step, pieces - 3, pieces - 1)
        keep(step, last, acc[...] + settle(step, pieces - 1, pieces))
    spread(last)
    network(2)

    scores = score_buf[...] + b4_ref[0]
    slot_f = lax.broadcasted_iota(jnp.int32, scores.shape, 0)
    column = slot_f + (col * tiles - 2)
    own = (slot_f >= 2) & (slot_f < 2 + tiles)
    begin = jnp.int32(0)
    for v in range(lengths_ref.shape[0]):
        end = begin + lengths_ref[v]
        member = own & (column >= begin) & (column < end)
        peaks_buf[mine, v : v + 1, :] = jnp.max(
            jnp.where(member, scores, -jnp.inf), axis=0, keepdims=True
        )
        begin = end

    flip = 2 * col // others

    def peak_copy(k):
        move = k % senders
        away = k // senders
        peer_q = (me + move) % senders
        peer_r = (1 - flip) * (others - 1 - away) + flip * away
        return peer_q, peer_r, pltpu.make_async_remote_copy(
            src_ref=peaks_buf.at[mine],
            dst_ref=peaks_buf.at[mine],
            send_sem=send_p.at[k],
            recv_sem=recv_p.at[mine],
            device_id={"qry": peer_q, "ref": peer_r},
            device_id_type=MESH,
        )

    def peak_wait(k, carry):
        peer = (mine + k) % peers
        pltpu.make_async_remote_copy(
            src_ref=peaks_buf.at[peer],
            dst_ref=peaks_buf.at[peer],
            send_sem=send_p.at[k],
            recv_sem=recv_p.at[peer],
            device_id={"qry": peer // others, "ref": peer % others},
            device_id_type=MESH,
        ).wait_recv()
        return carry

    def peak_start(k, carry):
        peer_q, peer_r, copy = peak_copy(k)

        @pl.when((peer_q != me) | (peer_r != col))
        def _():
            copy.start()

        return carry

    lax.fori_loop(0, peers, peak_start, 0)
    scores_ref[...] = jnp.transpose(scores)[2 : 2 + tiles, 2 : 2 + tiles]

    def drain(g, carry):
        own_to_sibling(g).wait_send()
        for step in range(chips - 1):
            for p in range(pieces):
                to_right(step, g, p).wait_send()
                to_sibling(step, g, p).wait_send()
        return carry

    lax.fori_loop(0, chunks, drain, 0)
    for k, (q, r, g) in moves:

        @pl.when(reachable(q, r))
        def _():
            halo_copy(k, q, r, g).wait_send()

    lax.fori_loop(1, peers, peak_wait, 0)
    lane = lax.broadcasted_iota(jnp.int32, peaks_buf.shape[1:], 1)
    total = jnp.zeros(peaks_buf.shape[1:], jnp.float32)
    for s in range(senders):
        best = jnp.max(peaks_buf[s * others : (s + 1) * others], axis=0)
        counted = (lane >= 2) & (lane < 2 + tiles) & (lane + (s * tiles - 2) < len_ref[0])
        total = total + jnp.where(counted, best, 0.0)
    total = jnp.sum(total, axis=1, keepdims=True) / len_ref[0].astype(jnp.float32)
    for v in range(lengths_ref.shape[0]):
        totals_ref[v] = jnp.sum(total[v : v + 1])

    def peak_drain(k, carry):
        peer_q, peer_r, copy = peak_copy(k)

        @pl.when((peer_q != me) | (peer_r != col))
        def _():
            copy.wait_send()

        return carry

    lax.fori_loop(0, peers, peak_drain, 0)


def build_weights(
    w1_ref, w2_ref, w3_ref, b1_ref, b2_ref, w1_rep, w1_flat, w1_full, w2_full, w3_full,
    b1_full, b2_full,
):
    for k in range(4):
        lanes = slice(k * 32, (k + 1) * 32)
        b1_full[:, lanes] = b1_ref[...]
        for di in range(3):
            w1_rep[3 * di : 3 * di + 3, lanes] = w1_ref[di]
    for k in range(2):
        b2_full[:, k * 64 : (k + 1) * 64] = b2_ref[...]
    w1_flat[...] = jnp.zeros_like(w1_flat)
    for u in range(2):
        for v in range(2):
            for a in range(2):
                for b in range(2):
                    at = (a * 2 + b) * 32
                    col = (u * 2 + v) * 128 + at
                    for k in range(9):
                        row = (2 * a + u + k // 3) * 8 + 2 * b + v + k % 3
                        w1_flat[row : row + 1, col : col + 32] = w1_rep[k : k + 1, at : at + 32]
    flat = w1_flat[...]
    high = flat.astype(jnp.bfloat16)
    w1_full[0:48] = high
    w1_full[48:96] = high
    w1_full[96:144] = (flat - high.astype(jnp.float32)).astype(jnp.bfloat16)

    w2_full[...] = jnp.zeros_like(w2_full)
    taps = {(0, 0): 0, (0, 1): 1, (1, 0): 2, (1, 1): -1}
    for g in range(2):
        for h in range(2):
            for a in range(2):
                for b in range(2):
                    row = ((g * 2 + h) * 4 + a * 2 + b) * 32
                    for u in range(2):
                        for v in range(2):
                            di = taps[g, a] - u + 1
                            dj = taps[h, b] - v + 1
                            if 0 <= di < 3 and 0 <= dj < 3:
                                col = u * 128 + v * 64
                                w2_full[row : row + 32, col : col + 64] = w2_ref[di * 3 + dj]
    for k in range(9):
        w3_full[k * 64 : (k + 1) * 64, :] = w3_ref[k]
    w3_full[576:640, :] = jnp.zeros((64, 128), jnp.bfloat16)


def inside_map(lo, hi, where):
    shape = (hi - lo, PITCH, 128)
    at_f = lax.broadcasted_iota(jnp.int32, shape, 0) + (where[1] - 2 + lo)
    at_p = lax.broadcasted_iota(jnp.int32, shape, 1) + (where[0] - 2)
    inside = (at_f >= 0) & (at_f < where[3]) & (at_p >= 0) & (at_p < where[2])
    return jnp.where(inside, 1.0, 0.0).reshape((hi - lo) * PITCH, 128)


def conv1(lo, hi, where, map_ref, w1_full, b1_full, z_buf, x_buf, first_buf):
    wide, frames = map_ref.shape[1:]
    top = max(0, (4 * lo - 1) // 8 * 8)
    end = min(wide, -(-(4 * hi + 3) // 8) * 8)
    source = lax.broadcasted_iota(jnp.int32, (3 * frames, 128), 0)
    target = lax.broadcasted_iota(jnp.int32, (3 * frames, 128), 1)
    whole = jnp.concatenate([map_ref[k, top:end] for k in range(3)], axis=1)
    high = whole.astype(jnp.bfloat16)
    lower = (whole - high.astype(jnp.float32)).astype(jnp.bfloat16)
    for rr in range(6):
        pick = jnp.where(source == 4 * target + (frames - 9) + rr, 1.0, 0.0).astype(jnp.bfloat16)
        for part, value in enumerate((high, lower)):
            z_buf[part, 8 + top : 8 + end, rr * 128 : (rr + 1) * 128] = jnp.dot(
                value, pick, preferred_element_type=jnp.float32
            )
    for block in range(lo, hi):
        pieces = []
        for part in (0, 1, 0):
            for rr in range(6):
                pieces.append(
                    z_buf[part, 4 * block + 7 : 4 * block + 15, rr * 128 : (rr + 1) * 128]
                )
        flat = jnp.concatenate(pieces, axis=0)
        x_buf[block * PITCH : (block + 1) * PITCH, :] = jnp.transpose(flat)[:PITCH]

    made = jnp.dot(
        x_buf[lo * PITCH : hi * PITCH].astype(jnp.bfloat16), w1_full[...],
        preferred_element_type=jnp.float32,
    )
    best = jnp.maximum(
        jnp.maximum(made[:, 0:128], made[:, 128:256]),
        jnp.maximum(made[:, 256:384], made[:, 384:512]),
    )
    first = jnp.maximum(best + b1_full[...], 0.0)
    first = jnp.where(inside_map(lo, hi, where) > 0.5, first, 0.0)
    first = first.astype(jnp.bfloat16).astype(jnp.float32)
    first_buf[LEAD + lo * PITCH : LEAD + hi * PITCH, :] = first


def conv2(lo, hi, where, w2_full, b2_full, first_buf, second_buf):
    lane = lax.broadcasted_iota(jnp.int32, (1, 128), 1)
    low_a = lane < 64
    low_b = (lane % 64) < 32
    rows = (hi - lo) * PITCH
    here = LEAD + lo * PITCH
    start = here - PITCH
    more = rows + 2 * PITCH
    first = first_buf[here : here + rows, :]
    shifted = jnp.where(
        low_a, first_buf[start + 1 : start + 1 + more, :], first_buf[start - 1 : start - 1 + more, :]
    )
    across = jnp.where(
        low_b, first_buf[here + PITCH : here + PITCH + rows, :], first_buf[start : start + rows, :]
    )
    both = jnp.where(low_b, shifted[2 * PITCH :], shifted[:rows])
    stacked = jnp.concatenate(
        [first, across, shifted[PITCH : PITCH + rows], both], axis=1
    ).astype(jnp.bfloat16)
    made = jnp.dot(stacked, w2_full[...], preferred_element_type=jnp.float32)
    best = jnp.maximum(made[:, 0:128], made[:, 128:256])
    best = jnp.maximum(best, pltpu.roll(best, 64, 1))
    second = jnp.maximum(best + b2_full[...], 0.0)
    second = jnp.where(inside_map(lo, hi, where) > 0.5, second, 0.0)
    second_buf[here : here + rows, :] = second.astype(jnp.bfloat16).astype(jnp.float32)


def conv3(lo, hi, w3_full, b3_ref, w4_ref, second_buf):
    lane = lax.broadcasted_iota(jnp.int32, (1, 128), 1)
    low_a = lane < 64
    rows = (hi - lo) * PITCH

    def moved(k):
        di, dj = k // 3, k % 3
        begin = LEAD + (lo + dj - 1) * PITCH + di - 1
        return second_buf[begin : begin + rows, :]

    groups = []
    for k in range(0, 9, 2):
        groups.append(jnp.where(low_a, moved(k), moved(k + 1)) if k < 8 else moved(k))
    stacked = jnp.concatenate(groups, axis=1).astype(jnp.bfloat16)
    made = jnp.dot(stacked, w3_full[...], preferred_element_type=jnp.float32)
    third = jnp.maximum(made + b3_ref[...], 0.0).astype(jnp.bfloat16).astype(jnp.float32)
    weighted = third * w4_ref[...].astype(jnp.float32)
    return jnp.sum(weighted.reshape(hi - lo, PITCH, 128), axis=2)


def body(
    query_feats, ref_feats, pair_table, lengths, query_len, conv1_weight, conv1_bias,
    conv2_weight, conv2_bias, conv3_weight, conv3_bias, conv4_weight, conv4_bias,
):
    senders = lax.axis_size("qry")
    others = lax.axis_size("ref")
    frames, regions, depth = query_feats.shape
    query_mat = jnp.transpose(query_feats, (1, 0, 2)).reshape(regions * frames, depth)
    ref_mat = jnp.transpose(ref_feats, (1, 2, 0, 3)).reshape(regions, -1, depth)
    videos = lengths.shape[0]
    shard = ref_mat.shape[1]
    chunks = shard // GROUP
    chips = senders // 2
    steps = max(1, chips - 1)
    cuts = [depth * k // 6 // 128 * 128 for k in range(7)]
    pieces = len(cuts) - 1
    tiles = frames // 4
    side = tiles + 4
    rows = side * PITCH
    scale = 1.0 / (regions * math.sqrt(depth))
    vmem = pl.BlockSpec(memory_space=pltpu.VMEM)
    smem = pl.BlockSpec(memory_space=pltpu.SMEM)
    hbm = pl.BlockSpec(memory_space=pltpu.HBM)
    dma = pltpu.SemaphoreType.DMA
    f32, bf16 = jnp.float32, jnp.bfloat16
    operands = (
        pair_table,
        lengths,
        query_len,
        conv4_bias,
        conv1_weight,
        conv1_bias[None],
        jnp.transpose(conv2_weight, (0, 1, 3, 2)).reshape(
            9, conv2_weight.shape[3], conv2_weight.shape[2]
        ),
        conv2_bias[None],
        jnp.transpose(conv3_weight, (0, 1, 3, 2)).reshape(
            9, conv3_weight.shape[3], conv3_weight.shape[2]
        ),
        conv3_bias[None],
        conv4_weight[None],
        query_mat,
        ref_mat,
    )
    kept = [
        (pltpu.SMEM if k < 4 else pltpu.VMEM)(operand.shape, operand.dtype)
        for k, operand in enumerate(operands[:11])
    ]
    scores, totals = pl.pallas_call(
        functools.partial(whole_kernel, chips, others, scale, cuts),
        out_shape=(
            pltpu.VMEM((tiles, tiles), f32),
            pltpu.SMEM((videos,), f32),
        ),
        in_specs=[hbm] * len(operands),
        out_specs=(vmem, smem),
        scratch_shapes=kept + [
            pltpu.VMEM(query_mat.shape, bf16),
            pltpu.VMEM((2, chunks, regions, GROUP, depth), bf16),
            pltpu.VMEM((steps, chunks, 2, regions, GROUP, depth), bf16),
            pltpu.VMEM((2 * regions * GROUP, regions * frames), f32),
            pltpu.VMEM((senders, shard, frames), f32),
            pltpu.VMEM((3, frames + 2 * HALO, frames), f32),
            pltpu.VMEM((2, frames + 4 * HALO, 768), f32),
            pltpu.VMEM((rows, 144), f32),
            pltpu.VMEM((rows + 2 * LEAD, 128), f32),
            pltpu.VMEM((rows + 2 * LEAD, 128), f32),
            pltpu.VMEM((16, 128), f32),
            pltpu.VMEM((48, 512), f32),
            pltpu.VMEM((144, 512), bf16),
            pltpu.VMEM((512, 256), bf16),
            pltpu.VMEM((640, 128), bf16),
            pltpu.VMEM((1, 128), f32),
            pltpu.VMEM((1, 128), f32),
            pltpu.VMEM((-(-side // 8) * 8, 128), f32),
            pltpu.VMEM((senders * others, videos, 128), f32),
            dma((11,)),
            dma((regions,)),
            dma((chunks,)),
            dma((chunks,)),
            dma((chunks,)),
            dma((steps, chunks, pieces)),
            dma((steps, chunks, pieces)),
            dma((steps, chunks, pieces)),
            dma((steps, chunks, pieces)),
            dma((2 * chunks + 6,)),
            dma((2 * chunks + 6,)),
            dma((senders * others,)),
            dma((senders * others,)),
            pltpu.SemaphoreType.REGULAR((max(1, others - 1),)),
        ],
        compiler_params=pltpu.CompilerParams(
            collective_id=0, has_side_effects=True, vmem_limit_bytes=56 << 20
        ),
        name="whole",
    )(*operands)
    return (scores, totals)


def solution(mesh):
    placed = (
        P(("groups", "qry"), None, None),
        P(("groups", "ref"), "qry", None, None),
        P("groups", None),
        P("groups"),
        P("groups"),
    ) + (P(),) * 8
    return jax.shard_map(
        body,
        mesh=mesh,
        in_specs=placed,
        out_specs=(P(("groups", "qry"), "ref"), P("groups")),
        check_vma=False,
    )
```

```python
import functools
import math

import jax
import jax.numpy as jnp
from jax import lax
from jax.experimental import pallas as pl
from jax.experimental.pallas import tpu as pltpu
from jax.sharding import PartitionSpec as P

MESH = pl.DeviceIdType.MESH
HALO = 8
PITCH = 40
LEAD = 48
GROUP = 8
NT = (((1,), (1,)), ((), ()))


def spans(flags):
    found = []
    for k, flag in enumerate(flags):
        if flag and (k == 0 or not flags[k - 1]):
            found.append([k, k + 1])
        elif flag:
            found[-1][1] = k + 1
    return [tuple(span) for span in found]


def plan(stages, chunks, frames, tiles):
    side = tiles + 4
    width = frames // chunks
    here, finished, work = set(), [[False] * side for _ in range(3)], []
    for stage in stages:
        here |= set(stage)
        ready = []
        for j in range(side):
            known = True
            for k in range(-1, 5):
                frame = 4 * (j - 2) + k
                outside = chunks - 1 if frame < 0 else 0
                known &= (frame // width if 0 <= frame < frames else outside) in here
            ready.append(known)
        layers = []
        for layer in range(3):
            if layer:
                edge = [False] * layer
                ready = [all(ready[j - 1 : j + 2]) for j in range(layer, side - layer)]
                ready = edge + ready + edge
            layers.append(spans([now and not was for now, was in zip(ready, finished[layer])]))
            finished[layer] = ready
        work.append(layers)
    return work


def chunk_order(chunks):
    return [k // 2 if k % 2 == 0 else chunks - 1 - k // 2 for k in range(chunks)]


def whole_kernel(
    chips, others, scale, cuts,
    pair_hbm, lengths_hbm, len_hbm, b4_hbm, w1_hbm, b1_hbm, w2_hbm, b2_hbm, w3_hbm, b3_hbm,
    w4_hbm, q_hbm, r_hbm,
    scores_ref, totals_ref,
    pair_ref, lengths_ref, len_ref, b4_ref, w1_ref, b1_ref, w2_ref, b2_ref, w3_ref, b3_ref, w4_ref,
    q_buf, r_own, r_far, acc, sims_buf, map_buf, z_buf, x_buf, first_buf, second_buf,
    w1_rep, w1_flat, w1_full, w2_full, w3_full, b1_full, b2_full, pick_full, score_buf, peaks_buf,
    small_sem, q_sem, own_sem, send_o, recv_o, send_x, recv_x, send_s, recv_s, send_h, recv_h,
    send_p, recv_p, far_sem,
):
    regions, shard, depth = r_hbm.shape
    frames = q_hbm.shape[0] // regions
    chunks = shard // GROUP
    width = GROUP * 2 * chips
    tiles = frames // 4
    order = chunk_order(chunks)
    last = order[-1]
    me = lax.axis_index("qry")
    chip = me // 2
    core = me % 2
    sibling = chip * 2 + (1 - core)
    right = ((chip + 1) % chips) * 2 + core
    senders = 2 * chips
    col = lax.axis_index("ref")
    peers = senders * others
    mine = me * others + col

    smalls = [
        pltpu.make_async_copy(source, target, small_sem.at[k])
        for k, (source, target) in enumerate(
            (
                (w1_hbm, w1_ref), (b1_hbm, b1_ref), (w2_hbm, w2_ref), (b2_hbm, b2_ref),
                (w3_hbm, w3_ref), (b3_hbm, b3_ref), (w4_hbm, w4_ref), (pair_hbm, pair_ref),
                (lengths_hbm, lengths_ref), (len_hbm, len_ref), (b4_hbm, b4_ref),
            )
        )
    ]

    def piece(p):
        return pl.ds(cuts[p], cuts[p + 1] - cuts[p])

    pieces = len(cuts) - 1

    def rows_of(g):
        return pl.ds(pl.multiple_of(g * GROUP, GROUP), GROUP)

    def batches(g):
        steps = (0, pieces - 3, pieces - 1, pieces) if g == last else (0, pieces - 2, pieces)
        return list(zip(steps[:-1], steps[1:]))

    def batch(g, p):
        return [lo <= p < hi for lo, hi in batches(g)].index(True)

    def all_of(ref, device, send_sem, recv_sem):
        return pltpu.make_async_remote_copy(
            src_ref=ref, dst_ref=ref, send_sem=send_sem, recv_sem=recv_sem,
            device_id=device, device_id_type=MESH,
        )

    def own_copy(g):
        return pltpu.make_async_copy(r_hbm.at[:, rows_of(g)], r_own.at[0, g], own_sem)

    def own_to_sibling(g):
        return pltpu.make_async_remote_copy(
            src_ref=r_hbm.at[:, rows_of(g)],
            dst_ref=r_own.at[1, g],
            send_sem=send_o,
            recv_sem=recv_o,
            device_id={"qry": sibling},
            device_id_type=MESH,
        )

    def q_copy(k):
        rows = pl.ds(k * frames, frames)
        return pltpu.make_async_copy(q_hbm.at[rows], q_buf.at[rows], q_sem)

    def to_right(step, g, p):
        if step == 0:
            source = r_hbm.at[:, rows_of(g), piece(p)]
        else:
            source = r_far.at[step - 1, g, 0, :, :, piece(p)]
        return pltpu.make_async_remote_copy(
            src_ref=source,
            dst_ref=r_far.at[step, g, 0, :, :, piece(p)],
            send_sem=send_x.at[step],
            recv_sem=recv_x.at[step, g, p],
            device_id={"qry": right},
            device_id_type=MESH,
        )

    def to_sibling(step, g, p):
        return pltpu.make_async_remote_copy(
            src_ref=r_far.at[step, g, 0, :, :, piece(p)],
            dst_ref=r_far.at[step, g, 1, :, :, piece(p)],
            send_sem=send_s.at[step],
            recv_sem=recv_s.at[step, g, batch(g, p)],
            device_id={"qry": sibling},
            device_id_type=MESH,
        )

    map_buf[...] = jnp.zeros_like(map_buf)
    barrier = pltpu.get_barrier_semaphore()
    for k in range(1, senders):
        device = {"qry": (me + k) % senders}
        pl.semaphore_signal(barrier, inc=1, device_id=device, device_id_type=MESH)

    def tell_columns(semaphore):
        for move, there in ((-1, col > 0), (1, col < others - 1)):

            @pl.when(there)
            def _():
                pl.semaphore_signal(
                    semaphore, inc=1, device_id={"ref": col + move}, device_id_type=MESH
                )

    columns_near = jnp.where(col > 0, 1, 0) + jnp.where(col < others - 1, 1, 0)
    tell_columns(barrier)
    pl.semaphore_wait(barrier, senders - 1 + columns_near)

    def enqueue(lo, hi):
        for k in range(lo, min(hi, chunks * pieces)):
            to_right(0, order[k // pieces], k % pieces).start()

    limits = [(chunks - 1) * pieces - 1] * chunks + [chunks * pieces - 2, chunks * pieces]
    limits = [max(limit, 0) for limit in limits[-chunks:]] if chunks > 1 else [pieces]
    enqueue(0, min(pieces, limits[0]))
    for k in range(regions):
        q_copy(k).start()
    for g in range(chunks):
        own_copy(g).start()
    for g in range(chunks):
        own_to_sibling(g).start()
    enqueue(min(pieces, limits[0]), limits[0])
    rounds = others - 1
    if rounds:
        tell_columns(far_sem.at[0])

    def next_round(k):
        if k < rounds:
            pl.semaphore_wait(far_sem.at[k], columns_near)
            if k + 1 < rounds:
                tell_columns(far_sem.at[k + 1])

    for copy in smalls:
        copy.start()
    z_buf[...] = jnp.zeros_like(z_buf)
    first_buf[...] = jnp.zeros_like(first_buf)
    second_buf[...] = jnp.zeros_like(second_buf)
    next_round(0)
    for copy in smalls:
        copy.wait()
    build_weights(
        w1_ref, w2_ref, w3_ref, b1_ref, b2_ref, w1_rep, w1_flat, w1_full, w2_full, w3_full,
        b1_full, b2_full, pick_full,
    )
    next_round(1)
    factor = pair_ref[me, col].astype(jnp.float32) * scale

    def similar(product, blocks):
        best = jnp.max(product.reshape(blocks, regions, GROUP, regions * frames), axis=1)
        total = best[:, :, :frames]
        for k in range(1, regions):
            total = total + best[:, :, k * frames : (k + 1) * frames]
        return total * factor

    def near(side):
        product = lax.dot_general(
            r_own[side].reshape(chunks * regions * GROUP, depth), q_buf[...], NT,
            preferred_element_type=jnp.float32,
        )
        return similar(product, chunks).reshape(shard, frames)

    pltpu.make_async_copy(q_hbm, q_buf, q_sem).wait()
    pltpu.make_async_copy(r_own.at[0], r_own.at[0], own_sem).wait()

    def near_side(side, carry):
        @pl.when(side == 1)
        def _():
            all_of(r_own.at[1], {"qry": sibling}, send_o, recv_o).wait_recv()

        sims_buf[chip * 2 + side * (1 - core) + (1 - side) * core] = near(side)
        return carry

    lax.fori_loop(0, 2, near_side, 0)
    for k in range(2, rounds):
        next_round(k)

    def sources(step):
        origin = (chip + chips - 1 - step) % chips
        return origin * 2 + core, origin * 2 + (1 - core)

    def arrive(step, g, p):
        to_right(step, g, p).wait_recv()
        to_sibling(step, g, p).start()
        if step < chips - 2:
            to_right(step + 1, g, p).start()

    def settle(step, g, lo, hi):
        columns = pl.ds(cuts[lo], cuts[hi] - cuts[lo])
        all_of(
            r_far.at[step, g, 1, :, :, columns], {"qry": sibling}, send_s.at[step],
            recv_s.at[step, g, batch(g, lo)],
        ).wait_recv()
        return part(step, g, lo, hi)

    def part(step, g, first_piece, final_piece):
        columns = pl.ds(cuts[first_piece], cuts[final_piece] - cuts[first_piece])
        block = r_far[step, g, :, :, :, columns].reshape(2 * regions * GROUP, columns.size)
        return lax.dot_general(
            block, q_buf[:, columns], NT, preferred_element_type=jnp.float32
        )

    def keep(step, g, product):
        total = similar(product, 2)
        for k, source in enumerate(sources(step)):
            sims_buf[source, rows_of(g)] = total[k]

    def reachable(move_q, move_r):
        fits = (me + move_q >= 0) & (me + move_q < senders)
        return fits & (col + move_r >= 0) & (col + move_r < others)

    def halo_copy(k, move_q, move_r, g):
        if move_r == 0:
            source = target = pl.ds(HALO + g * width, width)
        elif move_r == 1:
            source, target = pl.ds(frames, HALO), pl.ds(0, HALO)
        else:
            source, target = pl.ds(HALO, HALO), pl.ds(HALO + frames, HALO)
        return pltpu.make_async_remote_copy(
            src_ref=map_buf.at[1, source],
            dst_ref=map_buf.at[1 - move_q, target],
            send_sem=send_h.at[k],
            recv_sem=recv_h.at[k],
            device_id={"qry": me + move_q, "ref": col + move_r},
            device_id_type=MESH,
        )

    moves = [(q, 0, g) for g in range(chunks) for q in (-1, 1)]
    moves += [(q, r, 0 if r < 0 else chunks - 1) for r in (-1, 1) for q in (-1, 1, 0)]
    moves = list(enumerate(moves))

    def spread(g):
        for b in range(senders):
            rows = pl.ds(HALO + g * width + b, GROUP, stride=senders)
            map_buf.at[1][rows, :] = sims_buf[b, g * GROUP : (g + 1) * GROUP]
        for k, (q, r, source) in moves:
            if source == g:

                @pl.when(reachable(q, r))
                def _():
                    halo_copy(k, q, r, g).start()

    def halos(stage):
        for k, (q, r, g) in moves:
            if g in stage:

                @pl.when(reachable(-q, -r))
                def _():
                    halo_copy(k, q, r, g).wait_recv()

    where = (me * tiles, col * tiles, senders * tiles, others * tiles)
    stages = (order[: max(chunks - 2, 0)], order[max(chunks - 2, 0) : chunks - 1], [last])
    work = plan(stages, chunks, frames, tiles)

    def network(k):
        halos(stages[k])
        for lo, hi in work[k][0]:
            conv1(lo, hi, where, map_buf, pick_full, w1_full, b1_full, z_buf, x_buf, first_buf)
        for lo, hi in work[k][1]:
            conv2(lo, hi, where, w2_full, b2_full, first_buf, second_buf)
        for lo, hi in work[k][2]:
            score_buf[lo:hi, :PITCH] = conv3(lo, hi, w3_full, b3_ref, w4_ref, second_buf)

    for k, g in enumerate(order[:-1]):
        for step in range(chips - 1):
            for lo, hi in batches(g):
                for p in range(lo, hi):
                    arrive(step, g, p)
                if lo == 0:
                    acc[...] = settle(step, g, lo, hi)
                else:
                    keep(step, g, acc[...] + settle(step, g, lo, hi))
        spread(g)
        enqueue(limits[k], limits[k + 1])
    network(0)

    for step in range(chips - 1):
        for p in range(pieces - 3):
            arrive(step, last, p)
        acc[...] = settle(step, last, 0, pieces - 3)
        arrive(step, last, pieces - 3)
        if step == 0:
            network(1)
        arrive(step, last, pieces - 2)
        arrive(step, last, pieces - 1)
        acc[...] += settle(step, last, pieces - 3, pieces - 1)
        keep(step, last, acc[...] + settle(step, last, pieces - 1, pieces))
    spread(last)
    network(2)

    scores = score_buf[...] + b4_ref[0]
    slot_f = lax.broadcasted_iota(jnp.int32, scores.shape, 0)
    column = slot_f + (col * tiles - 2)
    own = (slot_f >= 2) & (slot_f < 2 + tiles)
    begin = jnp.int32(0)
    for v in range(lengths_ref.shape[0]):
        end = begin + lengths_ref[v]
        member = own & (column >= begin) & (column < end)
        peaks_buf[mine, v : v + 1, :] = jnp.max(
            jnp.where(member, scores, -jnp.inf), axis=0, keepdims=True
        )
        begin = end

    flip = 2 * col // others

    def peak_copy(k):
        move = k % senders
        away = k // senders
        peer_q = (me + move) % senders
        peer_r = (1 - flip) * (others - 1 - away) + flip * away
        return peer_q, peer_r, pltpu.make_async_remote_copy(
            src_ref=peaks_buf.at[mine],
            dst_ref=peaks_buf.at[mine],
            send_sem=send_p,
            recv_sem=recv_p,
            device_id={"qry": peer_q, "ref": peer_r},
            device_id_type=MESH,
        )

    def peak_start(k, carry):
        peer_q, peer_r, copy = peak_copy(k)

        @pl.when((peer_q != me) | (peer_r != col))
        def _():
            copy.start()

        return carry

    lax.fori_loop(0, peers, peak_start, 0)
    scores_ref[...] = jnp.transpose(scores)[2 : 2 + tiles, 2 : 2 + tiles]

    all_of(r_own.at[1], {"qry": sibling}, send_o, recv_o).wait_send()
    for step in range(chips - 1):
        sent = r_far.at[step, :, 0]
        all_of(sent, {"qry": right}, send_x.at[step], send_x.at[step]).wait_send()
        all_of(sent, {"qry": sibling}, send_s.at[step], send_s.at[step]).wait_send()
    for k, (q, r, g) in moves:

        @pl.when(reachable(q, r))
        def _():
            halo_copy(k, q, r, g).wait_send()

    heard = all_of(
        peaks_buf.at[pl.ds(0, peers - 1)], {"qry": sibling}, send_p, recv_p
    )
    heard.wait_recv()
    lane = lax.broadcasted_iota(jnp.int32, peaks_buf.shape[1:], 1)
    total = jnp.zeros(peaks_buf.shape[1:], jnp.float32)
    for s in range(senders):
        best = jnp.max(peaks_buf[s * others : (s + 1) * others], axis=0)
        counted = (lane >= 2) & (lane < 2 + tiles) & (lane + (s * tiles - 2) < len_ref[0])
        total = total + jnp.where(counted, best, 0.0)
    total = jnp.sum(total, axis=1, keepdims=True) / len_ref[0].astype(jnp.float32)
    for v in range(lengths_ref.shape[0]):
        totals_ref[v] = jnp.sum(total[v : v + 1])

    heard.wait_send()


def build_weights(
    w1_ref, w2_ref, w3_ref, b1_ref, b2_ref, w1_rep, w1_flat, w1_full, w2_full, w3_full,
    b1_full, b2_full, pick_full,
):
    for k in range(4):
        lanes = slice(k * 32, (k + 1) * 32)
        b1_full[:, lanes] = b1_ref[...]
        for di in range(3):
            w1_rep[3 * di : 3 * di + 3, lanes] = w1_ref[di]
    for k in range(2):
        b2_full[:, k * 64 : (k + 1) * 64] = b2_ref[...]
    w1_flat[...] = jnp.zeros_like(w1_flat)
    for u in range(2):
        for v in range(2):
            for a in range(2):
                for b in range(2):
                    at = (a * 2 + b) * 32
                    col = (u * 2 + v) * 128 + at
                    for k in range(9):
                        rr = 2 * a + u + k // 3
                        for part in range(2):
                            row = rr % 2 * 48 + part * 24 + rr // 2 * 8 + 2 * b + v + k % 3
                            w1_flat[row : row + 1, col : col + 32] = w1_rep[
                                k : k + 1, at : at + 32
                            ]
    flat = w1_flat[...]
    high = flat.astype(jnp.bfloat16)
    row = lax.broadcasted_iota(jnp.int32, flat.shape, 0)
    w1_full[0:128] = high
    w1_full[128:256] = jnp.where(
        row % 48 < 24, flat - high.astype(jnp.float32), 0.0
    ).astype(jnp.bfloat16)
    frames = pick_full.shape[0] // 3
    source = lax.broadcasted_iota(jnp.int32, (3 * frames, 128), 0)
    target = lax.broadcasted_iota(jnp.int32, (3 * frames, 128), 1)
    begin = 4 * (target % 64) + target // 64 + (frames - 9)
    for k in range(3):
        pick_full[:, k * 128 : (k + 1) * 128] = jnp.where(
            source == begin + 2 * k, 1.0, 0.0
        ).astype(jnp.bfloat16)

    w2_full[...] = jnp.zeros_like(w2_full)
    taps = {(0, 0): 0, (0, 1): 1, (1, 0): 2, (1, 1): -1}
    for g in range(2):
        for h in range(2):
            for a in range(2):
                for b in range(2):
                    row = ((g * 2 + h) * 4 + a * 2 + b) * 32
                    for u in range(2):
                        for v in range(2):
                            di = taps[g, a] - u + 1
                            dj = taps[h, b] - v + 1
                            if 0 <= di < 3 and 0 <= dj < 3:
                                col = u * 128 + v * 64
                                w2_full[row : row + 32, col : col + 64] = w2_ref[di * 3 + dj]
    for k in range(9):
        w3_full[k * 64 : (k + 1) * 64, :] = w3_ref[k]
    w3_full[576:640, :] = jnp.zeros((64, 128), jnp.bfloat16)


def inside_map(lo, hi, where):
    shape = (hi - lo, PITCH, 128)
    at_f = lax.broadcasted_iota(jnp.int32, shape, 0) + (where[1] - 2 + lo)
    at_p = lax.broadcasted_iota(jnp.int32, shape, 1) + (where[0] - 2)
    inside = (at_f >= 0) & (at_f < where[3]) & (at_p >= 0) & (at_p < where[2])
    return jnp.where(inside, 1.0, 0.0).reshape((hi - lo) * PITCH, 128)


def conv1(lo, hi, where, map_ref, pick_full, w1_full, b1_full, z_buf, x_buf, first_buf):
    wide = map_ref.shape[1]
    top = max(0, (4 * lo - 1) // 8 * 8)
    end = min(wide, -(-(4 * hi + 3) // 8) * 8)
    whole = jnp.concatenate([map_ref[k, top:end] for k in range(3)], axis=1)
    high = whole.astype(jnp.bfloat16)
    lower = (whole - high.astype(jnp.float32)).astype(jnp.bfloat16)
    for part, value in enumerate((high, lower)):
        z_buf[part, 8 + top : 8 + end, :] = jnp.dot(
            value, pick_full[...], preferred_element_type=jnp.float32
        )
    blank = jnp.zeros((PITCH, 32), jnp.float32)
    for block in range(lo, hi):
        pieces = [
            z_buf[part, 4 * block + 7 : 4 * block + 15, k * 128 : (k + 1) * 128]
            for part in range(2)
            for k in range(3)
        ]
        turned = jnp.transpose(jnp.concatenate(pieces, axis=0))
        x_buf[block * PITCH : (block + 1) * PITCH, :] = jnp.concatenate(
            [turned[:PITCH], turned[64 : 64 + PITCH], blank], axis=1
        )

    x = x_buf[lo * PITCH : hi * PITCH].astype(jnp.bfloat16)
    made = jnp.dot(
        jnp.concatenate([x, x], axis=1), w1_full[...], preferred_element_type=jnp.float32
    )
    best = jnp.maximum(
        jnp.maximum(made[:, 0:128], made[:, 128:256]),
        jnp.maximum(made[:, 256:384], made[:, 384:512]),
    )
    first = jnp.maximum(best + b1_full[...], 0.0)
    first = jnp.where(inside_map(lo, hi, where) > 0.5, first, 0.0)
    first = first.astype(jnp.bfloat16).astype(jnp.float32)
    first_buf[LEAD + lo * PITCH : LEAD + hi * PITCH, :] = first


def conv2(lo, hi, where, w2_full, b2_full, first_buf, second_buf):
    lane = lax.broadcasted_iota(jnp.int32, (1, 128), 1)
    low_a = lane < 64
    low_b = (lane % 64) < 32
    rows = (hi - lo) * PITCH
    here = LEAD + lo * PITCH
    start = here - PITCH
    more = rows + 2 * PITCH
    first = first_buf[here : here + rows, :]
    shifted = jnp.where(
        low_a, first_buf[start + 1 : start + 1 + more, :], first_buf[start - 1 : start - 1 + more, :]
    )
    across = jnp.where(
        low_b, first_buf[here + PITCH : here + PITCH + rows, :], first_buf[start : start + rows, :]
    )
    both = jnp.where(low_b, shifted[2 * PITCH :], shifted[:rows])
    stacked = jnp.concatenate(
        [first, across, shifted[PITCH : PITCH + rows], both], axis=1
    ).astype(jnp.bfloat16)
    made = jnp.dot(stacked, w2_full[...], preferred_element_type=jnp.float32)
    best = jnp.maximum(made[:, 0:128], made[:, 128:256])
    best = jnp.maximum(best, pltpu.roll(best, 64, 1))
    second = jnp.maximum(best + b2_full[...], 0.0)
    second = jnp.where(inside_map(lo, hi, where) > 0.5, second, 0.0)
    second_buf[here : here + rows, :] = second.astype(jnp.bfloat16).astype(jnp.float32)


def conv3(lo, hi, w3_full, b3_ref, w4_ref, second_buf):
    lane = lax.broadcasted_iota(jnp.int32, (1, 128), 1)
    low_a = lane < 64
    rows = (hi - lo) * PITCH

    def moved(k):
        di, dj = k // 3, k % 3
        begin = LEAD + (lo + dj - 1) * PITCH + di - 1
        return second_buf[begin : begin + rows, :]

    groups = []
    for k in range(0, 9, 2):
        groups.append(jnp.where(low_a, moved(k), moved(k + 1)) if k < 8 else moved(k))
    stacked = jnp.concatenate(groups, axis=1).astype(jnp.bfloat16)
    made = jnp.dot(stacked, w3_full[...], preferred_element_type=jnp.float32)
    third = jnp.maximum(made + b3_ref[...], 0.0).astype(jnp.bfloat16).astype(jnp.float32)
    weighted = third * w4_ref[...].astype(jnp.float32)
    return jnp.sum(weighted.reshape(hi - lo, PITCH, 128), axis=2)


def body(
    query_feats, ref_feats, pair_table, lengths, query_len, conv1_weight, conv1_bias,
    conv2_weight, conv2_bias, conv3_weight, conv3_bias, conv4_weight, conv4_bias,
):
    senders = lax.axis_size("qry")
    others = lax.axis_size("ref")
    frames, regions, depth = query_feats.shape
    query_mat = jnp.transpose(query_feats, (1, 0, 2)).reshape(regions * frames, depth)
    ref_mat = jnp.transpose(ref_feats, (1, 2, 0, 3)).reshape(regions, -1, depth)
    videos = lengths.shape[0]
    shard = ref_mat.shape[1]
    chunks = shard // GROUP
    chips = senders // 2
    steps = max(1, chips - 1)
    cuts = [depth * k // 6 // 128 * 128 for k in range(7)]
    pieces = len(cuts) - 1
    tiles = frames // 4
    side = tiles + 4
    rows = side * PITCH
    scale = 1.0 / (regions * math.sqrt(depth))
    vmem = pl.BlockSpec(memory_space=pltpu.VMEM)
    smem = pl.BlockSpec(memory_space=pltpu.SMEM)
    hbm = pl.BlockSpec(memory_space=pltpu.HBM)
    dma = pltpu.SemaphoreType.DMA
    f32, bf16 = jnp.float32, jnp.bfloat16
    operands = (
        pair_table,
        lengths,
        query_len,
        conv4_bias,
        conv1_weight,
        conv1_bias[None],
        jnp.transpose(conv2_weight, (0, 1, 3, 2)).reshape(
            9, conv2_weight.shape[3], conv2_weight.shape[2]
        ),
        conv2_bias[None],
        jnp.transpose(conv3_weight, (0, 1, 3, 2)).reshape(
            9, conv3_weight.shape[3], conv3_weight.shape[2]
        ),
        conv3_bias[None],
        conv4_weight[None],
        query_mat,
        ref_mat,
    )
    kept = [
        (pltpu.SMEM if k < 4 else pltpu.VMEM)(operand.shape, operand.dtype)
        for k, operand in enumerate(operands[:11])
    ]
    scores, totals = pl.pallas_call(
        functools.partial(whole_kernel, chips, others, scale, cuts),
        out_shape=(
            pltpu.VMEM((tiles, tiles), f32),
            pltpu.SMEM((videos,), f32),
        ),
        in_specs=[hbm] * len(operands),
        out_specs=(vmem, smem),
        scratch_shapes=kept + [
            pltpu.VMEM(query_mat.shape, bf16),
            pltpu.VMEM((2, chunks, regions, GROUP, depth), bf16),
            pltpu.VMEM((steps, chunks, 2, regions, GROUP, depth), bf16),
            pltpu.VMEM((2 * regions * GROUP, regions * frames), f32),
            pltpu.VMEM((senders, shard, frames), f32),
            pltpu.VMEM((3, frames + 2 * HALO, frames), f32),
            pltpu.VMEM((2, frames + 4 * HALO, 384), f32),
            pltpu.VMEM((rows, 128), f32),
            pltpu.VMEM((rows + 2 * LEAD, 128), f32),
            pltpu.VMEM((rows + 2 * LEAD, 128), f32),
            pltpu.VMEM((16, 128), f32),
            pltpu.VMEM((128, 512), f32),
            pltpu.VMEM((256, 512), bf16),
            pltpu.VMEM((512, 256), bf16),
            pltpu.VMEM((640, 128), bf16),
            pltpu.VMEM((1, 128), f32),
            pltpu.VMEM((1, 128), f32),
            pltpu.VMEM((3 * frames, 384), bf16),
            pltpu.VMEM((-(-side // 8) * 8, 128), f32),
            pltpu.VMEM((senders * others, videos, 128), f32),
            dma((11,)),
            dma(()),
            dma(()),
            dma(()),
            dma(()),
            dma((steps,)),
            dma((steps, chunks, pieces)),
            dma((steps,)),
            dma((steps, chunks, 3)),
            dma((2 * chunks + 6,)),
            dma((2 * chunks + 6,)),
            dma(()),
            dma(()),
            pltpu.SemaphoreType.REGULAR((max(1, others - 1),)),
        ],
        compiler_params=pltpu.CompilerParams(
            collective_id=0, has_side_effects=True, vmem_limit_bytes=56 << 20
        ),
        name="whole",
    )(*operands)
    return (scores, totals)


def solution(mesh):
    placed = (
        P(("groups", "qry"), None, None),
        P(("groups", "ref"), "qry", None, None),
        P("groups", None),
        P("groups"),
        P("groups"),
    ) + (P(),) * 8
    return jax.shard_map(
        body,
        mesh=mesh,
        in_specs=placed,
        out_specs=(P(("groups", "qry"), "ref"), P("groups")),
        check_vma=False,
    )
```

```python
import functools
import math

import jax
import jax.numpy as jnp
from jax import lax
from jax.experimental import pallas as pl
from jax.experimental.pallas import tpu as pltpu
from jax.sharding import PartitionSpec as P

MESH = pl.DeviceIdType.MESH
HALO = 8
PITCH = 40
LEAD = 48
OFF = 4
EDGES = ((0, 8), (32, 40))
ALL = ((0, 40),)
INNER = ((8, 32),)
GROUP = 8
NT = (((1,), (1,)), ((), ()))


def spans(flags):
    found = []
    for k, flag in enumerate(flags):
        if flag and (k == 0 or not flags[k - 1]):
            found.append([k, k + 1])
        elif flag:
            found[-1][1] = k + 1
    return [tuple(span) for span in found]


def plan(stages, chunks, frames, tiles):
    side = tiles + 4
    width = frames // chunks
    here, finished, work = set(), [[False] * side for _ in range(3)], []
    for stage in stages:
        here |= set(stage)
        ready = []
        for j in range(side):
            known = True
            for k in range(-1, 5):
                frame = 4 * (j - 2) + k
                outside = chunks - 1 if frame < 0 else 0
                known &= (frame // width if 0 <= frame < frames else outside) in here
            ready.append(known)
        layers = []
        for layer in range(3):
            if layer:
                edge = [False] * layer
                ready = [all(ready[j - 1 : j + 2]) for j in range(layer, side - layer)]
                ready = edge + ready + edge
            layers.append(spans([now and not was for now, was in zip(ready, finished[layer])]))
            finished[layer] = ready
        work.append(layers)
    return work


def chunk_order(chunks):
    return [k // 2 if k % 2 == 0 else chunks - 1 - k // 2 for k in range(chunks)]


def whole_kernel(
    chips, others, scale, cuts,
    pair_hbm, lengths_hbm, len_ref, b4_ref, w1_hbm, b1_hbm, w2_hbm, b2_hbm, w3_hbm, b3_hbm,
    w4_hbm, q_hbm, r_hbm,
    scores_ref, totals_ref,
    pair_ref, lengths_ref, w1_ref, b1_ref, w2_ref, b2_ref, w3_ref, b3_ref, w4_ref,
    q_buf, r_own, r_far, acc, sims_buf, map_buf, z_buf, x_buf, first_buf, second_buf,
    w1_rep, w1_flat, w1_full, w2_full, w3_full, b1_full, b2_full, pick_full, pick_edge, score_buf, peaks_buf,
    small_sem, q_sem, own_sem, send_o, recv_o, send_x, recv_x, send_s, recv_s, send_h, recv_h,
    send_p, recv_p, far_sem,
):
    regions, shard, depth = r_hbm.shape
    frames = q_hbm.shape[0] // regions
    chunks = shard // GROUP
    width = GROUP * 2 * chips
    tiles = frames // 4
    order = chunk_order(chunks)
    last = order[-1]
    me = lax.axis_index("qry")
    chip = me // 2
    core = me % 2
    sibling = chip * 2 + (1 - core)
    right = ((chip + 1) % chips) * 2 + core
    senders = 2 * chips
    col = lax.axis_index("ref")
    peers = senders * others
    mine = me * others + col

    smalls = [
        pltpu.make_async_copy(source, target, small_sem.at[k])
        for k, (source, target) in enumerate(
            (
                (w1_hbm, w1_ref), (b1_hbm, b1_ref), (w2_hbm, w2_ref), (b2_hbm, b2_ref),
                (w3_hbm, w3_ref), (b3_hbm, b3_ref), (w4_hbm, w4_ref), (pair_hbm, pair_ref),
                (lengths_hbm, lengths_ref),
            )
        )
    ]

    def piece(p):
        return pl.ds(cuts[p], cuts[p + 1] - cuts[p])

    pieces = len(cuts) - 1

    def rows_of(g):
        return pl.ds(pl.multiple_of(g * GROUP, GROUP), GROUP)

    def batches(g):
        steps = (0, pieces - 3, pieces - 1, pieces) if g == last else (0, pieces - 2, pieces)
        return list(zip(steps[:-1], steps[1:]))

    def batch(g, p):
        return [lo <= p < hi for lo, hi in batches(g)].index(True)

    def all_of(ref, device, send_sem, recv_sem):
        return pltpu.make_async_remote_copy(
            src_ref=ref, dst_ref=ref, send_sem=send_sem, recv_sem=recv_sem,
            device_id=device, device_id_type=MESH,
        )

    def own_copy(g):
        return pltpu.make_async_copy(r_hbm.at[:, rows_of(g)], r_own.at[0, g], own_sem)

    def own_to_sibling(g):
        return pltpu.make_async_remote_copy(
            src_ref=r_hbm.at[:, rows_of(g)],
            dst_ref=r_own.at[1, g],
            send_sem=send_o,
            recv_sem=recv_o,
            device_id={"qry": sibling},
            device_id_type=MESH,
        )

    def q_copy(k):
        rows = pl.ds(k * frames, frames)
        return pltpu.make_async_copy(q_hbm.at[rows], q_buf.at[rows], q_sem)

    def to_right(step, g, p):
        if step == 0:
            source = r_hbm.at[:, rows_of(g), piece(p)]
        else:
            source = r_far.at[step - 1, g, 0, :, :, piece(p)]
        return pltpu.make_async_remote_copy(
            src_ref=source,
            dst_ref=r_far.at[step, g, 0, :, :, piece(p)],
            send_sem=send_x.at[step],
            recv_sem=recv_x.at[step, g, p],
            device_id={"qry": right},
            device_id_type=MESH,
        )

    def to_sibling(step, g, p):
        return pltpu.make_async_remote_copy(
            src_ref=r_far.at[step, g, 0, :, :, piece(p)],
            dst_ref=r_far.at[step, g, 1, :, :, piece(p)],
            send_sem=send_s.at[step],
            recv_sem=recv_s.at[step, g, batch(g, p)],
            device_id={"qry": sibling},
            device_id_type=MESH,
        )

    map_buf[...] = jnp.zeros_like(map_buf)
    barrier = pltpu.get_barrier_semaphore()
    for k in range(1, senders):
        device = {"qry": (me + k) % senders}
        pl.semaphore_signal(barrier, inc=1, device_id=device, device_id_type=MESH)

    def tell_columns(semaphore):
        for move, there in ((-1, col > 0), (1, col < others - 1)):

            @pl.when(there)
            def _():
                pl.semaphore_signal(
                    semaphore, inc=1, device_id={"ref": col + move}, device_id_type=MESH
                )

    columns_near = jnp.where(col > 0, 1, 0) + jnp.where(col < others - 1, 1, 0)
    tell_columns(barrier)
    pl.semaphore_wait(barrier, senders - 1 + columns_near)

    def enqueue(lo, hi):
        for k in range(lo, min(hi, chunks * pieces)):
            to_right(0, order[k // pieces], k % pieces).start()

    limits = [(chunks - 1) * pieces - 1] * chunks + [chunks * pieces - 2, chunks * pieces]
    limits = [max(limit, 0) for limit in limits[-chunks:]] if chunks > 1 else [pieces]
    enqueue(0, min(pieces, limits[0]))
    for k in range(regions):
        q_copy(k).start()
    for g in range(chunks):
        own_copy(g).start()
    for g in range(chunks):
        own_to_sibling(g).start()
    enqueue(min(pieces, limits[0]), limits[0])
    rounds = others - 1
    if rounds:
        tell_columns(far_sem.at[0])

    def next_round(k):
        if k < rounds:
            pl.semaphore_wait(far_sem.at[k], columns_near)
            if k + 1 < rounds:
                tell_columns(far_sem.at[k + 1])

    for copy in smalls:
        copy.start()
    z_buf[...] = jnp.zeros_like(z_buf)
    first_buf[...] = jnp.zeros_like(first_buf)
    second_buf[...] = jnp.zeros_like(second_buf)
    next_round(0)
    for copy in smalls:
        copy.wait()
    build_weights(
        w1_ref, w2_ref, w3_ref, b1_ref, b2_ref, w1_rep, w1_flat, w1_full, w2_full, w3_full,
        b1_full, b2_full, pick_full, pick_edge,
    )
    next_round(1)
    factor = pair_ref[me, col].astype(jnp.float32) * scale

    def similar(product, blocks):
        best = jnp.max(product.reshape(blocks, regions, GROUP, regions * frames), axis=1)
        total = best[:, :, :frames]
        for k in range(1, regions):
            total = total + best[:, :, k * frames : (k + 1) * frames]
        return total * factor

    def near(side):
        product = lax.dot_general(
            r_own[side].reshape(chunks * regions * GROUP, depth), q_buf[...], NT,
            preferred_element_type=jnp.float32,
        )
        return similar(product, chunks).reshape(shard, frames)

    pltpu.make_async_copy(q_hbm, q_buf, q_sem).wait()
    pltpu.make_async_copy(r_own.at[0], r_own.at[0], own_sem).wait()

    def near_side(side, carry):
        @pl.when(side == 1)
        def _():
            all_of(r_own.at[1], {"qry": sibling}, send_o, recv_o).wait_recv()

        sims_buf[chip * 2 + side * (1 - core) + (1 - side) * core] = near(side)
        return carry

    lax.fori_loop(0, 2, near_side, 0)
    for k in range(2, rounds):
        next_round(k)

    def sources(step):
        origin = (chip + chips - 1 - step) % chips
        return origin * 2 + core, origin * 2 + (1 - core)

    def arrive(step, g, p):
        to_right(step, g, p).wait_recv()
        to_sibling(step, g, p).start()
        if step < chips - 2:
            to_right(step + 1, g, p).start()

    def settle(step, g, lo, hi):
        columns = pl.ds(cuts[lo], cuts[hi] - cuts[lo])
        all_of(
            r_far.at[step, g, 1, :, :, columns], {"qry": sibling}, send_s.at[step],
            recv_s.at[step, g, batch(g, lo)],
        ).wait_recv()
        return part(step, g, lo, hi)

    def part(step, g, first_piece, final_piece):
        columns = pl.ds(cuts[first_piece], cuts[final_piece] - cuts[first_piece])
        block = r_far[step, g, :, :, :, columns].reshape(2 * regions * GROUP, columns.size)
        return lax.dot_general(
            block, q_buf[:, columns], NT, preferred_element_type=jnp.float32
        )

    def keep(step, g, product):
        total = similar(product, 2)
        for k, source in enumerate(sources(step)):
            sims_buf[source, rows_of(g)] = total[k]

    def reachable(move_q, move_r):
        fits = (me + move_q >= 0) & (me + move_q < senders)
        return fits & (col + move_r >= 0) & (col + move_r < others)

    def halo_copy(k, move_q, move_r, g):
        if move_r == 0:
            source = target = pl.ds(HALO + g * width, width)
        elif move_r == 1:
            source, target = pl.ds(frames, HALO), pl.ds(0, HALO)
        else:
            source, target = pl.ds(HALO, HALO), pl.ds(HALO + frames, HALO)
        return pltpu.make_async_remote_copy(
            src_ref=map_buf.at[1, source],
            dst_ref=map_buf.at[1 - move_q, target],
            send_sem=send_h.at[k],
            recv_sem=recv_h.at[k],
            device_id={"qry": me + move_q, "ref": col + move_r},
            device_id_type=MESH,
        )

    moves = [(q, 0, g) for g in range(chunks) for q in (-1, 1)]
    moves += [(q, r, 0 if r < 0 else chunks - 1) for r in (-1, 1) for q in (-1, 1, 0)]
    moves = list(enumerate(moves))

    def spread(g):
        for b in range(senders):
            rows = pl.ds(HALO + g * width + b, GROUP, stride=senders)
            map_buf.at[1][rows, :] = sims_buf[b, g * GROUP : (g + 1) * GROUP]
        for k, (q, r, source) in moves:
            if source == g:

                @pl.when(reachable(q, r))
                def _():
                    halo_copy(k, q, r, g).start()

    def halos(stage):
        for k, (q, r, g) in moves:
            if g in stage:

                @pl.when(reachable(-q, -r))
                def _():
                    halo_copy(k, q, r, g).wait_recv()

    where = (me * tiles, col * tiles, senders * tiles, others * tiles)
    stages = (order[: max(chunks - 2, 0)], order[max(chunks - 2, 0) : chunks - 1], [last])
    work = plan(stages, chunks, frames, tiles)

    def convolve(k, parts, pick, groups, kept):
        for lo, hi in work[k][0]:
            conv1(
                lo, hi, groups, parts, where, map_buf, pick, w1_full, b1_full, z_buf, x_buf,
                first_buf,
            )
        for lo, hi in work[k][1]:
            conv2(lo, hi, groups, where, w2_full, b2_full, first_buf, second_buf)
        for lo, hi in work[k][2]:
            found = conv3(lo, hi, kept, w3_full, b3_ref, w4_ref, second_buf)
            at = 0
            for t, end in kept:
                score_buf[lo:hi, t:end] = found[:, at : at + end - t]
                at += end - t

    def network(k):
        halos(stages[k])
        convolve(k, (0, 1, 2), pick_full, ALL, ALL)

    for k, g in enumerate(order[:-1]):
        for step in range(chips - 1):
            for lo, hi in batches(g):
                for p in range(lo, hi):
                    arrive(step, g, p)
                if lo == 0:
                    acc[...] = settle(step, g, lo, hi)
                else:
                    keep(step, g, acc[...] + settle(step, g, lo, hi))
        spread(g)
        enqueue(limits[k], limits[k + 1])
    network(0)

    for step in range(chips - 1):
        for p in range(pieces - 3):
            arrive(step, last, p)
        acc[...] = settle(step, last, 0, pieces - 3)
        arrive(step, last, pieces - 3)
        if step == 0:
            network(1)
        arrive(step, last, pieces - 2)
        arrive(step, last, pieces - 1)
        acc[...] += settle(step, last, pieces - 3, pieces - 1)
        keep(step, last, acc[...] + settle(step, last, pieces - 1, pieces))
    spread(last)
    convolve(2, (1,), pick_full, ALL, INNER)
    halos(stages[2])
    convolve(2, (0, 1, 2), pick_edge, EDGES, EDGES)

    scores = score_buf[...] + b4_ref[0]
    slot_f = lax.broadcasted_iota(jnp.int32, scores.shape, 0)
    column = slot_f + (col * tiles - 2)
    own = (slot_f >= 2) & (slot_f < 2 + tiles)
    begin = jnp.int32(0)
    for v in range(lengths_ref.shape[0]):
        end = begin + lengths_ref[v]
        member = own & (column >= begin) & (column < end)
        peaks_buf[mine, v : v + 1, :] = jnp.max(
            jnp.where(member, scores, -jnp.inf), axis=0, keepdims=True
        )
        begin = end

    flip = 2 * col // others

    def peak_copy(k):
        move = k % senders
        away = k // senders
        peer_q = (me + move) % senders
        peer_r = (1 - flip) * (others - 1 - away) + flip * away
        return peer_q, peer_r, pltpu.make_async_remote_copy(
            src_ref=peaks_buf.at[mine],
            dst_ref=peaks_buf.at[mine],
            send_sem=send_p,
            recv_sem=recv_p,
            device_id={"qry": peer_q, "ref": peer_r},
            device_id_type=MESH,
        )

    def peak_start(k, carry):
        peer_q, peer_r, copy = peak_copy(k)

        @pl.when((peer_q != me) | (peer_r != col))
        def _():
            copy.start()

        return carry

    lax.fori_loop(0, peers, peak_start, 0)
    scores_ref[...] = jnp.transpose(scores)[OFF : OFF + tiles, 2 : 2 + tiles]

    all_of(r_own.at[1], {"qry": sibling}, send_o, recv_o).wait_send()
    for step in range(chips - 1):
        sent = r_far.at[step, :, 0]
        all_of(sent, {"qry": right}, send_x.at[step], send_x.at[step]).wait_send()
        all_of(sent, {"qry": sibling}, send_s.at[step], send_s.at[step]).wait_send()
    for k, (q, r, g) in moves:

        @pl.when(reachable(q, r))
        def _():
            halo_copy(k, q, r, g).wait_send()

    heard = all_of(
        peaks_buf.at[pl.ds(0, peers - 1)], {"qry": sibling}, send_p, recv_p
    )
    heard.wait_recv()
    lane = lax.broadcasted_iota(jnp.int32, peaks_buf.shape[1:], 1)
    total = jnp.zeros(peaks_buf.shape[1:], jnp.float32)
    for s in range(senders):
        best = jnp.max(peaks_buf[s * others : (s + 1) * others], axis=0)
        counted = (lane >= OFF) & (lane < OFF + tiles)
        counted = counted & (lane + (s * tiles - OFF) < len_ref[0])
        total = total + jnp.where(counted, best, 0.0)
    total = jnp.sum(total, axis=1, keepdims=True) / len_ref[0].astype(jnp.float32)
    for v in range(lengths_ref.shape[0]):
        totals_ref[v] = jnp.sum(total[v : v + 1])

    heard.wait_send()


def build_weights(
    w1_ref, w2_ref, w3_ref, b1_ref, b2_ref, w1_rep, w1_flat, w1_full, w2_full, w3_full,
    b1_full, b2_full, pick_full, pick_edge,
):
    for k in range(4):
        lanes = slice(k * 32, (k + 1) * 32)
        b1_full[:, lanes] = b1_ref[...]
        for di in range(3):
            w1_rep[3 * di : 3 * di + 3, lanes] = w1_ref[di]
    for k in range(2):
        b2_full[:, k * 64 : (k + 1) * 64] = b2_ref[...]
    w1_flat[...] = jnp.zeros_like(w1_flat)
    for u in range(2):
        for v in range(2):
            for a in range(2):
                for b in range(2):
                    at = (a * 2 + b) * 32
                    col = (u * 2 + v) * 128 + at
                    for k in range(9):
                        rr = 2 * a + u + k // 3
                        for part in range(2):
                            row = rr % 2 * 48 + part * 24 + rr // 2 * 8 + 2 * b + v + k % 3
                            w1_flat[row : row + 1, col : col + 32] = w1_rep[
                                k : k + 1, at : at + 32
                            ]
    flat = w1_flat[...]
    high = flat.astype(jnp.bfloat16)
    row = lax.broadcasted_iota(jnp.int32, flat.shape, 0)
    w1_full[0:128] = high
    w1_full[128:256] = jnp.where(
        row % 48 < 24, flat - high.astype(jnp.float32), 0.0
    ).astype(jnp.bfloat16)
    frames = pick_full.shape[0] // 3
    source = lax.broadcasted_iota(jnp.int32, (3 * frames, 128), 0)
    target = lax.broadcasted_iota(jnp.int32, (3 * frames, 128), 1)
    begin = 4 * (target % 64 - OFF) + target // 64 + (frames - 1)
    for k in range(3):
        pick_full[:, k * 128 : (k + 1) * 128] = jnp.where(
            source == begin + 2 * k, 1.0, 0.0
        ).astype(jnp.bfloat16)
    at = target % 16
    at = jnp.where(at < 8, at, at + 24)
    begin = 4 * (at - OFF) + target // 64 + (frames - 1)
    for k in range(3):
        pick_edge[:, k * 128 : (k + 1) * 128] = jnp.where(
            source == begin + 2 * k, 1.0, 0.0
        ).astype(jnp.bfloat16)

    w2_full[...] = jnp.zeros_like(w2_full)
    taps = {(0, 0): 0, (0, 1): 1, (1, 0): 2, (1, 1): -1}
    for g in range(2):
        for h in range(2):
            for a in range(2):
                for b in range(2):
                    row = ((g * 2 + h) * 4 + a * 2 + b) * 32
                    for u in range(2):
                        for v in range(2):
                            di = taps[g, a] - u + 1
                            dj = taps[h, b] - v + 1
                            if 0 <= di < 3 and 0 <= dj < 3:
                                col = u * 128 + v * 64
                                w2_full[row : row + 32, col : col + 64] = w2_ref[di * 3 + dj]
    for k in range(9):
        w3_full[k * 64 : (k + 1) * 64, :] = w3_ref[k]
    w3_full[576:640, :] = jnp.zeros((64, 128), jnp.bfloat16)


def span_of(groups):
    return sum(end - t for t, end in groups)


def inside_map(lo, hi, groups, where):
    shape = (hi - lo, span_of(groups), 128)
    at_f = lax.broadcasted_iota(jnp.int32, shape, 0) + (where[1] - 2 + lo)
    at_p = lax.broadcasted_iota(jnp.int32, shape, 1)
    if groups == EDGES:
        at_p = jnp.where(at_p < 8, at_p, at_p + 24)
    at_p = at_p + (where[0] - OFF)
    inside = (at_f >= 0) & (at_f < where[3]) & (at_p >= 0) & (at_p < where[2])
    return jnp.where(inside, 1.0, 0.0).reshape(shape[0] * shape[1], 128)


def rows_at(ref, lo, hi, shift, groups):
    if groups == ALL:
        return ref[LEAD + lo * PITCH + shift : LEAD + hi * PITCH + shift, :]
    found = []
    for block in range(lo, hi):
        base = LEAD + block * PITCH + shift
        found += [ref[base + t : base + end, :] for t, end in groups]
    return jnp.concatenate(found, axis=0)


def put_rows(ref, lo, hi, groups, value):
    if groups == ALL:
        ref[LEAD + lo * PITCH : LEAD + hi * PITCH, :] = value
        return
    at = 0
    for block in range(lo, hi):
        base = LEAD + block * PITCH
        for t, end in groups:
            ref[base + t : base + end, :] = value[at : at + end - t]
            at += end - t


def conv1(
    lo, hi, groups, parts, where, map_ref, pick_ref, w1_full, b1_full, z_buf, x_buf, first_buf
):
    wide, frames = map_ref.shape[1:]
    top = max(0, (4 * lo - 1) // 8 * 8)
    end = min(wide, -(-(4 * hi + 3) // 8) * 8)
    whole = [map_ref[k, top:end] for k in parts]
    whole = jnp.concatenate(whole, axis=1) if len(whole) > 1 else whole[0]
    high = whole.astype(jnp.bfloat16)
    lower = (whole - high.astype(jnp.float32)).astype(jnp.bfloat16)
    pick = pick_ref[parts[0] * frames : (parts[-1] + 1) * frames]
    for part, value in enumerate((high, lower)):
        z_buf[part, 8 + top : 8 + end, :] = jnp.dot(
            value, pick, preferred_element_type=jnp.float32
        )

    def window(block, part, k):
        return z_buf[part, 4 * block + 7 : 4 * block + 15, k * 128 : (k + 1) * 128]

    kinds = [(part, k) for part in range(2) for k in range(3)]
    if groups == ALL:
        blank = jnp.zeros((PITCH, 32), jnp.float32)
        for block in range(lo, hi):
            turned = jnp.transpose(
                jnp.concatenate([window(block, *kind) for kind in kinds], axis=0)
            )
            x_buf[block * PITCH : (block + 1) * PITCH, :] = jnp.concatenate(
                [turned[:PITCH], turned[64 : 64 + PITCH], blank], axis=1
            )
        x = x_buf[lo * PITCH : hi * PITCH]
    else:
        blank = jnp.zeros((64, 32), jnp.float32)
        place = lax.broadcasted_iota(jnp.int32, (8, 128), 1) % 64 // 16
        found = []
        for block in range(lo, hi, 4):
            pieces = []
            for kind in kinds:
                piece = window(block, *kind)
                for g in range(1, min(4, hi - block)):
                    piece = jnp.where(place == g, window(block + g, *kind), piece)
                pieces.append(piece)
            turned = jnp.transpose(jnp.concatenate(pieces, axis=0))
            found.append(jnp.concatenate([turned[:64], turned[64:], blank], axis=1))
        x = jnp.concatenate(found, axis=0)[: (hi - lo) * 16]
    x = x.astype(jnp.bfloat16)
    made = jnp.dot(
        jnp.concatenate([x, x], axis=1), w1_full[...], preferred_element_type=jnp.float32
    )
    best = jnp.maximum(
        jnp.maximum(made[:, 0:128], made[:, 128:256]),
        jnp.maximum(made[:, 256:384], made[:, 384:512]),
    )
    first = jnp.maximum(best + b1_full[...], 0.0)
    first = first * inside_map(lo, hi, groups, where)
    put_rows(first_buf, lo, hi, groups, first.astype(jnp.bfloat16).astype(jnp.float32))


def conv2(lo, hi, groups, where, w2_full, b2_full, first_buf, second_buf):
    lane = lax.broadcasted_iota(jnp.int32, (1, 128), 1)
    low_a = lane < 64
    low_b = (lane % 64) < 32
    one = span_of(groups)
    rows = (hi - lo) * one
    first = rows_at(first_buf, lo - 1, hi + 1, 0, groups)
    shifted = jnp.where(
        low_a,
        rows_at(first_buf, lo - 1, hi + 1, 1, groups),
        rows_at(first_buf, lo - 1, hi + 1, -1, groups),
    )
    across = jnp.where(low_b, first[2 * one :], first[:rows])
    both = jnp.where(low_b, shifted[2 * one :], shifted[:rows])
    stacked = jnp.concatenate(
        [first[one : one + rows], across, shifted[one : one + rows], both], axis=1
    ).astype(jnp.bfloat16)
    made = jnp.dot(stacked, w2_full[...], preferred_element_type=jnp.float32)
    best = jnp.maximum(made[:, 0:128], made[:, 128:256])
    best = jnp.maximum(best, pltpu.roll(best, 64, 1))
    second = jnp.maximum(best + b2_full[...], 0.0)
    second = second * inside_map(lo, hi, groups, where)
    put_rows(second_buf, lo, hi, groups, second.astype(jnp.bfloat16).astype(jnp.float32))


def conv3(lo, hi, groups, w3_full, b3_ref, w4_ref, second_buf):
    lane = lax.broadcasted_iota(jnp.int32, (1, 128), 1)
    low_a = lane < 64

    def moved(k):
        return rows_at(second_buf, lo + k % 3 - 1, hi + k % 3 - 1, k // 3 - 1, groups)

    taps = []
    for k in range(0, 9, 2):
        taps.append(jnp.where(low_a, moved(k), moved(k + 1)) if k < 8 else moved(k))
    stacked = jnp.concatenate(taps, axis=1).astype(jnp.bfloat16)
    made = jnp.dot(stacked, w3_full[...], preferred_element_type=jnp.float32)
    third = jnp.maximum(made + b3_ref[...], 0.0).astype(jnp.bfloat16).astype(jnp.float32)
    weighted = third * w4_ref[...].astype(jnp.float32)
    return jnp.sum(weighted.reshape(hi - lo, span_of(groups), 128), axis=2)


def body(
    query_feats, ref_feats, pair_table, lengths, query_len, conv1_weight, conv1_bias,
    conv2_weight, conv2_bias, conv3_weight, conv3_bias, conv4_weight, conv4_bias,
):
    senders = lax.axis_size("qry")
    others = lax.axis_size("ref")
    frames, regions, depth = query_feats.shape
    query_mat = jnp.transpose(query_feats, (1, 0, 2)).reshape(regions * frames, depth)
    ref_mat = jnp.transpose(ref_feats, (1, 2, 0, 3)).reshape(regions, -1, depth)
    videos = lengths.shape[0]
    shard = ref_mat.shape[1]
    chunks = shard // GROUP
    chips = senders // 2
    steps = max(1, chips - 1)
    cuts = [depth * k // 6 // 128 * 128 for k in range(7)]
    pieces = len(cuts) - 1
    tiles = frames // 4
    side = tiles + 4
    rows = side * PITCH
    scale = 1.0 / (regions * math.sqrt(depth))
    vmem = pl.BlockSpec(memory_space=pltpu.VMEM)
    smem = pl.BlockSpec(memory_space=pltpu.SMEM)
    hbm = pl.BlockSpec(memory_space=pltpu.HBM)
    dma = pltpu.SemaphoreType.DMA
    f32, bf16 = jnp.float32, jnp.bfloat16
    operands = (
        pair_table,
        lengths,
        query_len,
        conv4_bias,
        conv1_weight,
        conv1_bias[None],
        jnp.transpose(conv2_weight, (0, 1, 3, 2)).reshape(
            9, conv2_weight.shape[3], conv2_weight.shape[2]
        ),
        conv2_bias[None],
        jnp.transpose(conv3_weight, (0, 1, 3, 2)).reshape(
            9, conv3_weight.shape[3], conv3_weight.shape[2]
        ),
        conv3_bias[None],
        conv4_weight[None],
        query_mat,
        ref_mat,
    )
    kept = [
        (pltpu.SMEM if k < 4 else pltpu.VMEM)(operand.shape, operand.dtype)
        for k, operand in enumerate(operands[:11]) if k not in (2, 3)
    ]
    scores, totals = pl.pallas_call(
        functools.partial(whole_kernel, chips, others, scale, cuts),
        out_shape=(
            pltpu.VMEM((tiles, tiles), f32),
            pltpu.SMEM((videos,), f32),
        ),
        in_specs=[hbm] * 2 + [smem] * 2 + [hbm] * (len(operands) - 4),
        out_specs=(vmem, smem),
        scratch_shapes=kept + [
            pltpu.VMEM(query_mat.shape, bf16),
            pltpu.VMEM((2, chunks, regions, GROUP, depth), bf16),
            pltpu.VMEM((steps, chunks, 2, regions, GROUP, depth), bf16),
            pltpu.VMEM((2 * regions * GROUP, regions * frames), f32),
            pltpu.VMEM((senders, shard, frames), f32),
            pltpu.VMEM((3, frames + 2 * HALO, frames), f32),
            pltpu.VMEM((2, frames + 4 * HALO, 384), f32),
            pltpu.VMEM((rows, 128), f32),
            pltpu.VMEM((rows + 2 * LEAD, 128), f32),
            pltpu.VMEM((rows + 2 * LEAD, 128), f32),
            pltpu.VMEM((16, 128), f32),
            pltpu.VMEM((128, 512), f32),
            pltpu.VMEM((256, 512), bf16),
            pltpu.VMEM((512, 256), bf16),
            pltpu.VMEM((640, 128), bf16),
            pltpu.VMEM((1, 128), f32),
            pltpu.VMEM((1, 128), f32),
            pltpu.VMEM((3 * frames, 384), bf16),
            pltpu.VMEM((3 * frames, 384), bf16),
            pltpu.VMEM((-(-side // 8) * 8, 128), f32),
            pltpu.VMEM((senders * others, videos, 128), f32),
            dma((9,)),
            dma(()),
            dma(()),
            dma(()),
            dma(()),
            dma((steps,)),
            dma((steps, chunks, pieces)),
            dma((steps,)),
            dma((steps, chunks, 3)),
            dma((2 * chunks + 6,)),
            dma((2 * chunks + 6,)),
            dma(()),
            dma(()),
            pltpu.SemaphoreType.REGULAR((max(1, others - 1),)),
        ],
        compiler_params=pltpu.CompilerParams(
            collective_id=0, has_side_effects=True, vmem_limit_bytes=56 << 20
        ),
        name="whole",
    )(*operands)
    return (scores, totals)


def solution(mesh):
    placed = (
        P(("groups", "qry"), None, None),
        P(("groups", "ref"), "qry", None, None),
        P("groups", None),
        P("groups"),
        P("groups"),
    ) + (P(),) * 8
    return jax.shard_map(
        body,
        mesh=mesh,
        in_specs=placed,
        out_specs=(P(("groups", "qry"), "ref"), P("groups")),
        check_vma=False,
    )
```

```python
import functools
import math

import jax
import jax.numpy as jnp
from jax import lax
from jax.experimental import pallas as pl
from jax.experimental.pallas import tpu as pltpu
from jax.sharding import PartitionSpec as P

MESH = pl.DeviceIdType.MESH
HALO = 8
PITCH = 40
LEAD = 48
OFF = 4
EDGES = ((0, 8), (32, 40))
ALL = ((0, 40),)
INNER = ((8, 32),)
GROUP = 8
NT = (((1,), (1,)), ((), ()))


def spans(flags):
    found = []
    for k, flag in enumerate(flags):
        if flag and (k == 0 or not flags[k - 1]):
            found.append([k, k + 1])
        elif flag:
            found[-1][1] = k + 1
    return [tuple(span) for span in found]


def plan(stages, chunks, frames, tiles):
    side = tiles + 4
    width = frames // chunks
    here, finished, work = set(), [[False] * side for _ in range(3)], []
    for stage in stages:
        here |= set(stage)
        ready = []
        for j in range(side):
            known = True
            for k in range(-1, 5):
                frame = 4 * (j - 2) + k
                outside = chunks - 1 if frame < 0 else 0
                known &= (frame // width if 0 <= frame < frames else outside) in here
            ready.append(known)
        layers = []
        for layer in range(3):
            if layer:
                edge = [False] * layer
                ready = [all(ready[j - 1 : j + 2]) for j in range(layer, side - layer)]
                ready = edge + ready + edge
            layers.append(spans([now and not was for now, was in zip(ready, finished[layer])]))
            finished[layer] = ready
        work.append(layers)
    return work


def chunk_order(chunks):
    return [k // 2 if k % 2 == 0 else chunks - 1 - k // 2 for k in range(chunks)]


def whole_kernel(
    chips, others, scale, cuts,
    pair_hbm, lengths_hbm, len_ref, b4_ref, w1_hbm, b1_hbm, w2_hbm, b2_hbm, w3_hbm, b3_hbm,
    w4_hbm, q_hbm, r_hbm,
    scores_ref, totals_ref,
    pair_ref, lengths_ref, w1_ref, b1_ref, w2_ref, b2_ref, w3_ref, b3_ref, w4_ref,
    q_buf, r_own, r_far, acc, sims_buf, map_buf, z_buf, x_buf, first_buf, second_buf,
    w1_rep, w1_flat, w1_full, w2_full, w3_full, b1_full, b2_full, pick_full, pick_edge,
    score_buf, peaks_buf, edge_out, edge_in,
    small_sem, q_sem, own_sem, send_o, recv_o, send_x, recv_x, send_s, recv_s, send_h, recv_h,
    send_p, recv_p, far_sem, send_e, recv_e,
):
    regions, shard, depth = r_hbm.shape
    frames = q_hbm.shape[0] // regions
    chunks = shard // GROUP
    width = GROUP * 2 * chips
    tiles = frames // 4
    order = chunk_order(chunks)
    last = order[-1]
    me = lax.axis_index("qry")
    chip = me // 2
    core = me % 2
    sibling = chip * 2 + (1 - core)
    right = ((chip + 1) % chips) * 2 + core
    senders = 2 * chips
    col = lax.axis_index("ref")
    peers = senders * others
    mine = me * others + col

    smalls = [
        pltpu.make_async_copy(source, target, small_sem.at[k])
        for k, (source, target) in enumerate(
            (
                (w1_hbm, w1_ref), (b1_hbm, b1_ref), (w2_hbm, w2_ref), (b2_hbm, b2_ref),
                (w3_hbm, w3_ref), (b3_hbm, b3_ref), (w4_hbm, w4_ref), (pair_hbm, pair_ref),
                (lengths_hbm, lengths_ref),
            )
        )
    ]

    def piece(p):
        return pl.ds(cuts[p], cuts[p + 1] - cuts[p])

    pieces = len(cuts) - 1

    def rows_of(g):
        return pl.ds(pl.multiple_of(g * GROUP, GROUP), GROUP)

    def batches(g):
        steps = (0, pieces - 3, pieces - 1, pieces) if g == last else (0, pieces - 2, pieces)
        return list(zip(steps[:-1], steps[1:]))

    def batch(g, p):
        return [lo <= p < hi for lo, hi in batches(g)].index(True)

    def all_of(ref, device, send_sem, recv_sem):
        return pltpu.make_async_remote_copy(
            src_ref=ref, dst_ref=ref, send_sem=send_sem, recv_sem=recv_sem,
            device_id=device, device_id_type=MESH,
        )

    def own_copy(g):
        return pltpu.make_async_copy(r_hbm.at[:, rows_of(g)], r_own.at[0, g], own_sem)

    def own_to_sibling(g):
        return pltpu.make_async_remote_copy(
            src_ref=r_hbm.at[:, rows_of(g)],
            dst_ref=r_own.at[1, g],
            send_sem=send_o,
            recv_sem=recv_o,
            device_id={"qry": sibling},
            device_id_type=MESH,
        )

    def q_copy(k):
        rows = pl.ds(k * frames, frames)
        return pltpu.make_async_copy(q_hbm.at[rows], q_buf.at[rows], q_sem)

    def to_right(step, g, p):
        if step == 0:
            source = r_hbm.at[:, rows_of(g), piece(p)]
        else:
            source = r_far.at[step - 1, g, 0, :, :, piece(p)]
        return pltpu.make_async_remote_copy(
            src_ref=source,
            dst_ref=r_far.at[step, g, 0, :, :, piece(p)],
            send_sem=send_x.at[step],
            recv_sem=recv_x.at[step, g, p],
            device_id={"qry": right},
            device_id_type=MESH,
        )

    def to_sibling(step, g, p):
        return pltpu.make_async_remote_copy(
            src_ref=r_far.at[step, g, 0, :, :, piece(p)],
            dst_ref=r_far.at[step, g, 1, :, :, piece(p)],
            send_sem=send_s.at[step],
            recv_sem=recv_s.at[step, g, batch(g, p)],
            device_id={"qry": sibling},
            device_id_type=MESH,
        )

    map_buf[...] = jnp.zeros_like(map_buf)
    barrier = pltpu.get_barrier_semaphore()
    for k in range(1, senders):
        device = {"qry": (me + k) % senders}
        pl.semaphore_signal(barrier, inc=1, device_id=device, device_id_type=MESH)

    def tell_columns(semaphore):
        for move, there in ((-1, col > 0), (1, col < others - 1)):

            @pl.when(there)
            def _():
                pl.semaphore_signal(
                    semaphore, inc=1, device_id={"ref": col + move}, device_id_type=MESH
                )

    columns_near = jnp.where(col > 0, 1, 0) + jnp.where(col < others - 1, 1, 0)
    tell_columns(barrier)
    pl.semaphore_wait(barrier, senders - 1 + columns_near)

    def enqueue(lo, hi):
        for k in range(lo, min(hi, chunks * pieces)):
            to_right(0, order[k // pieces], k % pieces).start()

    limits = [(chunks - 1) * pieces - 1] * chunks + [chunks * pieces - 2, chunks * pieces]
    limits = [max(limit, 0) for limit in limits[-chunks:]] if chunks > 1 else [pieces]
    enqueue(0, min(pieces, limits[0]))
    for k in range(regions):
        q_copy(k).start()
    for g in range(chunks):
        own_copy(g).start()
    for g in range(chunks):
        own_to_sibling(g).start()
    enqueue(min(pieces, limits[0]), limits[0])
    rounds = others - 1
    if rounds:
        tell_columns(far_sem.at[0])

    def next_round(k):
        if k < rounds:
            pl.semaphore_wait(far_sem.at[k], columns_near)
            if k + 1 < rounds:
                tell_columns(far_sem.at[k + 1])

    for copy in smalls:
        copy.start()
    z_buf[...] = jnp.zeros_like(z_buf)
    first_buf[...] = jnp.zeros_like(first_buf)
    second_buf[...] = jnp.zeros_like(second_buf)
    next_round(0)
    for copy in smalls:
        copy.wait()
    build_weights(
        w1_ref, w2_ref, w3_ref, b1_ref, b2_ref, w1_rep, w1_flat, w1_full, w2_full, w3_full,
        b1_full, b2_full, pick_full, pick_edge,
    )
    next_round(1)
    factor = pair_ref[me, col].astype(jnp.float32) * scale

    def similar(product, blocks):
        best = jnp.max(product.reshape(blocks, regions, GROUP, regions * frames), axis=1)
        total = best[:, :, :frames]
        for k in range(1, regions):
            total = total + best[:, :, k * frames : (k + 1) * frames]
        return total * factor

    def near(side):
        product = lax.dot_general(
            r_own[side].reshape(chunks * regions * GROUP, depth), q_buf[...], NT,
            preferred_element_type=jnp.float32,
        )
        return similar(product, chunks).reshape(shard, frames)

    pltpu.make_async_copy(q_hbm, q_buf, q_sem).wait()
    pltpu.make_async_copy(r_own.at[0], r_own.at[0], own_sem).wait()

    def near_side(side, carry):
        @pl.when(side == 1)
        def _():
            all_of(r_own.at[1], {"qry": sibling}, send_o, recv_o).wait_recv()

        sims_buf[chip * 2 + side * (1 - core) + (1 - side) * core] = near(side)
        return carry

    lax.fori_loop(0, 2, near_side, 0)
    for k in range(2, rounds):
        next_round(k)

    def sources(step):
        origin = (chip + chips - 1 - step) % chips
        return origin * 2 + core, origin * 2 + (1 - core)

    def arrive(step, g, p):
        to_right(step, g, p).wait_recv()
        to_sibling(step, g, p).start()
        if step < chips - 2:
            to_right(step + 1, g, p).start()

    def settle(step, g, lo, hi):
        columns = pl.ds(cuts[lo], cuts[hi] - cuts[lo])
        all_of(
            r_far.at[step, g, 1, :, :, columns], {"qry": sibling}, send_s.at[step],
            recv_s.at[step, g, batch(g, lo)],
        ).wait_recv()
        return part(step, g, lo, hi)

    def part(step, g, first_piece, final_piece):
        columns = pl.ds(cuts[first_piece], cuts[final_piece] - cuts[first_piece])
        block = r_far[step, g, :, :, :, columns].reshape(2 * regions * GROUP, columns.size)
        return lax.dot_general(
            block, q_buf[:, columns], NT, preferred_element_type=jnp.float32
        )

    def keep(step, g, product):
        total = similar(product, 2)
        for k, source in enumerate(sources(step)):
            sims_buf[source, rows_of(g)] = total[k]

    def reachable(move_q, move_r):
        fits = (me + move_q >= 0) & (me + move_q < senders)
        return fits & (col + move_r >= 0) & (col + move_r < others)

    def halo_copy(k, move_q, move_r, g):
        if move_r == 0:
            source = target = pl.ds(HALO + g * width, width)
        elif move_r == 1:
            source, target = pl.ds(frames, HALO), pl.ds(0, HALO)
        else:
            source, target = pl.ds(HALO, HALO), pl.ds(HALO + frames, HALO)
        return pltpu.make_async_remote_copy(
            src_ref=map_buf.at[1, source],
            dst_ref=map_buf.at[1 - move_q, target],
            send_sem=send_h.at[k],
            recv_sem=recv_h.at[k],
            device_id={"qry": me + move_q, "ref": col + move_r},
            device_id_type=MESH,
        )

    moves = [(q, 0, g) for g in range(chunks) for q in (-1, 1)]
    moves += [(q, r, 0 if r < 0 else chunks - 1) for r in (-1, 1) for q in (-1, 1, 0)]
    moves = [(q, r, g) for q, r, g in moves if r or g == last]
    moves = list(enumerate(moves))

    def edge_copy(k, q):
        side = (1 - q) // 2
        return pltpu.make_async_remote_copy(
            src_ref=edge_out.at[k, 1 - side],
            dst_ref=edge_in.at[k, side],
            send_sem=send_e.at[k, side],
            recv_sem=recv_e.at[k, side],
            device_id={"qry": me + q},
            device_id_type=MESH,
        )

    def send_edges(k):
        turned = jnp.transpose(map_buf[1, HALO : HALO + frames, :])
        edge_out[k, 0] = turned[:HALO]
        edge_out[k, 1] = turned[frames - HALO :]
        for q in (-1, 1):

            @pl.when(reachable(q, 0))
            def _():
                edge_copy(k, q).start()

    def take_edges(k, stage):
        for q in (-1, 1):

            @pl.when(reachable(-q, 0))
            def _():
                edge_copy(k, q).wait_recv()
                turned = jnp.transpose(edge_in[k, (1 - q) // 2])
                lanes = slice(frames - HALO, frames) if q == 1 else slice(0, HALO)
                for g in stage:
                    rows = slice(HALO + g * width, HALO + (g + 1) * width)
                    map_buf[1 - q, rows, lanes] = turned[g * width : (g + 1) * width]

    def spread(g):
        for b in range(senders):
            rows = pl.ds(HALO + g * width + b, GROUP, stride=senders)
            map_buf.at[1][rows, :] = sims_buf[b, g * GROUP : (g + 1) * GROUP]
        for k, (q, r, source) in moves:
            if source == g:

                @pl.when(reachable(q, r))
                def _():
                    halo_copy(k, q, r, g).start()

    def halos(stage):
        for k, (q, r, g) in moves:
            if g in stage:

                @pl.when(reachable(-q, -r))
                def _():
                    halo_copy(k, q, r, g).wait_recv()

    where = (me * tiles, col * tiles, senders * tiles, others * tiles)
    stages = (order[: max(chunks - 2, 0)], order[max(chunks - 2, 0) : chunks - 1], [last])
    work = plan(stages, chunks, frames, tiles)

    def convolve(k, parts, pick, groups, kept):
        for lo, hi in work[k][0]:
            conv1(
                lo, hi, groups, parts, where, map_buf, pick, w1_full, b1_full, z_buf, x_buf,
                first_buf,
            )
        for lo, hi in work[k][1]:
            conv2(lo, hi, groups, where, w2_full, b2_full, first_buf, second_buf)
        for lo, hi in work[k][2]:
            found = conv3(lo, hi, kept, w3_full, b3_ref, w4_ref, second_buf)
            at = 0
            for t, end in kept:
                score_buf[lo:hi, t:end] = found[:, at : at + end - t]
                at += end - t

    def network(k):
        halos(stages[k])
        if stages[k]:
            take_edges(k - 2 + min(chunks - 1, 2), stages[k])
        convolve(k, (0, 1, 2), pick_full, ALL, ALL)

    for k, g in enumerate(order[:-1]):
        for step in range(chips - 1):
            for lo, hi in batches(g):
                for p in range(lo, hi):
                    arrive(step, g, p)
                if lo == 0:
                    acc[...] = settle(step, g, lo, hi)
                else:
                    keep(step, g, acc[...] + settle(step, g, lo, hi))
        spread(g)
        if k >= chunks - 3:
            send_edges(k - max(chunks - 3, 0))
        enqueue(limits[k], limits[k + 1])
    network(0)

    for step in range(chips - 1):
        for p in range(pieces - 3):
            arrive(step, last, p)
        acc[...] = settle(step, last, 0, pieces - 3)
        arrive(step, last, pieces - 3)
        if step == 0:
            network(1)
        arrive(step, last, pieces - 2)
        arrive(step, last, pieces - 1)
        acc[...] += settle(step, last, pieces - 3, pieces - 1)
        keep(step, last, acc[...] + settle(step, last, pieces - 1, pieces))
    spread(last)
    convolve(2, (1,), pick_full, ALL, INNER)
    halos(stages[2])
    convolve(2, (0, 1, 2), pick_edge, EDGES, EDGES)

    scores = score_buf[...] + b4_ref[0]
    slot_f = lax.broadcasted_iota(jnp.int32, scores.shape, 0)
    column = slot_f + (col * tiles - 2)
    own = (slot_f >= 2) & (slot_f < 2 + tiles)
    begin = jnp.int32(0)
    for v in range(lengths_ref.shape[0]):
        end = begin + lengths_ref[v]
        member = own & (column >= begin) & (column < end)
        peaks_buf[mine, v : v + 1, :] = jnp.max(
            jnp.where(member, scores, -jnp.inf), axis=0, keepdims=True
        )
        begin = end

    flip = 2 * col // others

    def peak_copy(k):
        move = k % senders
        away = k // senders
        peer_q = (me + move) % senders
        peer_r = (1 - flip) * (others - 1 - away) + flip * away
        return peer_q, peer_r, pltpu.make_async_remote_copy(
            src_ref=peaks_buf.at[mine],
            dst_ref=peaks_buf.at[mine],
            send_sem=send_p,
            recv_sem=recv_p,
            device_id={"qry": peer_q, "ref": peer_r},
            device_id_type=MESH,
        )

    def peak_start(k, carry):
        peer_q, peer_r, copy = peak_copy(k)

        @pl.when((peer_q != me) | (peer_r != col))
        def _():
            copy.start()

        return carry

    lax.fori_loop(0, peers, peak_start, 0)
    scores_ref[...] = jnp.transpose(scores)[OFF : OFF + tiles, 2 : 2 + tiles]

    all_of(r_own.at[1], {"qry": sibling}, send_o, recv_o).wait_send()
    for step in range(chips - 1):
        sent = r_far.at[step, :, 0]
        all_of(sent, {"qry": right}, send_x.at[step], send_x.at[step]).wait_send()
        all_of(sent, {"qry": sibling}, send_s.at[step], send_s.at[step]).wait_send()
    for k, (q, r, g) in moves:

        @pl.when(reachable(q, r))
        def _():
            halo_copy(k, q, r, g).wait_send()

    for k in range(min(chunks - 1, 2)):
        for q in (-1, 1):

            @pl.when(reachable(q, 0))
            def _():
                edge_copy(k, q).wait_send()

    heard = all_of(
        peaks_buf.at[pl.ds(0, peers - 1)], {"qry": sibling}, send_p, recv_p
    )
    heard.wait_recv()
    lane = lax.broadcasted_iota(jnp.int32, peaks_buf.shape[1:], 1)
    total = jnp.zeros(peaks_buf.shape[1:], jnp.float32)
    for s in range(senders):
        best = jnp.max(peaks_buf[s * others : (s + 1) * others], axis=0)
        counted = (lane >= OFF) & (lane < OFF + tiles)
        counted = counted & (lane + (s * tiles - OFF) < len_ref[0])
        total = total + jnp.where(counted, best, 0.0)
    total = jnp.sum(total, axis=1, keepdims=True) / len_ref[0].astype(jnp.float32)
    for v in range(lengths_ref.shape[0]):
        totals_ref[v] = jnp.sum(total[v : v + 1])

    heard.wait_send()


def build_weights(
    w1_ref, w2_ref, w3_ref, b1_ref, b2_ref, w1_rep, w1_flat, w1_full, w2_full, w3_full,
    b1_full, b2_full, pick_full, pick_edge,
):
    for k in range(4):
        lanes = slice(k * 32, (k + 1) * 32)
        b1_full[:, lanes] = b1_ref[...]
        for di in range(3):
            w1_rep[3 * di : 3 * di + 3, lanes] = w1_ref[di]
    for k in range(2):
        b2_full[:, k * 64 : (k + 1) * 64] = b2_ref[...]
    w1_flat[...] = jnp.zeros_like(w1_flat)
    for u in range(2):
        for v in range(2):
            for a in range(2):
                for b in range(2):
                    at = (a * 2 + b) * 32
                    col = (u * 2 + v) * 128 + at
                    for k in range(9):
                        rr = 2 * a + u + k // 3
                        for part in range(2):
                            row = rr % 2 * 48 + part * 24 + rr // 2 * 8 + 2 * b + v + k % 3
                            w1_flat[row : row + 1, col : col + 32] = w1_rep[
                                k : k + 1, at : at + 32
                            ]
    flat = w1_flat[...]
    high = flat.astype(jnp.bfloat16)
    row = lax.broadcasted_iota(jnp.int32, flat.shape, 0)
    w1_full[0:128] = high
    w1_full[128:256] = jnp.where(
        row % 48 < 24, flat - high.astype(jnp.float32), 0.0
    ).astype(jnp.bfloat16)
    frames = pick_full.shape[0] // 3
    source = lax.broadcasted_iota(jnp.int32, (3 * frames, 128), 0)
    target = lax.broadcasted_iota(jnp.int32, (3 * frames, 128), 1)
    begin = 4 * (target % 64 - OFF) + target // 64 + (frames - 1)
    for k in range(3):
        pick_full[:, k * 128 : (k + 1) * 128] = jnp.where(
            source == begin + 2 * k, 1.0, 0.0
        ).astype(jnp.bfloat16)
    at = target % 16
    at = jnp.where(at < 8, at, at + 24)
    begin = 4 * (at - OFF) + target // 64 + (frames - 1)
    for k in range(3):
        pick_edge[:, k * 128 : (k + 1) * 128] = jnp.where(
            source == begin + 2 * k, 1.0, 0.0
        ).astype(jnp.bfloat16)

    w2_full[...] = jnp.zeros_like(w2_full)
    taps = {(0, 0): 0, (0, 1): 1, (1, 0): 2, (1, 1): -1}
    for g in range(2):
        for h in range(2):
            for a in range(2):
                for b in range(2):
                    row = ((g * 2 + h) * 4 + a * 2 + b) * 32
                    for u in range(2):
                        for v in range(2):
                            di = taps[g, a] - u + 1
                            dj = taps[h, b] - v + 1
                            if 0 <= di < 3 and 0 <= dj < 3:
                                col = u * 128 + v * 64
                                w2_full[row : row + 32, col : col + 64] = w2_ref[di * 3 + dj]
    for k in range(9):
        w3_full[k * 64 : (k + 1) * 64, :] = w3_ref[k]
    w3_full[576:640, :] = jnp.zeros((64, 128), jnp.bfloat16)


def span_of(groups):
    return sum(end - t for t, end in groups)


def inside_map(lo, hi, groups, where):
    shape = (hi - lo, span_of(groups), 128)
    at_f = lax.broadcasted_iota(jnp.int32, shape, 0) + (where[1] - 2 + lo)
    at_p = lax.broadcasted_iota(jnp.int32, shape, 1)
    if groups == EDGES:
        at_p = jnp.where(at_p < 8, at_p, at_p + 24)
    at_p = at_p + (where[0] - OFF)
    inside = (at_f >= 0) & (at_f < where[3]) & (at_p >= 0) & (at_p < where[2])
    return jnp.where(inside, 1.0, 0.0).reshape(shape[0] * shape[1], 128)


def rows_at(ref, lo, hi, shift, groups):
    if groups == ALL:
        return ref[LEAD + lo * PITCH + shift : LEAD + hi * PITCH + shift, :]
    found = []
    for block in range(lo, hi):
        base = LEAD + block * PITCH + shift
        found += [ref[base + t : base + end, :] for t, end in groups]
    return jnp.concatenate(found, axis=0)


def put_rows(ref, lo, hi, groups, value):
    if groups == ALL:
        ref[LEAD + lo * PITCH : LEAD + hi * PITCH, :] = value
        return
    at = 0
    for block in range(lo, hi):
        base = LEAD + block * PITCH
        for t, end in groups:
            ref[base + t : base + end, :] = value[at : at + end - t]
            at += end - t


def conv1(
    lo, hi, groups, parts, where, map_ref, pick_ref, w1_full, b1_full, z_buf, x_buf, first_buf
):
    wide, frames = map_ref.shape[1:]
    top = max(0, (4 * lo - 1) // 8 * 8)
    end = min(wide, -(-(4 * hi + 3) // 8) * 8)
    whole = [map_ref[k, top:end] for k in parts]
    whole = jnp.concatenate(whole, axis=1) if len(whole) > 1 else whole[0]
    high = whole.astype(jnp.bfloat16)
    lower = (whole - high.astype(jnp.float32)).astype(jnp.bfloat16)
    pick = pick_ref[parts[0] * frames : (parts[-1] + 1) * frames]
    for part, value in enumerate((high, lower)):
        z_buf[part, 8 + top : 8 + end, :] = jnp.dot(
            value, pick, preferred_element_type=jnp.float32
        )

    def window(block, part, k):
        return z_buf[part, 4 * block + 7 : 4 * block + 15, k * 128 : (k + 1) * 128]

    kinds = [(part, k) for part in range(2) for k in range(3)]
    if groups == ALL:
        blank = jnp.zeros((PITCH, 32), jnp.float32)
        for block in range(lo, hi):
            turned = jnp.transpose(
                jnp.concatenate([window(block, *kind) for kind in kinds], axis=0)
            )
            x_buf[block * PITCH : (block + 1) * PITCH, :] = jnp.concatenate(
                [turned[:PITCH], turned[64 : 64 + PITCH], blank], axis=1
            )
        x = x_buf[lo * PITCH : hi * PITCH]
    else:
        blank = jnp.zeros((64, 32), jnp.float32)
        place = lax.broadcasted_iota(jnp.int32, (8, 128), 1) % 64 // 16
        found = []
        for block in range(lo, hi, 4):
            pieces = []
            for kind in kinds:
                piece = window(block, *kind)
                for g in range(1, min(4, hi - block)):
                    piece = jnp.where(place == g, window(block + g, *kind), piece)
                pieces.append(piece)
            turned = jnp.transpose(jnp.concatenate(pieces, axis=0))
            found.append(jnp.concatenate([turned[:64], turned[64:], blank], axis=1))
        x = jnp.concatenate(found, axis=0)[: (hi - lo) * 16]
    x = x.astype(jnp.bfloat16)
    made = jnp.dot(
        jnp.concatenate([x, x], axis=1), w1_full[...], preferred_element_type=jnp.float32
    )
    best = jnp.maximum(
        jnp.maximum(made[:, 0:128], made[:, 128:256]),
        jnp.maximum(made[:, 256:384], made[:, 384:512]),
    )
    first = jnp.maximum(best + b1_full[...], 0.0)
    first = first * inside_map(lo, hi, groups, where)
    put_rows(first_buf, lo, hi, groups, first.astype(jnp.bfloat16).astype(jnp.float32))


def conv2(lo, hi, groups, where, w2_full, b2_full, first_buf, second_buf):
    lane = lax.broadcasted_iota(jnp.int32, (1, 128), 1)
    low_a = lane < 64
    low_b = (lane % 64) < 32
    one = span_of(groups)
    rows = (hi - lo) * one
    first = rows_at(first_buf, lo - 1, hi + 1, 0, groups)
    shifted = jnp.where(
        low_a,
        rows_at(first_buf, lo - 1, hi + 1, 1, groups),
        rows_at(first_buf, lo - 1, hi + 1, -1, groups),
    )
    across = jnp.where(low_b, first[2 * one :], first[:rows])
    both = jnp.where(low_b, shifted[2 * one :], shifted[:rows])
    stacked = jnp.concatenate(
        [first[one : one + rows], across, shifted[one : one + rows], both], axis=1
    ).astype(jnp.bfloat16)
    made = jnp.dot(stacked, w2_full[...], preferred_element_type=jnp.float32)
    best = jnp.maximum(made[:, 0:128], made[:, 128:256])
    best = jnp.maximum(best, pltpu.roll(best, 64, 1))
    second = jnp.maximum(best + b2_full[...], 0.0)
    second = second * inside_map(lo, hi, groups, where)
    put_rows(second_buf, lo, hi, groups, second.astype(jnp.bfloat16).astype(jnp.float32))


def conv3(lo, hi, groups, w3_full, b3_ref, w4_ref, second_buf):
    lane = lax.broadcasted_iota(jnp.int32, (1, 128), 1)
    low_a = lane < 64

    def moved(k):
        return rows_at(second_buf, lo + k % 3 - 1, hi + k % 3 - 1, k // 3 - 1, groups)

    taps = []
    for k in range(0, 9, 2):
        taps.append(jnp.where(low_a, moved(k), moved(k + 1)) if k < 8 else moved(k))
    stacked = jnp.concatenate(taps, axis=1).astype(jnp.bfloat16)
    made = jnp.dot(stacked, w3_full[...], preferred_element_type=jnp.float32)
    third = jnp.maximum(made + b3_ref[...], 0.0).astype(jnp.bfloat16).astype(jnp.float32)
    weighted = third * w4_ref[...].astype(jnp.float32)
    return jnp.sum(weighted.reshape(hi - lo, span_of(groups), 128), axis=2)


def body(
    query_feats, ref_feats, pair_table, lengths, query_len, conv1_weight, conv1_bias,
    conv2_weight, conv2_bias, conv3_weight, conv3_bias, conv4_weight, conv4_bias,
):
    senders = lax.axis_size("qry")
    others = lax.axis_size("ref")
    frames, regions, depth = query_feats.shape
    query_mat = jnp.transpose(query_feats, (1, 0, 2)).reshape(regions * frames, depth)
    ref_mat = jnp.transpose(ref_feats, (1, 2, 0, 3)).reshape(regions, -1, depth)
    videos = lengths.shape[0]
    shard = ref_mat.shape[1]
    chunks = shard // GROUP
    chips = senders // 2
    steps = max(1, chips - 1)
    cuts = [depth * k // 6 // 128 * 128 for k in range(7)]
    pieces = len(cuts) - 1
    tiles = frames // 4
    side = tiles + 4
    rows = side * PITCH
    scale = 1.0 / (regions * math.sqrt(depth))
    vmem = pl.BlockSpec(memory_space=pltpu.VMEM)
    smem = pl.BlockSpec(memory_space=pltpu.SMEM)
    hbm = pl.BlockSpec(memory_space=pltpu.HBM)
    dma = pltpu.SemaphoreType.DMA
    f32, bf16 = jnp.float32, jnp.bfloat16
    operands = (
        pair_table,
        lengths,
        query_len,
        conv4_bias,
        conv1_weight,
        conv1_bias[None],
        jnp.transpose(conv2_weight, (0, 1, 3, 2)).reshape(
            9, conv2_weight.shape[3], conv2_weight.shape[2]
        ),
        conv2_bias[None],
        jnp.transpose(conv3_weight, (0, 1, 3, 2)).reshape(
            9, conv3_weight.shape[3], conv3_weight.shape[2]
        ),
        conv3_bias[None],
        conv4_weight[None],
        query_mat,
        ref_mat,
    )
    kept = [
        (pltpu.SMEM if k < 4 else pltpu.VMEM)(operand.shape, operand.dtype)
        for k, operand in enumerate(operands[:11]) if k not in (2, 3)
    ]
    scores, totals = pl.pallas_call(
        functools.partial(whole_kernel, chips, others, scale, cuts),
        out_shape=(
            pltpu.VMEM((tiles, tiles), f32),
            pltpu.SMEM((videos,), f32),
        ),
        in_specs=[hbm] * 2 + [smem] * 2 + [hbm] * (len(operands) - 4),
        out_specs=(vmem, smem),
        scratch_shapes=kept + [
            pltpu.VMEM(query_mat.shape, bf16),
            pltpu.VMEM((2, chunks, regions, GROUP, depth), bf16),
            pltpu.VMEM((steps, chunks, 2, regions, GROUP, depth), bf16),
            pltpu.VMEM((2 * regions * GROUP, regions * frames), f32),
            pltpu.VMEM((senders, shard, frames), f32),
            pltpu.VMEM((3, frames + 2 * HALO, frames), f32),
            pltpu.VMEM((2, frames + 4 * HALO, 384), f32),
            pltpu.VMEM((rows, 128), f32),
            pltpu.VMEM((rows + 2 * LEAD, 128), f32),
            pltpu.VMEM((rows + 2 * LEAD, 128), f32),
            pltpu.VMEM((16, 128), f32),
            pltpu.VMEM((128, 512), f32),
            pltpu.VMEM((256, 512), bf16),
            pltpu.VMEM((512, 256), bf16),
            pltpu.VMEM((640, 128), bf16),
            pltpu.VMEM((1, 128), f32),
            pltpu.VMEM((1, 128), f32),
            pltpu.VMEM((3 * frames, 384), bf16),
            pltpu.VMEM((3 * frames, 384), bf16),
            pltpu.VMEM((-(-side // 8) * 8, 128), f32),
            pltpu.VMEM((senders * others, videos, 128), f32),
            pltpu.VMEM((2, 2, HALO, frames), f32),
            pltpu.VMEM((2, 2, HALO, frames), f32),
            dma((9,)),
            dma(()),
            dma(()),
            dma(()),
            dma(()),
            dma((steps,)),
            dma((steps, chunks, pieces)),
            dma((steps,)),
            dma((steps, chunks, 3)),
            dma((8,)),
            dma((8,)),
            dma(()),
            dma(()),
            pltpu.SemaphoreType.REGULAR((max(1, others - 1),)),
            dma((2, 2)),
            dma((2, 2)),
        ],
        compiler_params=pltpu.CompilerParams(
            collective_id=0, has_side_effects=True, vmem_limit_bytes=56 << 20
        ),
        name="whole",
    )(*operands)
    return (scores, totals)


def solution(mesh):
    placed = (
        P(("groups", "qry"), None, None),
        P(("groups", "ref"), "qry", None, None),
        P("groups", None),
        P("groups"),
        P("groups"),
    ) + (P(),) * 8
    return jax.shard_map(
        body,
        mesh=mesh,
        in_specs=placed,
        out_specs=(P(("groups", "qry"), "ref"), P("groups")),
        check_vma=False,
    )
```

```python
import functools
import math

import jax
import jax.numpy as jnp
from jax import lax
from jax.experimental import pallas as pl
from jax.experimental.pallas import tpu as pltpu
from jax.sharding import PartitionSpec as P

MESH = pl.DeviceIdType.MESH
HALO = 8
PITCH = 40
LEAD = 48
OFF = 4
EDGES = ((0, 8), (32, 40))
ALL = ((0, 40),)
INNER = ((8, 32),)
GROUP = 8
NT = (((1,), (1,)), ((), ()))


def spans(flags):
    found = []
    for k, flag in enumerate(flags):
        if flag and (k == 0 or not flags[k - 1]):
            found.append([k, k + 1])
        elif flag:
            found[-1][1] = k + 1
    return [tuple(span) for span in found]


def plan(stages, chunks, frames, tiles):
    side = tiles + 4
    width = frames // chunks
    here, finished, work = set(), [[False] * side for _ in range(3)], []
    for stage in stages:
        here |= set(stage)
        ready = []
        for j in range(side):
            known = True
            for k in range(-1, 5):
                frame = 4 * (j - 2) + k
                outside = chunks - 1 if frame < 0 else 0
                known &= (frame // width if 0 <= frame < frames else outside) in here
            ready.append(known)
        layers = []
        for layer in range(3):
            if layer:
                edge = [False] * layer
                ready = [all(ready[j - 1 : j + 2]) for j in range(layer, side - layer)]
                ready = edge + ready + edge
            layers.append(spans([now and not was for now, was in zip(ready, finished[layer])]))
            finished[layer] = ready
        work.append(layers)
    return work


def chunk_order(chunks):
    return [k // 2 if k % 2 == 0 else chunks - 1 - k // 2 for k in range(chunks)]


def whole_kernel(
    chips, others, scale, cuts,
    pair_hbm, lengths_hbm, len_ref, b4_ref, w1_hbm, b1_hbm, w2_hbm, b2_hbm, w3_hbm, b3_hbm,
    w4_hbm, q_hbm, r_hbm,
    scores_ref, totals_ref,
    pair_ref, lengths_ref, w1_ref, b1_ref, w2_ref, b2_ref, w3_ref, b3_ref, w4_ref,
    q_buf, r_own, r_far, acc, sims_buf, map_buf, z_buf, x_buf, first_buf, second_buf,
    w1_rep, w1_flat, w1_full, w2_full, w3_full, b1_full, b2_full, pick_full, pick_edge,
    score_buf, peaks_buf, edge_out, edge_in,
    small_sem, q_sem, own_sem, send_o, recv_o, send_x, recv_x, send_s, recv_s, send_h, recv_h,
    send_p, recv_p, far_sem, send_e, recv_e,
):
    regions, shard, depth = r_hbm.shape
    frames = q_hbm.shape[0] // regions
    chunks = shard // GROUP
    width = GROUP * 2 * chips
    tiles = frames // 4
    order = chunk_order(chunks)
    last = order[-1]
    me = lax.axis_index("qry")
    chip = me // 2
    core = me % 2
    sibling = chip * 2 + (1 - core)
    right = ((chip + 1) % chips) * 2 + core
    senders = 2 * chips
    col = lax.axis_index("ref")
    peers = senders * others
    mine = me * others + col

    smalls = [
        pltpu.make_async_copy(source, target, small_sem.at[k])
        for k, (source, target) in enumerate(
            (
                (w1_hbm, w1_ref), (b1_hbm, b1_ref), (w2_hbm, w2_ref), (b2_hbm, b2_ref),
                (w3_hbm, w3_ref), (b3_hbm, b3_ref), (w4_hbm, w4_ref), (pair_hbm, pair_ref),
                (lengths_hbm, lengths_ref),
            )
        )
    ]

    def piece(p):
        return pl.ds(cuts[p], cuts[p + 1] - cuts[p])

    pieces = len(cuts) - 1

    def rows_of(g):
        return pl.ds(pl.multiple_of(g * GROUP, GROUP), GROUP)

    def batches(g):
        steps = (0, *range(pieces - 3, pieces + 1)) if g == last else (0, pieces - 2, pieces)
        return list(zip(steps[:-1], steps[1:]))

    def batch(g, p):
        return [lo <= p < hi for lo, hi in batches(g)].index(True)

    def all_of(ref, device, send_sem, recv_sem):
        return pltpu.make_async_remote_copy(
            src_ref=ref, dst_ref=ref, send_sem=send_sem, recv_sem=recv_sem,
            device_id=device, device_id_type=MESH,
        )

    def own_copy(g):
        return pltpu.make_async_copy(r_hbm.at[:, rows_of(g)], r_own.at[0, g], own_sem)

    def own_to_sibling(g):
        return pltpu.make_async_remote_copy(
            src_ref=r_hbm.at[:, rows_of(g)],
            dst_ref=r_own.at[1, g],
            send_sem=send_o,
            recv_sem=recv_o,
            device_id={"qry": sibling},
            device_id_type=MESH,
        )

    def q_copy(k):
        rows = pl.ds(k * frames, frames)
        return pltpu.make_async_copy(q_hbm.at[rows], q_buf.at[rows], q_sem)

    def to_right(step, g, p):
        if step == 0:
            source = r_hbm.at[:, rows_of(g), piece(p)]
        else:
            source = r_far.at[step - 1, g, 0, :, :, piece(p)]
        return pltpu.make_async_remote_copy(
            src_ref=source,
            dst_ref=r_far.at[step, g, 0, :, :, piece(p)],
            send_sem=send_x.at[step],
            recv_sem=recv_x.at[step, g, p],
            device_id={"qry": right},
            device_id_type=MESH,
        )

    def to_sibling(step, g, p):
        return pltpu.make_async_remote_copy(
            src_ref=r_far.at[step, g, 0, :, :, piece(p)],
            dst_ref=r_far.at[step, g, 1, :, :, piece(p)],
            send_sem=send_s.at[step],
            recv_sem=recv_s.at[step, g, batch(g, p)],
            device_id={"qry": sibling},
            device_id_type=MESH,
        )

    map_buf[...] = jnp.zeros_like(map_buf)
    barrier = pltpu.get_barrier_semaphore()
    for k in range(1, senders):
        device = {"qry": (me + k) % senders}
        pl.semaphore_signal(barrier, inc=1, device_id=device, device_id_type=MESH)

    def tell_columns(semaphore):
        for move, there in ((-1, col > 0), (1, col < others - 1)):

            @pl.when(there)
            def _():
                pl.semaphore_signal(
                    semaphore, inc=1, device_id={"ref": col + move}, device_id_type=MESH
                )

    columns_near = jnp.where(col > 0, 1, 0) + jnp.where(col < others - 1, 1, 0)
    tell_columns(barrier)
    pl.semaphore_wait(barrier, senders - 1 + columns_near)

    def enqueue(lo, hi):
        for k in range(lo, min(hi, chunks * pieces)):
            to_right(0, order[k // pieces], k % pieces).start()

    limits = [(chunks - 1) * pieces - 1] * chunks + [chunks * pieces - 2, chunks * pieces]
    limits = [max(limit, 0) for limit in limits[-chunks:]] if chunks > 1 else [pieces]
    enqueue(0, min(pieces, limits[0]))
    for k in range(regions):
        q_copy(k).start()
    for g in range(chunks):
        own_copy(g).start()
    for g in range(chunks):
        own_to_sibling(g).start()
    enqueue(min(pieces, limits[0]), limits[0])
    rounds = others - 1
    if rounds:
        tell_columns(far_sem.at[0])

    def next_round(k):
        if k < rounds:
            pl.semaphore_wait(far_sem.at[k], columns_near)
            if k + 1 < rounds:
                tell_columns(far_sem.at[k + 1])

    for copy in smalls:
        copy.start()
    z_buf[...] = jnp.zeros_like(z_buf)
    first_buf[...] = jnp.zeros_like(first_buf)
    second_buf[...] = jnp.zeros_like(second_buf)
    next_round(0)
    for copy in smalls:
        copy.wait()
    build_weights(
        w1_ref, w2_ref, w3_ref, b1_ref, b2_ref, w1_rep, w1_flat, w1_full, w2_full, w3_full,
        b1_full, b2_full, pick_full, pick_edge,
    )
    next_round(1)
    factor = pair_ref[me, col].astype(jnp.float32) * scale

    def similar(product, blocks):
        best = jnp.max(product.reshape(blocks, regions, GROUP, regions * frames), axis=1)
        total = best[:, :, :frames]
        for k in range(1, regions):
            total = total + best[:, :, k * frames : (k + 1) * frames]
        return total * factor

    def near(side):
        product = lax.dot_general(
            r_own[side].reshape(chunks * regions * GROUP, depth), q_buf[...], NT,
            preferred_element_type=jnp.float32,
        )
        return similar(product, chunks).reshape(shard, frames)

    pltpu.make_async_copy(q_hbm, q_buf, q_sem).wait()
    pltpu.make_async_copy(r_own.at[0], r_own.at[0], own_sem).wait()

    def near_side(side, carry):
        @pl.when(side == 1)
        def _():
            all_of(r_own.at[1], {"qry": sibling}, send_o, recv_o).wait_recv()

        sims_buf[chip * 2 + side * (1 - core) + (1 - side) * core] = near(side)
        return carry

    lax.fori_loop(0, 2, near_side, 0)
    for k in range(2, rounds):
        next_round(k)

    def sources(step):
        origin = (chip + chips - 1 - step) % chips
        return origin * 2 + core, origin * 2 + (1 - core)

    def arrive(step, g, p):
        to_right(step, g, p).wait_recv()
        to_sibling(step, g, p).start()
        if step < chips - 2:
            to_right(step + 1, g, p).start()

    def settle(step, g, lo, hi):
        columns = pl.ds(cuts[lo], cuts[hi] - cuts[lo])
        all_of(
            r_far.at[step, g, 1, :, :, columns], {"qry": sibling}, send_s.at[step],
            recv_s.at[step, g, batch(g, lo)],
        ).wait_recv()
        return part(step, g, lo, hi)

    def part(step, g, first_piece, final_piece):
        columns = pl.ds(cuts[first_piece], cuts[final_piece] - cuts[first_piece])
        block = r_far[step, g, :, :, :, columns].reshape(2 * regions * GROUP, columns.size)
        return lax.dot_general(
            block, q_buf[:, columns], NT, preferred_element_type=jnp.float32
        )

    def keep(step, g, product):
        total = similar(product, 2)
        for k, source in enumerate(sources(step)):
            sims_buf[source, rows_of(g)] = total[k]

    def reachable(move_q, move_r):
        fits = (me + move_q >= 0) & (me + move_q < senders)
        return fits & (col + move_r >= 0) & (col + move_r < others)

    def halo_copy(k, move_q, move_r, g):
        if move_r == 0:
            source = target = pl.ds(HALO + g * width, width)
        elif move_r == 1:
            source, target = pl.ds(frames, HALO), pl.ds(0, HALO)
        else:
            source, target = pl.ds(HALO, HALO), pl.ds(HALO + frames, HALO)
        return pltpu.make_async_remote_copy(
            src_ref=map_buf.at[1, source],
            dst_ref=map_buf.at[1 - move_q, target],
            send_sem=send_h.at[k],
            recv_sem=recv_h.at[k],
            device_id={"qry": me + move_q, "ref": col + move_r},
            device_id_type=MESH,
        )

    moves = [(q, 0, g) for g in range(chunks) for q in (-1, 1)]
    moves += [(q, r, 0 if r < 0 else chunks - 1) for r in (-1, 1) for q in (-1, 1, 0)]
    moves = [(q, r, g) for q, r, g in moves if r or g == last]
    moves = list(enumerate(moves))

    def edge_copy(k, q):
        side = (1 - q) // 2
        return pltpu.make_async_remote_copy(
            src_ref=edge_out.at[k, 1 - side],
            dst_ref=edge_in.at[k, side],
            send_sem=send_e.at[k, side],
            recv_sem=recv_e.at[k, side],
            device_id={"qry": me + q},
            device_id_type=MESH,
        )

    def send_edges(k):
        turned = jnp.transpose(map_buf[1, HALO : HALO + frames, :])
        edge_out[k, 0] = turned[:HALO]
        edge_out[k, 1] = turned[frames - HALO :]
        for q in (-1, 1):

            @pl.when(reachable(q, 0))
            def _():
                edge_copy(k, q).start()

    def take_edges(k, stage):
        for q in (-1, 1):

            @pl.when(reachable(-q, 0))
            def _():
                edge_copy(k, q).wait_recv()
                turned = jnp.transpose(edge_in[k, (1 - q) // 2])
                lanes = slice(frames - HALO, frames) if q == 1 else slice(0, HALO)
                for g in stage:
                    rows = slice(HALO + g * width, HALO + (g + 1) * width)
                    map_buf[1 - q, rows, lanes] = turned[g * width : (g + 1) * width]

    def spread(g):
        for b in range(senders):
            rows = pl.ds(HALO + g * width + b, GROUP, stride=senders)
            map_buf.at[1][rows, :] = sims_buf[b, g * GROUP : (g + 1) * GROUP]
        for k, (q, r, source) in moves:
            if source == g:

                @pl.when(reachable(q, r))
                def _():
                    halo_copy(k, q, r, g).start()

    def halos(stage):
        for k, (q, r, g) in moves:
            if g in stage:

                @pl.when(reachable(-q, -r))
                def _():
                    halo_copy(k, q, r, g).wait_recv()

    where = (me * tiles, col * tiles, senders * tiles, others * tiles)
    stages = (order[: max(chunks - 2, 0)], order[max(chunks - 2, 0) : chunks - 1], [last])
    work = plan(stages, chunks, frames, tiles)

    def convolve(k, parts, pick, groups, kept):
        for lo, hi in work[k][0]:
            conv1(
                lo, hi, groups, parts, where, map_buf, pick, w1_full, b1_full, z_buf, x_buf,
                first_buf,
            )
        for lo, hi in work[k][1]:
            conv2(lo, hi, groups, where, w2_full, b2_full, first_buf, second_buf)
        for lo, hi in work[k][2]:
            found = conv3(lo, hi, kept, w3_full, b3_ref, w4_ref, second_buf)
            at = 0
            for t, end in kept:
                score_buf[lo:hi, t:end] = found[:, at : at + end - t]
                at += end - t

    def network(k):
        halos(stages[k])
        if stages[k]:
            take_edges(k - 2 + min(chunks - 1, 2), stages[k])
        convolve(k, (0, 1, 2), pick_full, ALL, ALL)

    for k, g in enumerate(order[:-1]):
        for step in range(chips - 1):
            for lo, hi in batches(g):
                for p in range(lo, hi):
                    arrive(step, g, p)
                if lo == 0:
                    acc[...] = settle(step, g, lo, hi)
                else:
                    keep(step, g, acc[...] + settle(step, g, lo, hi))
        spread(g)
        if k >= chunks - 3:
            send_edges(k - max(chunks - 3, 0))
        enqueue(limits[k], limits[k + 1])
    network(0)

    for step in range(chips - 1):
        for p in range(pieces - 3):
            arrive(step, last, p)
        acc[...] = settle(step, last, 0, pieces - 3)
        arrive(step, last, pieces - 3)
        if step == 0:
            network(1)
        acc[...] += settle(step, last, pieces - 3, pieces - 2)
        arrive(step, last, pieces - 2)
        arrive(step, last, pieces - 1)
        acc[...] += settle(step, last, pieces - 2, pieces - 1)
        keep(step, last, acc[...] + settle(step, last, pieces - 1, pieces))
    spread(last)
    convolve(2, (1,), pick_full, ALL, INNER)
    halos(stages[2])
    convolve(2, (0, 1, 2), pick_edge, EDGES, EDGES)

    scores = score_buf[...] + b4_ref[0]
    slot_f = lax.broadcasted_iota(jnp.int32, scores.shape, 0)
    column = slot_f + (col * tiles - 2)
    own = (slot_f >= 2) & (slot_f < 2 + tiles)
    begin = jnp.int32(0)
    for v in range(lengths_ref.shape[0]):
        end = begin + lengths_ref[v]
        member = own & (column >= begin) & (column < end)
        peaks_buf[mine, v : v + 1, :] = jnp.max(
            jnp.where(member, scores, -jnp.inf), axis=0, keepdims=True
        )
        begin = end

    flip = 2 * col // others

    def peak_copy(k):
        move = k % senders
        away = k // senders
        peer_q = (me + move) % senders
        peer_r = (1 - flip) * (others - 1 - away) + flip * away
        return peer_q, peer_r, pltpu.make_async_remote_copy(
            src_ref=peaks_buf.at[mine],
            dst_ref=peaks_buf.at[mine],
            send_sem=send_p,
            recv_sem=recv_p,
            device_id={"qry": peer_q, "ref": peer_r},
            device_id_type=MESH,
        )

    def peak_start(k, carry):
        peer_q, peer_r, copy = peak_copy(k)

        @pl.when((peer_q != me) | (peer_r != col))
        def _():
            copy.start()

        return carry

    lax.fori_loop(0, peers, peak_start, 0)
    scores_ref[...] = jnp.transpose(scores)[OFF : OFF + tiles, 2 : 2 + tiles]

    all_of(r_own.at[1], {"qry": sibling}, send_o, recv_o).wait_send()
    for step in range(chips - 1):
        sent = r_far.at[step, :, 0]
        all_of(sent, {"qry": right}, send_x.at[step], send_x.at[step]).wait_send()
        all_of(sent, {"qry": sibling}, send_s.at[step], send_s.at[step]).wait_send()
    for k, (q, r, g) in moves:

        @pl.when(reachable(q, r))
        def _():
            halo_copy(k, q, r, g).wait_send()

    for k in range(min(chunks - 1, 2)):
        for q in (-1, 1):

            @pl.when(reachable(q, 0))
            def _():
                edge_copy(k, q).wait_send()

    heard = all_of(
        peaks_buf.at[pl.ds(0, peers - 1)], {"qry": sibling}, send_p, recv_p
    )
    heard.wait_recv()
    lane = lax.broadcasted_iota(jnp.int32, peaks_buf.shape[1:], 1)
    total = jnp.zeros(peaks_buf.shape[1:], jnp.float32)
    for s in range(senders):
        best = jnp.max(peaks_buf[s * others : (s + 1) * others], axis=0)
        counted = (lane >= OFF) & (lane < OFF + tiles)
        counted = counted & (lane + (s * tiles - OFF) < len_ref[0])
        total = total + jnp.where(counted, best, 0.0)
    total = jnp.sum(total, axis=1, keepdims=True) / len_ref[0].astype(jnp.float32)
    for v in range(lengths_ref.shape[0]):
        totals_ref[v] = jnp.sum(total[v : v + 1])

    heard.wait_send()


def build_weights(
    w1_ref, w2_ref, w3_ref, b1_ref, b2_ref, w1_rep, w1_flat, w1_full, w2_full, w3_full,
    b1_full, b2_full, pick_full, pick_edge,
):
    for k in range(4):
        lanes = slice(k * 32, (k + 1) * 32)
        b1_full[:, lanes] = b1_ref[...]
        for di in range(3):
            w1_rep[3 * di : 3 * di + 3, lanes] = w1_ref[di]
    for k in range(2):
        b2_full[:, k * 64 : (k + 1) * 64] = b2_ref[...]
    w1_flat[...] = jnp.zeros_like(w1_flat)
    for u in range(2):
        for v in range(2):
            for a in range(2):
                for b in range(2):
                    at = (a * 2 + b) * 32
                    col = (u * 2 + v) * 128 + at
                    for k in range(9):
                        rr = 2 * a + u + k // 3
                        for part in range(2):
                            row = rr % 2 * 48 + part * 24 + rr // 2 * 8 + 2 * b + v + k % 3
                            w1_flat[row : row + 1, col : col + 32] = w1_rep[
                                k : k + 1, at : at + 32
                            ]
    flat = w1_flat[...]
    high = flat.astype(jnp.bfloat16)
    row = lax.broadcasted_iota(jnp.int32, flat.shape, 0)
    w1_full[0:128] = high
    w1_full[128:256] = jnp.where(
        row % 48 < 24, flat - high.astype(jnp.float32), 0.0
    ).astype(jnp.bfloat16)
    frames = pick_full.shape[0] // 3
    source = lax.broadcasted_iota(jnp.int32, (3 * frames, 128), 0)
    target = lax.broadcasted_iota(jnp.int32, (3 * frames, 128), 1)
    begin = 4 * (target % 64 - OFF) + target // 64 + (frames - 1)
    for k in range(3):
        pick_full[:, k * 128 : (k + 1) * 128] = jnp.where(
            source == begin + 2 * k, 1.0, 0.0
        ).astype(jnp.bfloat16)
    at = target % 16
    at = jnp.where(at < 8, at, at + 24)
    begin = 4 * (at - OFF) + target // 64 + (frames - 1)
    for k in range(3):
        pick_edge[:, k * 128 : (k + 1) * 128] = jnp.where(
            source == begin + 2 * k, 1.0, 0.0
        ).astype(jnp.bfloat16)

    w2_full[...] = jnp.zeros_like(w2_full)
    taps = {(0, 0): 0, (0, 1): 1, (1, 0): 2, (1, 1): -1}
    for g in range(2):
        for h in range(2):
            for a in range(2):
                for b in range(2):
                    row = ((g * 2 + h) * 4 + a * 2 + b) * 32
                    for u in range(2):
                        for v in range(2):
                            di = taps[g, a] - u + 1
                            dj = taps[h, b] - v + 1
                            if 0 <= di < 3 and 0 <= dj < 3:
                                col = u * 128 + v * 64
                                w2_full[row : row + 32, col : col + 64] = w2_ref[di * 3 + dj]
    for k in range(9):
        w3_full[k * 64 : (k + 1) * 64, :] = w3_ref[k]
    w3_full[576:640, :] = jnp.zeros((64, 128), jnp.bfloat16)


def span_of(groups):
    return sum(end - t for t, end in groups)


def inside_map(lo, hi, groups, where):
    shape = (hi - lo, span_of(groups), 128)
    at_f = lax.broadcasted_iota(jnp.int32, shape, 0) + (where[1] - 2 + lo)
    at_p = lax.broadcasted_iota(jnp.int32, shape, 1)
    if groups == EDGES:
        at_p = jnp.where(at_p < 8, at_p, at_p + 24)
    at_p = at_p + (where[0] - OFF)
    inside = (at_f >= 0) & (at_f < where[3]) & (at_p >= 0) & (at_p < where[2])
    return jnp.where(inside, 1.0, 0.0).reshape(shape[0] * shape[1], 128)


def rows_at(ref, lo, hi, shift, groups):
    if groups == ALL:
        return ref[LEAD + lo * PITCH + shift : LEAD + hi * PITCH + shift, :]
    found = []
    for block in range(lo, hi):
        base = LEAD + block * PITCH + shift
        found += [ref[base + t : base + end, :] for t, end in groups]
    return jnp.concatenate(found, axis=0)


def put_rows(ref, lo, hi, groups, value):
    if groups == ALL:
        ref[LEAD + lo * PITCH : LEAD + hi * PITCH, :] = value
        return
    at = 0
    for block in range(lo, hi):
        base = LEAD + block * PITCH
        for t, end in groups:
            ref[base + t : base + end, :] = value[at : at + end - t]
            at += end - t


def conv1(
    lo, hi, groups, parts, where, map_ref, pick_ref, w1_full, b1_full, z_buf, x_buf, first_buf
):
    wide, frames = map_ref.shape[1:]
    top = max(0, (4 * lo - 1) // 8 * 8)
    end = min(wide, -(-(4 * hi + 3) // 8) * 8)
    whole = [map_ref[k, top:end] for k in parts]
    whole = jnp.concatenate(whole, axis=1) if len(whole) > 1 else whole[0]
    high = whole.astype(jnp.bfloat16)
    lower = (whole - high.astype(jnp.float32)).astype(jnp.bfloat16)
    pick = pick_ref[parts[0] * frames : (parts[-1] + 1) * frames]
    for part, value in enumerate((high, lower)):
        z_buf[part, 8 + top : 8 + end, :] = jnp.dot(
            value, pick, preferred_element_type=jnp.float32
        )

    def window(block, part, k):
        return z_buf[part, 4 * block + 7 : 4 * block + 15, k * 128 : (k + 1) * 128]

    kinds = [(part, k) for part in range(2) for k in range(3)]
    if groups == ALL:
        blank = jnp.zeros((PITCH, 32), jnp.float32)
        for block in range(lo, hi):
            turned = jnp.transpose(
                jnp.concatenate([window(block, *kind) for kind in kinds], axis=0)
            )
            x_buf[block * PITCH : (block + 1) * PITCH, :] = jnp.concatenate(
                [turned[:PITCH], turned[64 : 64 + PITCH], blank], axis=1
            )
        x = x_buf[lo * PITCH : hi * PITCH]
    else:
        blank = jnp.zeros((64, 32), jnp.float32)
        place = lax.broadcasted_iota(jnp.int32, (8, 128), 1) % 64 // 16
        found = []
        for block in range(lo, hi, 4):
            pieces = []
            for kind in kinds:
                piece = window(block, *kind)
                for g in range(1, min(4, hi - block)):
                    piece = jnp.where(place == g, window(block + g, *kind), piece)
                pieces.append(piece)
            turned = jnp.transpose(jnp.concatenate(pieces, axis=0))
            found.append(jnp.concatenate([turned[:64], turned[64:], blank], axis=1))
        x = jnp.concatenate(found, axis=0)[: (hi - lo) * 16]
    x = x.astype(jnp.bfloat16)
    made = jnp.dot(
        jnp.concatenate([x, x], axis=1), w1_full[...], preferred_element_type=jnp.float32
    )
    best = jnp.maximum(
        jnp.maximum(made[:, 0:128], made[:, 128:256]),
        jnp.maximum(made[:, 256:384], made[:, 384:512]),
    )
    first = jnp.maximum(best + b1_full[...], 0.0)
    first = first * inside_map(lo, hi, groups, where)
    put_rows(first_buf, lo, hi, groups, first.astype(jnp.bfloat16).astype(jnp.float32))


def conv2(lo, hi, groups, where, w2_full, b2_full, first_buf, second_buf):
    lane = lax.broadcasted_iota(jnp.int32, (1, 128), 1)
    low_a = lane < 64
    low_b = (lane % 64) < 32
    one = span_of(groups)
    rows = (hi - lo) * one
    first = rows_at(first_buf, lo - 1, hi + 1, 0, groups)
    shifted = jnp.where(
        low_a,
        rows_at(first_buf, lo - 1, hi + 1, 1, groups),
        rows_at(first_buf, lo - 1, hi + 1, -1, groups),
    )
    across = jnp.where(low_b, first[2 * one :], first[:rows])
    both = jnp.where(low_b, shifted[2 * one :], shifted[:rows])
    stacked = jnp.concatenate(
        [first[one : one + rows], across, shifted[one : one + rows], both], axis=1
    ).astype(jnp.bfloat16)
    made = jnp.dot(stacked, w2_full[...], preferred_element_type=jnp.float32)
    best = jnp.maximum(made[:, 0:128], made[:, 128:256])
    best = jnp.maximum(best, pltpu.roll(best, 64, 1))
    second = jnp.maximum(best + b2_full[...], 0.0)
    second = second * inside_map(lo, hi, groups, where)
    put_rows(second_buf, lo, hi, groups, second.astype(jnp.bfloat16).astype(jnp.float32))


def conv3(lo, hi, groups, w3_full, b3_ref, w4_ref, second_buf):
    lane = lax.broadcasted_iota(jnp.int32, (1, 128), 1)
    low_a = lane < 64

    def moved(k):
        return rows_at(second_buf, lo + k % 3 - 1, hi + k % 3 - 1, k // 3 - 1, groups)

    taps = []
    for k in range(0, 9, 2):
        taps.append(jnp.where(low_a, moved(k), moved(k + 1)) if k < 8 else moved(k))
    stacked = jnp.concatenate(taps, axis=1).astype(jnp.bfloat16)
    made = jnp.dot(stacked, w3_full[...], preferred_element_type=jnp.float32)
    third = jnp.maximum(made + b3_ref[...], 0.0).astype(jnp.bfloat16).astype(jnp.float32)
    weighted = third * w4_ref[...].astype(jnp.float32)
    return jnp.sum(weighted.reshape(hi - lo, span_of(groups), 128), axis=2)


def body(
    query_feats, ref_feats, pair_table, lengths, query_len, conv1_weight, conv1_bias,
    conv2_weight, conv2_bias, conv3_weight, conv3_bias, conv4_weight, conv4_bias,
):
    senders = lax.axis_size("qry")
    others = lax.axis_size("ref")
    frames, regions, depth = query_feats.shape
    query_mat = jnp.transpose(query_feats, (1, 0, 2)).reshape(regions * frames, depth)
    ref_mat = jnp.transpose(ref_feats, (1, 2, 0, 3)).reshape(regions, -1, depth)
    videos = lengths.shape[0]
    shard = ref_mat.shape[1]
    chunks = shard // GROUP
    chips = senders // 2
    steps = max(1, chips - 1)
    cuts = [depth * k // 30 // 128 * 128 for k in (0, 5, 10, 16, 22, 27, 30)]
    pieces = len(cuts) - 1
    tiles = frames // 4
    side = tiles + 4
    rows = side * PITCH
    scale = 1.0 / (regions * math.sqrt(depth))
    vmem = pl.BlockSpec(memory_space=pltpu.VMEM)
    smem = pl.BlockSpec(memory_space=pltpu.SMEM)
    hbm = pl.BlockSpec(memory_space=pltpu.HBM)
    dma = pltpu.SemaphoreType.DMA
    f32, bf16 = jnp.float32, jnp.bfloat16
    operands = (
        pair_table,
        lengths,
        query_len,
        conv4_bias,
        conv1_weight,
        conv1_bias[None],
        jnp.transpose(conv2_weight, (0, 1, 3, 2)).reshape(
            9, conv2_weight.shape[3], conv2_weight.shape[2]
        ),
        conv2_bias[None],
        jnp.transpose(conv3_weight, (0, 1, 3, 2)).reshape(
            9, conv3_weight.shape[3], conv3_weight.shape[2]
        ),
        conv3_bias[None],
        conv4_weight[None],
        query_mat,
        ref_mat,
    )
    kept = [
        (pltpu.SMEM if k < 4 else pltpu.VMEM)(operand.shape, operand.dtype)
        for k, operand in enumerate(operands[:11]) if k not in (2, 3)
    ]
    scores, totals = pl.pallas_call(
        functools.partial(whole_kernel, chips, others, scale, cuts),
        out_shape=(
            pltpu.VMEM((tiles, tiles), f32),
            pltpu.SMEM((videos,), f32),
        ),
        in_specs=[hbm] * 2 + [smem] * 2 + [hbm] * (len(operands) - 4),
        out_specs=(vmem, smem),
        scratch_shapes=kept + [
            pltpu.VMEM(query_mat.shape, bf16),
            pltpu.VMEM((2, chunks, regions, GROUP, depth), bf16),
            pltpu.VMEM((steps, chunks, 2, regions, GROUP, depth), bf16),
            pltpu.VMEM((2 * regions * GROUP, regions * frames), f32),
            pltpu.VMEM((senders, shard, frames), f32),
            pltpu.VMEM((3, frames + 2 * HALO, frames), f32),
            pltpu.VMEM((2, frames + 4 * HALO, 384), f32),
            pltpu.VMEM((rows, 128), f32),
            pltpu.VMEM((rows + 2 * LEAD, 128), f32),
            pltpu.VMEM((rows + 2 * LEAD, 128), f32),
            pltpu.VMEM((16, 128), f32),
            pltpu.VMEM((128, 512), f32),
            pltpu.VMEM((256, 512), bf16),
            pltpu.VMEM((512, 256), bf16),
            pltpu.VMEM((640, 128), bf16),
            pltpu.VMEM((1, 128), f32),
            pltpu.VMEM((1, 128), f32),
            pltpu.VMEM((3 * frames, 384), bf16),
            pltpu.VMEM((3 * frames, 384), bf16),
            pltpu.VMEM((-(-side // 8) * 8, 128), f32),
            pltpu.VMEM((senders * others, videos, 128), f32),
            pltpu.VMEM((2, 2, HALO, frames), f32),
            pltpu.VMEM((2, 2, HALO, frames), f32),
            dma((9,)),
            dma(()),
            dma(()),
            dma(()),
            dma(()),
            dma((steps,)),
            dma((steps, chunks, pieces)),
            dma((steps,)),
            dma((steps, chunks, 4)),
            dma((8,)),
            dma((8,)),
            dma(()),
            dma(()),
            pltpu.SemaphoreType.REGULAR((max(1, others - 1),)),
            dma((2, 2)),
            dma((2, 2)),
        ],
        compiler_params=pltpu.CompilerParams(
            collective_id=0, has_side_effects=True, vmem_limit_bytes=56 << 20
        ),
        name="whole",
    )(*operands)
    return (scores, totals)


def solution(mesh):
    placed = (
        P(("groups", "qry"), None, None),
        P(("groups", "ref"), "qry", None, None),
        P("groups", None),
        P("groups"),
        P("groups"),
    ) + (P(),) * 8
    return jax.shard_map(
        body,
        mesh=mesh,
        in_specs=placed,
        out_specs=(P(("groups", "qry"), "ref"), P("groups")),
        check_vma=False,
    )
```
